32 devices in a mesh: batch: 16 (over z, y, core), head: 2 (over x).
Axes of the slice: x: 2, y: 2, z: 4, core: 2. Of those that a mesh axis runs over, the one named last changes fastest.
Arguments:
- tokens: bfloat16 [16384, 768], P('batch', 'head'), may hold values from -6 to 6
- w_qkv: bfloat16 [768, 3, 768], P(None, None, 'head'), may hold values from -0.21875 to 0.21875
- w_out: bfloat16 [768, 768], replicated, may hold values from -3 to 3
- gain_one: float32 [768], replicated, may hold values from 0.25 to 1.75
- attention_norm_bias: float32 [768], replicated, may hold values from -3 to 3
- w_up: bfloat16 [768, 3072], P(None, 'head'), may hold values from -0.21875 to 0.21875
- b_up: float32 [3072], P('head'), may hold values from -3 to 3
- w_down: bfloat16 [3072, 768], P('head'), may hold values from -0.109375 to 0.109375
- gain_two: float32 [768], replicated, may hold values from 0.25 to 1.75
- shift_two: float32 [768], replicated, may hold values from -3 to 3
- block_perm: int32 [12, 2], P('head'), may hold values from 0 to 1, each once within a row
- mask_index: int32 [16, 256], P('batch'), may hold values from 0 to 1023, as said below
- mask_count: int32 [16], P('batch'), may hold values from 51 to 256, as said below
- cotangent: bfloat16 [16, 256, 768], P('batch'), may hold values from -6 to 6
Outputs:
- result: bfloat16 [16384, 768], P('batch', 'head')
- grad_tokens: bfloat16 [16384, 768], P('batch', 'head')
- grad_w_qkv: float32 [768, 3, 768], P(None, None, 'head')
- grad_w_out: float32 [768, 768], P('head')
- grad_gain_one: float32 [768], replicated
- grad_shift_one: float32 [768], replicated
- grad_w_up: float32 [768, 3072], P(None, 'head')
- up_bias_gradient: float32 [3072], P('head')
- grad_w_down: float32 [3072, 768], P('head')
- grad_gain_two: float32 [768], replicated
- grad_shift_two: float32 [768], replicated
The draws below stay inside these ranges and needn't reach their ends.
Inputs may be any that keep to these rules, and one draw needn't show every extreme that they name: `mask_index`: each row holds 256 distinct positions of one sequence; only its first mask_count entries are used. `mask_count`: some sequence has exactly 256 masked positions.
All inputs are finite; a program needn't handle non-finite values.
Results may differ from the reference program's by a relative error of at most 0.019.
Values may be sent and summed in bfloat16 or wider, within the bound.
A program may use at most 192 MiB of HBM per device.

```python
import jax
import jax.numpy as jnp
from jax import lax

D = 768
HEADS = 12
HEAD_DIM = 64
FF = 3072
SEQ_LEN = 1024
NBLK = 2
BLOCK = 512
MAXM = 256
MINM = 51
SEQS = 16
TOKENS = 16384


def draw_mask_index(key, part):
    row_keys = jax.random.split(key, SEQS)

    def one_row(row_key):
        return jax.random.permutation(row_key, SEQ_LEN)[:MAXM].astype(jnp.int32)
    return jax.vmap(one_row)(row_keys)


def draw_mask_count(key, part):
    key_one, key_two = jax.random.split(key)
    counts_drawn = jax.random.randint(key_one, (SEQS,), MINM, MAXM + 1, dtype=jnp.int32)
    chosen_seq = jax.random.randint(key_two, (), 0, SEQS, dtype=jnp.int32)
    return jnp.where(jnp.arange(SEQS, dtype=jnp.int32) == chosen_seq, MAXM, counts_drawn).astype(jnp.int32)


def block_scale(key, shape, cuts, smallest, largest):
    gain = 1.0
    for position, parts in cuts:
        steps = jax.random.uniform(jax.random.fold_in(jax.random.fold_in(key, 6), position), (parts,), jnp.float32, smallest / len(cuts), largest / len(cuts))
        gain = gain * jnp.repeat(jnp.exp(steps), shape[position] // parts).reshape((-1,) + (1,) * (len(shape) - 1 - position))
    return gain


def centred(rng, shape, width, most, pieces=(), kind=jnp.bfloat16):
    loudness = block_scale(rng, shape, pieces, -0.22, 0.18) if pieces else 1.0
    result = jax.random.normal(rng, shape, jnp.float32) * width * loudness
    return jnp.minimum(jnp.maximum(result, -most), most).astype(kind)


def setup_inputs(seed: int = 0) -> dict:
    key_list = jax.random.split(jax.random.key(seed), 15)
    tokens = centred(key_list[0], (TOKENS, D), 1.0, 6.0, ((0, 16), (1, 2)))
    w_qkv = centred(key_list[1], (D, 3, D), D ** -0.5, 0.21875, ((2, 2),))
    w_out = centred(key_list[2], (D, D), 4 ** -0.5, 3.0)
    gain_one = jnp.clip(1.0 + 0.15 * jax.random.normal(key_list[3], (D,), jnp.float32), 0.25, 1.75)
    attention_norm_bias = centred(key_list[4], (D,), 0.5, 3.0, (), jnp.float32)
    w_up = centred(key_list[5], (D, FF), D ** -0.5, 0.21875, ((1, 2),))
    b_up = centred(key_list[6], (FF,), 0.5, 3.0, ((0, 2),), jnp.float32)
    w_down = centred(key_list[7], (FF, D), FF ** -0.5, 0.109375, ((0, 2),))
    gain_two = jnp.clip(1.0 + 0.15 * jax.random.normal(key_list[8], (D,), jnp.float32), 0.25, 1.75)
    shift_two = centred(key_list[9], (D,), 0.5, 3.0, (), jnp.float32)
    block_perm = jax.vmap(lambda own: jax.random.permutation(own, NBLK))(jax.random.split(key_list[10], HEADS)).reshape((HEADS, NBLK)).astype(jnp.int32)
    mask_index = draw_mask_index(jax.random.fold_in(key_list[14], 71), 0)
    mask_count = draw_mask_count(jax.random.fold_in(key_list[14], 71), 0)
    cotangent = centred(key_list[13], (SEQS, MAXM, D), 1.0, 6.0, ((0, 16),))
    return {"tokens": tokens, "w_qkv": w_qkv, "w_out": w_out, "gain_one": gain_one, "attention_norm_bias": attention_norm_bias, "w_up": w_up, "b_up": b_up, "w_down": w_down, "gain_two": gain_two, "shift_two": shift_two, "block_perm": block_perm, "mask_index": mask_index, "mask_count": mask_count, "cotangent": cotangent}


@jax.custom_vjp
def low(v):
    return lax.optimization_barrier(v.astype(jnp.bfloat16)).astype(jnp.float32)

@jax.custom_vjp
def low_back(v):
    return v

def low_keep(v):
    return (low(v), None)

def low_pass(kept, grad):
    return (grad,)

def back_keep(v):
    return (v, None)

def back_low(kept, grad):
    return (low(grad),)
low.defvjp(low_keep, low_pass)
low_back.defvjp(back_keep, back_low)
HIGH = lax.Precision.HIGHEST
norm_eps = 1e-06

def layer_norm(values, gain_vec, shift_vec):
    mean_v = lax.optimization_barrier(jnp.mean(values, axis=-1, keepdims=True))
    centered = values - mean_v
    var_v = lax.optimization_barrier(jnp.mean(centered * centered, axis=-1, keepdims=True))
    return centered * lax.rsqrt(var_v + norm_eps) * gain_vec + shift_vec

def forward_one(seq_input, w_qkv, w_out, gain_one, attention_norm_bias, w_up, b_up, w_down, gain_two, shift_two, block_perm):
    qkv_all = jnp.dot(seq_input, w_qkv.reshape(D, 3 * D), precision=HIGH)
    qkv_all = low(low_back(qkv_all))
    arranged = qkv_all.reshape(NBLK, BLOCK, 3, HEADS, HEAD_DIM).transpose(2, 3, 0, 1, 4)
    queries = arranged[0]
    keys_all = arranged[1]
    values_all = arranged[2]
    selector = (block_perm[:, :, None] == jnp.arange(NBLK, dtype=jnp.int32)[None, None, :]).astype(jnp.float32)
    key_sel = jnp.einsum('hbc,hcld->hbld', selector, keys_all, precision=HIGH)
    value_sel = jnp.einsum('hbc,hcld->hbld', selector, values_all, precision=HIGH)
    scores = jnp.einsum('hbqd,hbkd->hbqk', queries, key_sel, precision=HIGH) * HEAD_DIM ** (-0.5)
    scores = low_back(scores)
    weights_soft = low(jax.nn.softmax(scores, axis=-1))
    context = jnp.einsum('hbqk,hbkd->hbqd', weights_soft, value_sel, precision=HIGH)
    context = low(low_back(context.transpose(1, 2, 0, 3).reshape(SEQ_LEN, D)))
    attn_out = low_back(jnp.dot(context, w_out, precision=HIGH))
    normed_one = layer_norm(seq_input + attn_out, gain_one, attention_norm_bias)
    hidden_in = low_back(jnp.dot(low(normed_one), w_up, precision=HIGH) + b_up)
    hidden = low(jax.nn.gelu(hidden_in, approximate=False))
    branch = low_back(jnp.dot(hidden, w_down, precision=HIGH))
    return layer_norm(normed_one + branch, gain_two, shift_two)

def reference(tokens, w_qkv, w_out, gain_one, attention_norm_bias, w_up, b_up, w_down, gain_two, shift_two, block_perm, mask_index, mask_count, cotangent):
    params = tuple((weight.astype(jnp.float32) for weight in (w_qkv, w_out, gain_one, attention_norm_bias, w_up, b_up, w_down, gain_two, shift_two)))
    sequence_tokens = tokens.astype(jnp.float32).reshape(SEQS, SEQ_LEN, D)

    def layer_fn(inputs, *weights):
        return forward_one(inputs, *weights, block_perm)

    def advance(running, element):
        seq_input, positions, live_count, cot_rows = element
        validity = (jnp.arange(MAXM, dtype=jnp.int32) < live_count).astype(jnp.float32)
        dense_grad = jnp.zeros((SEQ_LEN, D), jnp.float32).at[positions].add(cot_rows.astype(jnp.float32) * validity[:, None])
        outputs, pullback = jax.vjp(layer_fn, seq_input, *params)
        gradients = pullback(dense_grad)
        running = tuple((earlier + later for earlier, later in zip(running, gradients[1:])))
        return (running, (outputs.astype(jnp.bfloat16), gradients[0].astype(jnp.bfloat16)))
    start_sums = tuple((jnp.zeros_like(weight) for weight in params))
    totals, (seq_outputs, seq_grads) = lax.scan(advance, start_sums, (sequence_tokens, mask_index, mask_count, cotangent))
    return (seq_outputs.reshape(TOKENS, D), seq_grads.reshape(TOKENS, D), totals[0], totals[1], totals[2], totals[3], totals[4], totals[5], totals[6], totals[7], totals[8])
```

```python
import jax
import jax.numpy as jnp
from jax import lax
from jax.sharding import PartitionSpec as P

HEAD_DIM = 64
norm_eps = 1e-06
root_half = 0.7071067811865476
inv_root_two_pi = 0.3989422804014327
LOW = jnp.bfloat16
WIDE = jnp.float32


def dot(a, b, dims=((1,), (0,))):
    return lax.dot_general(a, b, (dims, ((), ())), preferred_element_type=WIDE)


def normalize(values):
    centered = values - jnp.mean(values, axis=-1, keepdims=True)
    inverse = lax.rsqrt(jnp.mean(centered * centered, axis=-1, keepdims=True) + norm_eps)
    return centered * inverse, inverse


def norm_backward(upstream, normal, inverse, gain_vec):
    scaled = upstream * gain_vec
    grad = inverse * (
        scaled
        - jnp.mean(scaled, axis=-1, keepdims=True)
        - normal * jnp.mean(scaled * normal, axis=-1, keepdims=True)
    )
    return grad, jnp.sum(upstream * normal, axis=0), jnp.sum(upstream, axis=0)


def swap(x, axis, bit):
    n = lax.axis_size(axis)
    return lax.ppermute(x, axis, [(i, i ^ bit) for i in range(n)])


def gather_features(x, head_pos):
    other = swap(x, "head", 1)
    first = head_pos == 0
    return jnp.concatenate((jnp.where(first, x, other), jnp.where(first, other, x)), axis=1)


def sum_batch(grad):
    n = lax.axis_size("batch")
    pos = lax.axis_index("batch")
    shape = grad.shape
    x = grad.reshape(n, shape[0] // n, shape[1])
    bits = [1 << k for k in range(n.bit_length() - 1)]
    for bit in bits:
        half = x.shape[0] // 2
        mine = lax.rem(lax.div(pos, bit), 2)
        keep = lax.dynamic_slice_in_dim(x, mine * half, half, 0)
        send = lax.dynamic_slice_in_dim(x, (1 - mine) * half, half, 0)
        x = keep + swap(send.astype(LOW), "batch", bit).astype(WIDE)
    x = x.astype(LOW)
    for bit in reversed(bits):
        mine = lax.rem(lax.div(pos, bit), 2) == 0
        other = swap(x, "batch", bit)
        x = jnp.concatenate((jnp.where(mine, x, other), jnp.where(mine, other, x)), axis=0)
    return x.reshape(shape).astype(WIDE)


def body(tokens, w_qkv, w_out, gain_one, attention_norm_bias, w_up, b_up, w_down, gain_two,
         shift_two, block_perm, mask_index, mask_count, cotangent):
    width = w_out.shape[0]
    local = w_qkv.shape[2]
    groups = local // HEAD_DIM
    rows = tokens.shape[0]
    blocks = block_perm.shape[1]
    block_len = rows // blocks
    scale = HEAD_DIM ** (-0.5)
    head_pos = lax.axis_index("head")
    slots = mask_index.shape[1]
    full = gather_features(tokens, head_pos)
    flat = w_qkv.reshape(width, 3 * local)
    qkv = dot(full, flat).astype(LOW)
    query, key, value = (qkv[:, i * local:(i + 1) * local] for i in range(3))

    places = jnp.arange(rows, dtype=jnp.int32)
    index = mask_index[0][:, None]
    live = jnp.arange(slots, dtype=jnp.int32)[:, None] < mask_count[0]
    pick = ((index == places[None, :]) & live).astype(LOW)

    def split(x):
        return x.reshape(x.shape[0], groups, HEAD_DIM).transpose(1, 0, 2)

    tokens_c = dot(pick, full).astype(LOW)
    query_c = split(dot(pick, query).astype(LOW))
    key_h, value_h, query_h = split(key), split(value), split(query)
    place_block = places // block_len
    wanted = jnp.where(index // block_len == 0, block_perm[:, 0][:, None, None], block_perm[:, 1][:, None, None])
    allowed = wanted == place_block[None, None, :]
    scores = jnp.einsum("gqd,gkd->gqk", query_c, key_h, preferred_element_type=WIDE) * scale
    scores = jnp.where(allowed, scores, -1e30)
    peak = jnp.max(scores, -1, keepdims=True)
    expd = jnp.exp(scores - peak)
    probs = expd / jnp.sum(expd, -1, keepdims=True)
    probs_low = probs.astype(LOW)
    ctx_c = jnp.einsum("gqk,gkd->gqd", probs_low, value_h, preferred_element_type=WIDE).astype(LOW)
    ctx_c = ctx_c.transpose(1, 0, 2).reshape(slots, local)
    ctx_all = gather_features(ctx_c, head_pos)
    pre_one = tokens_c.astype(WIDE) + dot(ctx_all, w_out)
    normal_one, inverse_one = normalize(pre_one)
    normed_one = normal_one * gain_one + attention_norm_bias
    low_one = normed_one.astype(LOW)
    hidden_in = dot(low_one, w_up) + b_up
    cdf = 0.5 * (1.0 + lax.erf(hidden_in * root_half))
    hidden = (hidden_in * cdf).astype(LOW)
    slope = cdf + hidden_in * inv_root_two_pi * jnp.exp(-0.5 * hidden_in * hidden_in)
    part = dot(hidden, w_down).astype(LOW)
    branch = part.astype(WIDE) + swap(part, "head", 1).astype(WIDE)
    normal_two, inverse_two = normalize(normed_one + branch)
    upstream = jnp.where(live, cotangent[0].astype(WIDE), 0.0)
    grad_two, g_gain_two, g_shift_two = norm_backward(upstream, normal_two, inverse_two, gain_two)
    grad_branch = grad_two.astype(LOW)
    g_down = dot(hidden, grad_branch, ((0,), (0,)))
    grad_in = (dot(grad_branch, w_down, ((1,), (1,))) * slope).astype(LOW)
    g_bias = jnp.sum(grad_in.astype(WIDE), axis=0)
    g_up = dot(low_one, grad_in, ((0,), (0,)))
    back = dot(grad_in, w_up, ((1,), (1,))).astype(LOW)
    grad_normed = grad_two + (back.astype(WIDE) + swap(back, "head", 1).astype(WIDE))
    grad_one, g_gain_one, g_shift_one = norm_backward(grad_normed, normal_one, inverse_one, gain_one)
    grad_attn = grad_one.astype(LOW)
    g_out = dot(ctx_c, grad_attn, ((0,), (0,)))
    own_rows = lax.dynamic_slice_in_dim(w_out, head_pos * local, local, 0)
    grad_ctx = split(dot(grad_attn, own_rows, ((1,), (1,))).astype(LOW))
    dprobs = jnp.einsum("gqd,gkd->gqk", grad_ctx, value_h, preferred_element_type=WIDE)
    inner = jnp.sum(dprobs * probs, -1, keepdims=True)
    dscores = (probs * (dprobs - inner)).astype(LOW)
    d_query = jnp.einsum("gqk,gkd->gqd", dscores, key_h, preferred_element_type=WIDE) * scale
    d_key = jnp.einsum("gqk,gqd->gkd", dscores, query_c, preferred_element_type=WIDE) * scale
    d_value = jnp.einsum("gqk,gqd->gkd", probs_low, grad_ctx, preferred_element_type=WIDE)

    def join(x):
        return x.astype(LOW).transpose(1, 0, 2).reshape(x.shape[1], local)

    d_query, d_key, d_value = join(d_query), join(d_key), join(d_value)
    d_kv = jnp.concatenate((d_key, d_value), axis=1)
    g_q = dot(tokens_c, d_query, ((0,), (0,)))
    g_kv = dot(full, d_kv, ((0,), (0,)))
    g_qkv = jnp.concatenate((g_q, g_kv), axis=1)
    dense_q = dot(pick, d_query, ((0,), (0,))).astype(LOW)
    d_all = jnp.concatenate((dense_q, d_kv), axis=1)
    own = width // 2
    flat_own = lax.dynamic_slice_in_dim(flat, head_pos * own, own, 0)
    flat_far = lax.dynamic_slice_in_dim(flat, (1 - head_pos) * own, own, 0)
    far = dot(d_all, flat_far, ((1,), (1,))).astype(LOW)
    near = dot(d_all, flat_own, ((1,), (1,)))
    got = swap(far, "head", 1)
    mine = lax.dynamic_slice_in_dim(grad_one, head_pos * own, own, 1)
    high = mine.astype(LOW)
    rest = (mine - high.astype(WIDE)).astype(LOW)
    spread = dot(pick, high, ((0,), (0,))) + dot(pick, rest, ((0,), (0,)))
    grad_tokens = (near + got.astype(WIDE) + spread).astype(LOW)

    def choose(x):
        x = x.reshape(groups, blocks, block_len, HEAD_DIM)
        picked = x
        for source in range(blocks):
            picked = jnp.where((block_perm == source)[:, :, None, None], x[:, source:source + 1], picked)
        return picked

    q4 = query_h.reshape(groups, blocks, block_len, HEAD_DIM)
    k4, v4 = choose(key_h), choose(value_h)
    sc = jnp.einsum("gbqd,gbkd->gbqk", q4, k4, preferred_element_type=WIDE) * scale
    top = jnp.max(sc, -1, keepdims=True)
    ex = jnp.exp(sc - top)
    pr = (ex / jnp.sum(ex, -1, keepdims=True)).astype(LOW)
    ctx = jnp.einsum("gbqk,gbkd->gbqd", pr, v4, preferred_element_type=WIDE).astype(LOW)
    ctx = ctx.transpose(1, 2, 0, 3).reshape(rows, local)
    pre = full.astype(WIDE) + dot(gather_features(ctx, head_pos), w_out)
    normed = normalize(pre)[0] * gain_one + attention_norm_bias
    hid_in = dot(normed.astype(LOW), w_up) + b_up
    hid = (hid_in * (0.5 * (1.0 + lax.erf(hid_in * root_half)))).astype(LOW)
    down_own = lax.dynamic_slice_in_dim(w_down, head_pos * own, own, 1)
    down_far = lax.dynamic_slice_in_dim(w_down, (1 - head_pos) * own, own, 1)
    sent = swap(dot(hid, down_far).astype(LOW), "head", 1)
    cols = lax.dynamic_slice_in_dim(normed, head_pos * own, own, 1)
    pre_two = cols + (dot(hid, down_own) + sent.astype(WIDE))
    mean_own = jnp.mean(pre_two, -1, keepdims=True)
    dev = pre_two - mean_own
    stats = jnp.concatenate((mean_own, jnp.mean(dev * dev, -1, keepdims=True)), axis=1)
    far_stats = swap(stats, "head", 1)
    mean_far, var_far = far_stats[:, :1], far_stats[:, 1:]
    mean_all = 0.5 * (mean_own + mean_far)
    gap = 0.5 * (mean_own - mean_far)
    var_all = 0.5 * (stats[:, 1:] + var_far) + gap * gap
    gain_own = lax.dynamic_slice_in_dim(gain_two, head_pos * own, own, 0)
    shift_own = lax.dynamic_slice_in_dim(shift_two, head_pos * own, own, 0)
    result = ((pre_two - mean_all) * lax.rsqrt(var_all + norm_eps) * gain_own + shift_own).astype(LOW)

    g_qkv, g_out, g_up, g_down = (sum_batch(g) for g in (g_qkv, g_out, g_up, g_down))
    small = jnp.concatenate((g_gain_one, g_shift_one, g_gain_two, g_shift_two, g_bias))
    for k in range(lax.axis_size("batch").bit_length() - 1):
        small = small + swap(small, "batch", 1 << k)
    return (result, grad_tokens, g_qkv.reshape(width, 3, local), g_out, small[:width],
            small[width:2 * width], g_up, small[4 * width:], g_down, small[2 * width:3 * width],
            small[3 * width:4 * width])


def solution(mesh):
    return jax.shard_map(
        body,
        mesh=mesh,
        in_specs=(P("batch", "head"), P(None, None, "head"), P(), P(), P(), P(None, "head"), P("head"),
                  P("head", None), P(), P(), P("head", None), P("batch", None), P("batch"),
                  P("batch", None, None)),
        out_specs=(P("batch", "head"), P("batch", "head"), P(None, None, "head"), P("head", None), P(), P(),
                   P(None, "head"), P("head"), P("head", None), P(), P()),
        check_vma=False,
    )
```

```python
import functools

import jax
import jax.numpy as jnp
from jax import lax
from jax.experimental import pallas as pl
from jax.experimental.pallas import tpu as pltpu
from jax.sharding import PartitionSpec as P

HEAD_DIM = 64
norm_eps = 1e-06
root_half = 0.7071067811865476
inv_root_two_pi = 0.3989422804014327
log2_e = 1.4426950408889634
LOW = jnp.bfloat16
WIDE = jnp.float32
LANES = 128
MESH = pl.DeviceIdType.MESH
VMEM_BYTES = 67043328


def dot(a, b):
    return lax.dot_general(a, b, (((1,), (0,)), ((), ())), preferred_element_type=WIDE)


def dot_nt(a, b):
    return lax.dot_general(a, b, (((1,), (1,)), ((), ())), preferred_element_type=WIDE)


def dot_tn(a, b):
    return lax.dot_general(a, b, (((0,), (0,)), ((), ())), preferred_element_type=WIDE)


def normalize(values):
    centered = values - jnp.mean(values, axis=-1, keepdims=True)
    inverse = lax.rsqrt(jnp.mean(centered * centered, axis=-1, keepdims=True) + norm_eps)
    return centered * inverse, inverse


def norm_backward(upstream, normal, inverse, gain_vec):
    scaled = upstream * gain_vec
    return inverse * (
        scaled
        - jnp.mean(scaled, axis=-1, keepdims=True)
        - normal * jnp.mean(scaled * normal, axis=-1, keepdims=True)
    )


def col_sum(x):
    return jnp.sum(x, axis=0, keepdims=True)


def cat(parts):
    return jnp.concatenate(parts, axis=1)


class Ring:
    def __init__(self, order, extra, first, out, recv, send, keep, fin, xsend, xrecv, sems, peer, bit_of):
        self.order, self.extra = order, extra
        self.first, self.out = first, out
        self.recv, self.send, self.keep, self.fin = recv, send, keep, fin
        self.xsend, self.xrecv = xsend, xrecv
        self.ssem, self.rsem, self.lsem = sems
        self.peer = peer
        self.mine = [bit_of(b) for b in order]
        units = first.shape[0]
        self.sizes = [units >> (k + 1) for k in range(len(order))]
        self.base = []
        base = 0
        for k in range(len(order)):
            base = base + self.mine[k] * self.sizes[k]
            self.base.append(base)

    def _copy(self, src, dst, slot, bit):
        return pltpu.make_async_remote_copy(
            src_ref=src, dst_ref=dst, send_sem=self.ssem.at[slot], recv_sem=self.rsem.at[slot],
            device_id=self.peer(bit), device_id_type=MESH)

    def _rs(self, k):
        size = self.sizes[k]
        if k == 0:
            src = self.first.at[pl.ds((1 - self.mine[0]) * size, size)]
        else:
            src = self.send[k - 1]
        return self._copy(src, self.recv[k], k, self.order[k])

    def _x(self, j):
        return self._copy(self.xsend, self.xrecv.at[pl.ds(j, 1)], len(self.order) + j, self.extra[j])

    def _ag(self, k):
        last = len(self.order) - 1
        slot = len(self.order) + len(self.extra) + k
        if k == last:
            return self._copy(self.fin, self.out.at[pl.ds(self.base[k], 1)], slot, self.order[k])
        size = self.sizes[k]
        part = self.out.at[pl.ds(self.base[k], size)]
        return self._copy(part, part, slot, self.order[k])

    def _own(self):
        return pltpu.make_async_copy(self.fin, self.out.at[pl.ds(self.base[-1], 1)], self.lsem)

    def start(self):
        self._rs(0).start()

    def _value(self, k, u):
        got = self.recv[k][u].astype(WIDE)
        if k == 0:
            return self.first[self.mine[0] * self.sizes[0] + u].astype(WIDE) + got
        return self.keep[k - 1][u] + got

    def reduce(self, k):
        self._rs(k).wait_recv()
        if k + 1 < len(self.order):
            half = self.sizes[k + 1]
            mine = self.mine[k + 1]

            def out_part(j, c):
                self.send[k][j] = self._value(k, (1 - mine) * half + j).astype(LOW)
                return c

            lax.fori_loop(0, half, out_part, 0)
            self._rs(k + 1).start()

            def own_part(j, c):
                self.keep[k][j] = self._value(k, mine * half + j)
                return c

            lax.fori_loop(0, half, own_part, 0)
        else:
            total = self._value(k, 0)
            for j in range(len(self.extra)):
                self.xsend[0] = total.astype(LOW)
                self._x(j).start()
                self._x(j).wait()
                total = self.xsend[0].astype(WIDE) + self.xrecv[j].astype(WIDE)
            self.fin[0] = total.astype(LOW)
            self._ag(k).start()
            self._own().start()

    def gather(self, k):
        self._ag(k + 1).wait_recv()
        if k + 2 == len(self.order):
            self._own().wait()
        if k >= 0:
            self._ag(k).start()

    def finish(self):
        for k in range(len(self.order)):
            self._rs(k).wait_send()
            self._ag(k).wait_send()


def kernel(n, refs):
    (tokens, wqkv_hbm, wout_hbm, wup_hbm, wdown_hbm, gain_one, shift_one, b_up, gain_two, shift_two,
     perm, count, index, cot,
     result, grad_tokens, o_down, o_up, o_out, o_qkv, small_out,
     wqkv, wout, wup, wdown, wsem,
     tok, qkv, sel_t, sel, blk, tokc, qc, probs, ctxc, normal_one, inverse_one, normed_one, low_one, slope,
     hidden, part, part_got, gb, gtwo, gin, back, back_got, gattn, gctx, dqc, dall, far, far_got, near,
     ctx, pre_two, down_far, down_got, stats, stats_got,
     f_down, f_up, f_out, f_qkv, small, small_got,
     xs_send, xs_recv, lsem, ring_refs) = refs
    rows, own = tokens.shape
    width = wout.shape[0]
    local = wqkv.shape[1] // 3
    pairs = local // LANES
    slots = index.shape[1]
    ff = wup.shape[1]
    block_len = rows // 2
    tile = 256
    tiles = rows // tile
    scale = HEAD_DIM ** (-0.5)
    b = lax.axis_index("batch")
    h = lax.axis_index("head")
    other = 1 - h
    bits = [1 << k for k in range(n.bit_length() - 1)]

    def bit_of(bit):
        return lax.rem(lax.div(b, bit), 2)

    def peer(bit):
        return (b + bit - 2 * bit * bit_of(bit), h)

    x_peer = (b, other)

    def x_copy(src, dst, slot):
        return pltpu.make_async_remote_copy(
            src_ref=src, dst_ref=dst, send_sem=xs_send.at[slot], recv_sem=xs_recv.at[slot],
            device_id=x_peer, device_id_type=MESH)

    loads = [pltpu.make_async_copy(s, d, wsem.at[i]) for i, (s, d) in enumerate(
        ((wqkv_hbm, wqkv), (wout_hbm, wout), (wup_hbm, wup), (wdown_hbm, wdown)))]
    for cp in loads:
        cp.start()
    barrier = pltpu.get_barrier_semaphore()
    pl.semaphore_signal(barrier, inc=1, device_id=x_peer, device_id_type=MESH)
    for bit in bits:
        pl.semaphore_signal(barrier, inc=1, device_id=peer(bit), device_id_type=MESH)
    pl.semaphore_wait(barrier, 1 + len(bits))

    own_cols = pl.ds(pl.multiple_of(h * own, LANES), own)
    far_cols = pl.ds(pl.multiple_of(other * own, LANES), own)

    def row_tile(r):
        return pl.ds(pl.multiple_of(r * tile, tile), tile)

    def tok_copy(r):
        return x_copy(tokens.at[row_tile(r)], tok.at[row_tile(r), own_cols], r)

    for r in range(tiles):
        tok_copy(r).start()
    own_tok = pltpu.make_async_copy(tokens, tok.at[:, own_cols], lsem.at[0])
    own_tok.start()

    lane_slot = lax.broadcasted_iota(jnp.int32, (1, slots), 1)
    idx = jnp.where(lane_slot < count[...], index[...], -1)
    picked = jnp.where(lax.broadcasted_iota(jnp.int32, (rows, slots), 0) == idx, 1.0, 0.0)
    sel_t[...] = picked.astype(LOW)
    picked = jnp.transpose(picked)
    sel[...] = picked.astype(LOW)
    blk[...] = jnp.broadcast_to(jnp.sum(picked[:, block_len:], axis=1, keepdims=True), blk.shape)
    own_tok.wait()
    loads[0].wait()

    def qkv_tile(r, c):
        tok_copy(r).wait_recv()
        out = dot(tok[row_tile(r), :], wqkv[...]).astype(LOW)
        for j in range(3 * pairs):
            qkv[j, row_tile(r), :] = out[:, j * LANES:(j + 1) * LANES]
        return c

    lax.fori_loop(0, tiles, qkv_tile, 0)

    low_lane = lax.broadcasted_iota(jnp.int32, (1, LANES), 1) < HEAD_DIM
    tokc[...] = dot(sel[...], tok[...]).astype(LOW)

    def keep_head(x, e):
        return jnp.where(low_lane, x, 0.0).astype(LOW) if e == 0 else jnp.where(low_lane, 0.0, x).astype(LOW)

    def second(head):
        pair = perm[pl.ds(head, 1), :].astype(WIDE)
        return (pair[:, :1] + blk[:, :1] * (pair[:, 1:] - pair[:, :1])) > 0.5

    def masked_attention(p, c):
        q2 = dot(sel[...], qkv[p]).astype(LOW)
        qc[p] = q2
        halves = []
        for e in range(2):
            head = 2 * p + e
            late = second(head)
            qm = keep_head(q2.astype(WIDE), e)
            s = jnp.where(late, dot_nt(qm, qkv[pairs + p, block_len:, :]),
                          dot_nt(qm, qkv[pairs + p, :block_len, :])) * (scale * log2_e)
            ex = jnp.exp2(s - jnp.max(s, axis=-1, keepdims=True))
            pr = ex * (1.0 / jnp.sum(ex, axis=-1, keepdims=True))
            probs[head] = pr
            pr = pr.astype(LOW)
            halves.append(jnp.where(late, dot(pr, qkv[2 * pairs + p, block_len:, :]),
                                    dot(pr, qkv[2 * pairs + p, :block_len, :])))
        ctxc[h * pairs + p] = jnp.where(low_lane, halves[0], halves[1]).astype(LOW)
        return c

    lax.fori_loop(0, pairs, masked_attention, 0)
    mine_c = ctxc.at[pl.ds(h * pairs, pairs)]
    ctxc_copy = x_copy(mine_c, mine_c, 4)
    ctxc_copy.start()

    def attend(i, c):
        p = lax.div(i, 2)
        q_block = lax.rem(i, 2)
        q_rows = pl.ds(pl.multiple_of(q_block * block_len, block_len), block_len)
        q2 = qkv[p, q_rows, :].astype(WIDE)
        even, odd = (perm[pl.ds(2 * p + e, 1), :].astype(WIDE) for e in range(2))
        late = jnp.where(low_lane, jnp.where(q_block == 0, even[:, :1], even[:, 1:]),
                         jnp.where(q_block == 0, odd[:, :1], odd[:, 1:])) > 0.5

        def chosen(j):
            return jnp.where(late, qkv[j, block_len:, :].astype(WIDE), qkv[j, :block_len, :].astype(WIDE)).astype(LOW)

        k2, v2 = chosen(pairs + p), chosen(2 * pairs + p)
        halves = []
        for e in range(2):
            s = dot_nt(keep_head(q2, e), k2) * (scale * log2_e)
            ex = jnp.exp2(s - jnp.max(s, axis=-1, keepdims=True))
            inv = 1.0 / jnp.sum(ex, axis=-1, keepdims=True)
            halves.append(dot(ex.astype(LOW), v2) * inv)
        ctx[h * pairs + p, q_rows, :] = jnp.where(low_lane, halves[0], halves[1]).astype(LOW)
        return c

    attend_units = 2 * pairs
    cut = attend_units // 3
    lax.fori_loop(0, cut, attend, 0)

    ctxc_copy.wait_recv()
    for cp in loads[1:]:
        cp.wait()
    pre = tokc[...].astype(WIDE) + dot(cat([ctxc[j] for j in range(2 * pairs)]), wout[...])
    nrm_c, inv_c = normalize(pre)
    normal_one[...] = nrm_c
    inverse_one[...] = jnp.broadcast_to(inv_c, inverse_one.shape)
    nrm_c = nrm_c * gain_one[...] + shift_one[...]
    normed_one[...] = nrm_c
    low_one[...] = nrm_c.astype(LOW)
    ff_tile = 384

    def up_tile(i, c):
        cols = pl.ds(pl.multiple_of(i * ff_tile, ff_tile), ff_tile)
        u = dot(low_one[...], wup[:, cols]) + b_up[:, cols]
        cdf = 0.5 * (1.0 + lax.erf(u * root_half))
        hidden[:, cols] = (u * cdf).astype(LOW)
        slope[:, cols] = cdf + u * inv_root_two_pi * jnp.exp(-0.5 * u * u)
        return c

    lax.fori_loop(0, ff // ff_tile, up_tile, 0)
    part[...] = dot(hidden[...], wdown[...]).astype(LOW)
    part_copy = x_copy(part, part_got, 5)
    part_copy.start()
    lax.fori_loop(cut, attend_units, attend, 0)
    part_copy.wait_recv()

    normal_two, inv_two = normalize(normed_one[...] + (part[...].astype(WIDE) + part_got[...].astype(WIDE)))
    alive = lax.broadcasted_iota(jnp.int32, (slots, 1), 0) < count[...]
    up = jnp.where(alive, cot[...].astype(WIDE), 0.0)
    g2 = norm_backward(up, normal_two, inv_two, gain_two[...])
    gtwo[...] = g2
    gb[...] = g2.astype(LOW)
    small[2:3, :] = cat([col_sum(up * normal_two), col_sum(up)])

    def in_tile(i, c):
        cols = pl.ds(pl.multiple_of(i * ff_tile, ff_tile), ff_tile)
        g = (dot_nt(gb[...], wdown[cols, :]) * slope[:, cols]).astype(LOW)
        gin[:, cols] = g
        small[0:1, cols] = col_sum(g.astype(WIDE))
        return c

    lax.fori_loop(0, ff // ff_tile, in_tile, 0)
    back[...] = dot_nt(gin[...], wup[...]).astype(LOW)
    back_copy = x_copy(back, back_got, 6)
    back_copy.start()

    rings = ring_refs
    ring_down, ring_up, ring_out, ring_qkv = (
        Ring(peer=peer, bit_of=bit_of, **r) for r in rings)

    def put(first, unit, value):
        r = first.shape[1]
        for j in range(value.shape[0] // r):
            first[unit + j] = value[j * r:(j + 1) * r, :]

    units = f_down.shape[0]

    def down_tile(i, c):
        cols = pl.ds(pl.multiple_of(i * ff_tile, ff_tile), ff_tile)
        put(f_down, i * (ff_tile * units // ff), dot_tn(hidden[:, cols], gb[...]).astype(LOW))
        return c

    lax.fori_loop(0, ff // ff_tile, down_tile, 0)
    ring_down.start()

    def up_grad_tile(i, c):
        cols = pl.ds(pl.multiple_of(i * ff_tile, ff_tile), ff_tile)
        put(f_up, i * (ff_tile * units // width), dot_tn(low_one[:, cols], gin[...]).astype(LOW))
        return c

    lax.fori_loop(0, width // ff_tile, up_grad_tile, 0)
    ring_up.start()
    ring_down.reduce(0)
    ring_up.reduce(0)
    back_copy.wait_recv()

    gn = gtwo[...] + (back[...].astype(WIDE) + back_got[...].astype(WIDE))
    small[1:2, :] = cat([col_sum(gn * normal_one[...]), col_sum(gn)])
    g1 = norm_backward(gn, normal_one[...], inverse_one[:, :1], gain_one[...])
    gtwo[...] = g1
    gattn[...] = g1.astype(LOW)
    own_rows = pl.ds(pl.multiple_of(h * local, LANES), local)
    gc = dot_nt(gattn[...], wout[own_rows, :]).astype(LOW)
    for p in range(pairs):
        gctx[p] = gc[:, p * LANES:(p + 1) * LANES]

    def masked_backward(p, c):
        q2 = qc[p].astype(WIDE)
        g2 = gctx[p].astype(WIDE)
        k2 = cat([qkv[pairs + p, :block_len, :], qkv[pairs + p, block_len:, :]])
        dk = jnp.zeros((block_len, 2 * LANES), WIDE)
        dv = jnp.zeros((block_len, 2 * LANES), WIDE)
        dq = []
        for e in range(2):
            head = 2 * p + e
            late = second(head)
            gm = keep_head(g2, e)
            dp = jnp.where(late, dot_nt(gm, qkv[2 * pairs + p, block_len:, :]),
                           dot_nt(gm, qkv[2 * pairs + p, :block_len, :]))
            pr = probs[head]
            t = dp * pr
            ds = (t - pr * jnp.sum(t, axis=-1, keepdims=True)).astype(LOW)
            qm = keep_head(q2, e).astype(WIDE)
            gm = gm.astype(WIDE)
            dk = dk + dot_tn(ds, cat([jnp.where(late, 0.0, qm), jnp.where(late, qm, 0.0)]).astype(LOW))
            dv = dv + dot_tn(pr.astype(LOW),
                             cat([jnp.where(late, 0.0, gm), jnp.where(late, gm, 0.0)]).astype(LOW))
            both = dot(ds, k2)
            dq.append(jnp.where(late, both[:, LANES:], both[:, :LANES]))
        d = (jnp.where(low_lane, dq[0], dq[1]) * scale).astype(LOW)
        dqc[p] = d
        dall[p] = dot(sel_t[...], d).astype(LOW)
        dk = (dk * scale).astype(LOW)
        dv = dv.astype(LOW)
        dall[pairs + p, :block_len, :] = dk[:, :LANES]
        dall[pairs + p, block_len:, :] = dk[:, LANES:]
        dall[2 * pairs + p, :block_len, :] = dv[:, :LANES]
        dall[2 * pairs + p, block_len:, :] = dv[:, LANES:]
        return c

    lax.fori_loop(0, pairs, masked_backward, 0)

    small[3:8, :] = jnp.zeros((5, small.shape[1]), WIDE)

    def small_copy(k):
        return pltpu.make_async_remote_copy(
            src_ref=small.at[pl.ds(8 * k, 8)], dst_ref=small_got.at[pl.ds(8 * k, 8)],
            send_sem=xs_send.at[18 + k], recv_sem=xs_recv.at[18 + k],
            device_id=peer(bits[k]), device_id_type=MESH)

    def small_step(k):
        small_copy(k).wait_recv()
        total = small[8 * k:8 * k + 8, :] + small_got[8 * k:8 * k + 8, :]
        if k + 1 < len(bits):
            small[8 * k + 8:8 * k + 16, :] = total
            small_copy(k + 1).start()
        else:
            small_out[...] = total

    small_copy(0).start()

    put(f_out, 0, dot_tn(cat([ctxc[h * pairs + p] for p in range(pairs)]), gattn[...]).astype(LOW))
    ring_out.start()

    def qkv_grad_tile(i, c):
        cols = pl.ds(pl.multiple_of(i * ff_tile, ff_tile), ff_tile)
        gq = dot_tn(tokc[:, cols], cat([dqc[p] for p in range(pairs)]))
        gkv = dot_tn(tok[:, cols], cat([dall[pairs + j] for j in range(2 * pairs)]))
        put(f_qkv, i * (ff_tile * units // width), cat([gq, gkv]).astype(LOW))
        return c

    lax.fori_loop(0, width // ff_tile, qkv_grad_tile, 0)
    ring_qkv.start()
    small_step(0)

    def far_copy(r):
        return x_copy(far.at[row_tile(r)], far_got.at[row_tile(r)], 7 + r)

    def far_tile(r, c):
        d = cat([dall[j, row_tile(r), :] for j in range(3 * pairs)])
        far[row_tile(r), :] = dot_nt(d, wqkv[far_cols, :]).astype(LOW)
        far_copy(r).start()
        return c

    def ctx_copy():
        part_ref = ctx.at[pl.ds(h * pairs, pairs)]
        return x_copy(part_ref, part_ref, 11)

    ctx_copy().start()
    lax.fori_loop(0, tiles, far_tile, 0)
    ring_out.reduce(0)
    ring_qkv.reduce(0)
    ring_down.reduce(1)
    ring_up.reduce(1)
    for k in range(1, len(bits)):
        small_step(k)
    mine = gtwo[:, own_cols]
    high = mine.astype(LOW)
    rest = (mine - high.astype(WIDE)).astype(LOW)
    halves = cat([high, rest])

    def near_tile(r, c):
        d = cat([dall[j, row_tile(r), :] for j in range(3 * pairs)])
        spread = dot(sel_t[row_tile(r), :], halves)
        near[row_tile(r), :] = dot_nt(d, wqkv[own_cols, :]) + (spread[:, :own] + spread[:, own:])
        return c

    lax.fori_loop(0, tiles, near_tile, 0)
    ring_down.reduce(2)
    ring_up.reduce(2)
    ctx_copy().wait_recv()

    def down_copy(r):
        return x_copy(down_far.at[row_tile(r)], down_got.at[row_tile(r)], 12 + r)

    def layer_tile(r, c):
        rs = row_tile(r)
        pre_r = tok[rs, :].astype(WIDE) + dot(cat([ctx[j, rs, :] for j in range(2 * pairs)]), wout[...])
        normed = normalize(pre_r)[0] * gain_one[...] + shift_one[...]
        normed_one[...] = normed
        u = dot(normed.astype(LOW), wup[...]) + b_up[...]
        hid = (u * (0.5 * (1.0 + lax.erf(u * root_half)))).astype(LOW)
        down_far[rs, :] = dot(hid, wdown[:, far_cols]).astype(LOW)
        down_copy(r).start()
        pre_two[rs, :] = normed_one[:, own_cols] + dot(hid, wdown[:, own_cols])
        return c

    lax.fori_loop(0, tiles // 2, layer_tile, 0)
    ring_out.reduce(1)
    ring_qkv.reduce(1)
    ring_down.reduce(3)
    ring_up.reduce(3)
    lax.fori_loop(tiles // 2, tiles, layer_tile, 0)
    ring_out.reduce(2)
    ring_qkv.reduce(2)
    ring_down.gather(2)
    ring_up.gather(2)

    def grad_tile(r, c):
        far_copy(r).wait_recv()
        far_copy(r).wait_send()
        far[row_tile(r), :] = (near[row_tile(r), :] + far_got[row_tile(r), :].astype(WIDE)).astype(LOW)
        return c

    lax.fori_loop(0, tiles, grad_tile, 0)
    grad_out = pltpu.make_async_copy(far, grad_tokens, lsem.at[1])
    grad_out.start()
    ring_out.reduce(3)
    ring_qkv.reduce(3)
    ring_down.gather(1)
    ring_up.gather(1)

    first_lane = lax.broadcasted_iota(jnp.int32, (1, LANES), 1) < 1

    def stat_tile(r, c):
        rs = row_tile(r)
        down_copy(r).wait_recv()
        x = pre_two[rs, :] + down_got[rs, :].astype(WIDE)
        pre_two[rs, :] = x
        mean = jnp.mean(x, axis=-1, keepdims=True)
        dev = x - mean
        var = jnp.mean(dev * dev, axis=-1, keepdims=True)
        both = jnp.where(first_lane, mean, var)
        stats[r] = jnp.transpose(both)[:8, :]
        return c

    lax.fori_loop(0, tiles, stat_tile, 0)
    stats_copy = x_copy(stats, stats_got, 16)
    stats_copy.start()
    ring_out.gather(2)
    ring_qkv.gather(2)
    ring_down.gather(0)
    ring_up.gather(0)
    stats_copy.wait_recv()

    def result_tile(r, c):
        rs = row_tile(r)
        x = pre_two[rs, :]
        fill = jnp.zeros((LANES - 8, tile), WIDE)
        one = jnp.transpose(jnp.concatenate([stats[r], fill], axis=0))
        two = jnp.transpose(jnp.concatenate([stats_got[r], fill], axis=0))
        mean = 0.5 * (one[:, :1] + two[:, :1])
        gap = 0.5 * (one[:, :1] - two[:, :1])
        var = 0.5 * (one[:, 1:2] + two[:, 1:2]) + gap * gap
        down_copy(r).wait_send()
        down_far[rs, :] = ((x - mean) * lax.rsqrt(var + norm_eps) * gain_two[:, own_cols]
                         + shift_two[:, own_cols]).astype(LOW)
        return c

    lax.fori_loop(0, tiles, result_tile, 0)
    result_out = pltpu.make_async_copy(down_far, result, lsem.at[2])
    result_out.start()
    ring_out.gather(1)
    ring_qkv.gather(1)
    ring_out.gather(0)
    ring_qkv.gather(0)
    for ring in (ring_down, ring_up, ring_out, ring_qkv):
        ring.gather(-1)

    for r in range(tiles):
        tok_copy(r).wait_send()
    grad_out.wait()
    result_out.wait()
    for cp in (ctxc_copy, part_copy, back_copy, ctx_copy(), stats_copy):
        cp.wait_send()
    for k in range(len(bits)):
        small_copy(k).wait_send()
    for ring in (ring_down, ring_up, ring_out, ring_qkv):
        ring.finish()


def build(n, tokens, wqkv, wout, gain_one, shift_one, wup, b_up, wdown, gain_two, shift_two, perm, index,
          count, cot):
    rows, own = tokens.shape
    width = wout.shape[0]
    local = wqkv.shape[1] // 3
    pairs = local // LANES
    heads = local // HEAD_DIM
    slots = index.shape[1]
    ff = wup.shape[1]
    block_len = rows // 2
    tile = 256
    steps = n.bit_length() - 1
    bits = [1 << k for k in range(steps)]
    depth = min(4, steps)
    units = 1 << depth
    halving, extra = bits[:depth], bits[depth:]

    vm = pltpu.VMEM
    groups = {"down": (ff // units, width), "up": (width // units, ff), "out": (local // units, width),
              "qkv": (width // units, 3 * local)}
    orders = {g: halving for g in groups}
    dma = pltpu.SemaphoreType.DMA

    def ring_scratch(g):
        r, c = groups[g]
        sizes = [units >> (k + 1) for k in range(depth)]
        return {
            "recv": [vm((s, r, c), LOW) for s in sizes],
            "send": [vm((s, r, c), LOW) for s in sizes[1:]],
            "keep": [vm((s, r, c), WIDE) for s in sizes[1:]],
            "fin": vm((1, r, c), LOW),
            "xsend": vm((1, r, c) if extra else (1, 8, LANES), LOW),
            "xrecv": vm((len(extra), r, c) if extra else (1, 8, LANES), LOW),
            "sems": (dma((2 * depth + len(extra),)), dma((2 * depth + len(extra),)), dma(())),
        }

    f = [vm((units,) + groups[g], LOW) for g in groups]
    scratch = [
        vm(wqkv.shape, LOW), vm(wout.shape, LOW), vm(wup.shape, LOW), vm(wdown.shape, LOW), dma((4,)),
        vm((rows, width), LOW), vm((3 * pairs, rows, LANES), LOW), vm((rows, slots), LOW), vm((slots, rows), LOW),
        vm((slots, LANES), WIDE), vm((slots, width), LOW), vm((pairs, slots, LANES), LOW),
        vm((heads, slots, block_len), WIDE), vm((2 * pairs, slots, LANES), LOW), vm((slots, width), WIDE),
        vm((slots, LANES), WIDE), vm((slots, width), WIDE), vm((slots, width), LOW), vm((slots, ff), WIDE),
        vm((slots, ff), LOW), vm((slots, width), LOW), vm((slots, width), LOW), vm((slots, width), LOW),
        vm((slots, width), WIDE), vm((slots, ff), LOW), vm((slots, width), LOW), vm((slots, width), LOW),
        vm((slots, width), LOW), vm((pairs, slots, LANES), LOW),
        vm((pairs, slots, LANES), LOW), vm((3 * pairs, rows, LANES), LOW), vm((rows, own), LOW),
        vm((rows, own), LOW), vm((rows, own), WIDE),
        vm((2 * pairs, rows, LANES), LOW), vm((rows, own), WIDE), vm((rows, own), LOW),
        vm((rows, own), LOW), vm((rows // tile, 8, tile), WIDE), vm((rows // tile, 8, tile), WIDE),
        *f, vm((8 * steps, ff), WIDE), vm((8 * steps, ff), WIDE),
        dma((18 + steps,)), dma((18 + steps,)), dma((3,)),
    ]
    plain = len(scratch)
    ring_specs = [ring_scratch(g) for g in groups]
    flat, tree = jax.tree.flatten(ring_specs, is_leaf=lambda x: not isinstance(x, (dict, list, tuple)))
    n_in, n_out = 14, 7

    def run(*refs):
        head_refs = refs[:n_in + n_out + plain]
        rings = jax.tree.unflatten(tree, refs[n_in + n_out + plain:])
        firsts = head_refs[-(len(groups) + 5):-5]
        outs = refs[n_in + 2:n_in + 2 + len(groups)]
        full = []
        for g, ring, first, out in zip(groups, rings, firsts, outs):
            full.append(dict(order=orders[g], extra=extra, first=first, out=out, **ring))
        kernel(n, (*head_refs, full))

    hbm = pl.BlockSpec(memory_space=pl.ANY)
    v = pl.BlockSpec(memory_space=pltpu.VMEM)
    shape = jax.ShapeDtypeStruct
    return pl.pallas_call(
        run,
        out_shape=(shape((rows, own), LOW), shape((rows, own), LOW),
                   *(shape((units,) + groups[g], LOW) for g in groups), shape((8, ff), WIDE)),
        in_specs=[hbm, hbm, hbm, hbm, hbm, v, v, v, v, v, v, v, v, v],
        out_specs=(hbm, hbm, hbm, hbm, hbm, hbm, v),
        scratch_shapes=scratch + flat,
        compiler_params=pltpu.CompilerParams(
            collective_id=0, has_side_effects=True, vmem_limit_bytes=VMEM_BYTES),
        name="layer",
    )(tokens, wqkv, wout, wup, wdown, gain_one, shift_one, b_up, gain_two, shift_two, perm, count, index, cot)


def body(n, tokens, w_qkv, w_out, gain_one, attention_norm_bias, w_up, b_up, w_down, gain_two, shift_two,
         block_perm, mask_index, mask_count, cotangent):
    width = w_out.shape[0]
    local = w_qkv.shape[2]

    def row(x):
        return x.reshape(1, -1)

    result, grad_tokens, g_down, g_up, g_out, g_qkv, small = build(
        n, tokens, w_qkv.reshape(width, 3 * local), w_out, row(gain_one), row(attention_norm_bias), w_up,
        row(b_up), w_down, row(gain_two), row(shift_two), block_perm, mask_index, mask_count.reshape(1, 1), cotangent[0])
    return (
        result, grad_tokens, g_qkv.reshape(width, 3, local).astype(WIDE), g_out.reshape(local, width).astype(WIDE),
        small[1, :width], small[1, width:], g_up.reshape(w_up.shape).astype(WIDE), small[0],
        g_down.reshape(w_down.shape).astype(WIDE), small[2, :width], small[2, width:])


def solution(mesh):
    return jax.shard_map(
        functools.partial(body, mesh.shape["batch"]),
        mesh=mesh,
        in_specs=(P("batch", "head"), P(None, None, "head"), P(), P(), P(), P(None, "head"), P("head"),
                  P("head", None), P(), P(), P("head", None), P("batch", None), P("batch"),
                  P("batch", None, None)),
        out_specs=(P("batch", "head"), P("batch", "head"), P(None, None, "head"), P("head", None), P(), P(),
                   P(None, "head"), P("head"), P("head", None), P(), P()),
        check_vma=False,
    )
```

```python
import functools

import jax
import jax.numpy as jnp
from jax import lax
from jax.experimental import pallas as pl
from jax.experimental.pallas import tpu as pltpu
from jax.sharding import PartitionSpec as P

HEAD_DIM = 64
norm_eps = 1e-06
root_half = 0.7071067811865476
inv_root_two_pi = 0.3989422804014327
log2_e = 1.4426950408889634
LOW = jnp.bfloat16
WIDE = jnp.float32
LANES = 128
MESH = pl.DeviceIdType.MESH
VMEM_BYTES = 67043328


def dot(a, b):
    return lax.dot_general(a, b, (((1,), (0,)), ((), ())), preferred_element_type=WIDE)


def dot_nt(a, b):
    return lax.dot_general(a, b, (((1,), (1,)), ((), ())), preferred_element_type=WIDE)


def dot_tn(a, b):
    return lax.dot_general(a, b, (((0,), (0,)), ((), ())), preferred_element_type=WIDE)


def normalize(values):
    centered = values - jnp.mean(values, axis=-1, keepdims=True)
    inverse = lax.rsqrt(jnp.mean(centered * centered, axis=-1, keepdims=True) + norm_eps)
    return centered * inverse, inverse


def norm_backward(upstream, normal, inverse, gain_vec):
    scaled = upstream * gain_vec
    return inverse * (
        scaled
        - jnp.mean(scaled, axis=-1, keepdims=True)
        - normal * jnp.mean(scaled * normal, axis=-1, keepdims=True)
    )


def col_sum(x):
    return jnp.sum(x, axis=0, keepdims=True)


def cat(parts):
    return jnp.concatenate(parts, axis=1)


class Ring:
    def __init__(self, order, extra, first, out, recv, send, keep, fin, xsend, xrecv, sems, peer, bit_of):
        self.order, self.extra = order, extra
        self.first, self.out = first, out
        self.recv, self.send, self.keep, self.fin = recv, send, keep, fin
        self.xsend, self.xrecv = xsend, xrecv
        self.ssem, self.rsem, self.lsem = sems
        self.peer = peer
        self.mine = [bit_of(b) for b in order]
        units = first.shape[0]
        self.sizes = [units >> (k + 1) for k in range(len(order))]
        self.base = []
        base = 0
        for k in range(len(order)):
            base = base + self.mine[k] * self.sizes[k]
            self.base.append(base)

    def _copy(self, src, dst, slot, bit):
        return pltpu.make_async_remote_copy(
            src_ref=src, dst_ref=dst, send_sem=self.ssem.at[slot], recv_sem=self.rsem.at[slot],
            device_id=self.peer(bit), device_id_type=MESH)

    def _rs(self, k):
        size = self.sizes[k]
        if k == 0:
            src = self.first.at[pl.ds((1 - self.mine[0]) * size, size)]
        else:
            src = self.send[k - 1]
        return self._copy(src, self.recv[k], k, self.order[k])

    def _x(self, j):
        return self._copy(self.xsend, self.xrecv.at[pl.ds(j, 1)], len(self.order) + j, self.extra[j])

    def _ag(self, k):
        last = len(self.order) - 1
        slot = len(self.order) + len(self.extra) + k
        if k == last:
            return self._copy(self.fin, self.out.at[pl.ds(self.base[k], 1)], slot, self.order[k])
        size = self.sizes[k]
        part = self.out.at[pl.ds(self.base[k], size)]
        return self._copy(part, part, slot, self.order[k])

    def _own(self):
        return pltpu.make_async_copy(self.fin, self.out.at[pl.ds(self.base[-1], 1)], self.lsem)

    def start(self):
        self._rs(0).start()

    def _value(self, k, u):
        got = self.recv[k][u].astype(WIDE)
        if k == 0:
            return self.first[self.mine[0] * self.sizes[0] + u].astype(WIDE) + got
        return self.keep[k - 1][u] + got

    def reduce(self, k):
        self._rs(k).wait_recv()
        if k + 1 < len(self.order):
            half = self.sizes[k + 1]
            mine = self.mine[k + 1]

            def out_part(j, c):
                self.send[k][j] = self._value(k, (1 - mine) * half + j).astype(LOW)
                return c

            lax.fori_loop(0, half, out_part, 0)
            self._rs(k + 1).start()

            def own_part(j, c):
                self.keep[k][j] = self._value(k, mine * half + j)
                return c

            lax.fori_loop(0, half, own_part, 0)
        else:
            total = self._value(k, 0)
            for j in range(len(self.extra)):
                self.xsend[0] = total.astype(LOW)
                self._x(j).start()
                self._x(j).wait()
                total = self.xsend[0].astype(WIDE) + self.xrecv[j].astype(WIDE)
            self.fin[0] = total.astype(LOW)
            self._ag(k).start()
            self._own().start()

    def gather(self, k):
        self._ag(k + 1).wait_recv()
        if k + 2 == len(self.order):
            self._own().wait()
        if k >= 0:
            self._ag(k).start()

    def finish(self):
        for k in range(len(self.order)):
            self._rs(k).wait_send()
            self._ag(k).wait_send()


def kernel(n, refs):
    (tokens, wqkv_hbm, wout_hbm, wup_hbm, wdown_hbm, *vectors,
     perm, count, index, cot,
     result, grad_tokens, o_down, o_up, o_out, o_qkv, small_out,
     wqkv, wout, wup, wdown, wsem, vecs,
     tok, qkv, sel_t, sel, blk, tokc, qc, probs, ctxc, normal_one, inverse_one, normed_one, low_one, slope,
     hidden, part, part_got, gb, gtwo, gin, back, back_got, gattn, gctx, dqc, dall, far, far_got, near,
     ctx, pre_two, down_far, down_got, stats, stats_got,
     f_down, f_up, f_out, f_qkv, small, small_got,
     xs_send, xs_recv, lsem, ring_refs) = refs
    rows, own = tokens.shape
    width = wout.shape[0]
    local = wqkv.shape[1] // 3
    pairs = local // LANES
    slots = index.shape[1]
    ff = wup.shape[1]
    block_len = rows // 2
    tile = 256
    tiles = rows // tile
    scale = HEAD_DIM ** (-0.5)
    b = lax.axis_index("batch")
    h = lax.axis_index("head")
    other = 1 - h
    bits = [1 << k for k in range(n.bit_length() - 1)]

    def bit_of(bit):
        return lax.rem(lax.div(b, bit), 2)

    def peer(bit):
        return (b + bit - 2 * bit * bit_of(bit), h)

    x_peer = (b, other)

    def x_copy(src, dst, slot):
        return pltpu.make_async_remote_copy(
            src_ref=src, dst_ref=dst, send_sem=xs_send.at[slot], recv_sem=xs_recv.at[slot],
            device_id=x_peer, device_id_type=MESH)

    loads = [pltpu.make_async_copy(s, d, wsem.at[i]) for i, (s, d) in enumerate(
        [(wqkv_hbm.at[j], wqkv.at[:, pl.ds(j * local, local)]) for j in range(3)]
        + [(wout_hbm, wout), (wup_hbm, wup), (wdown_hbm, wdown)])]
    for cp in loads:
        cp.start()
    barrier = pltpu.get_barrier_semaphore()
    pl.semaphore_signal(barrier, inc=1, device_id=x_peer, device_id_type=MESH)
    for bit in bits:
        pl.semaphore_signal(barrier, inc=1, device_id=peer(bit), device_id_type=MESH)
    pl.semaphore_wait(barrier, 1 + len(bits))

    own_cols = pl.ds(pl.multiple_of(h * own, LANES), own)
    far_cols = pl.ds(pl.multiple_of(other * own, LANES), own)

    def row_tile(r):
        return pl.ds(pl.multiple_of(r * tile, tile), tile)

    def tok_copy(r):
        return x_copy(tokens.at[row_tile(r)], tok.at[row_tile(r), own_cols], r)

    for r in range(tiles):
        tok_copy(r).start()
    own_tok = pltpu.make_async_copy(tokens, tok.at[:, own_cols], lsem.at[0])
    own_tok.start()

    for i, vector in enumerate(vectors):
        vecs[i:i + 1, :vector.shape[0]] = vector[...].reshape(1, -1)
    gain_one, shift_one, gain_two, shift_two = (vecs.at[i:i + 1, :width] for i in range(4))
    b_up = vecs.at[4:5, :]

    lane_slot = lax.broadcasted_iota(jnp.int32, (1, slots), 1)
    idx = jnp.where(lane_slot < count[...], index[...], -1)
    picked = jnp.where(lax.broadcasted_iota(jnp.int32, (rows, slots), 0) == idx, 1.0, 0.0)
    sel_t[...] = picked.astype(LOW)
    picked = jnp.transpose(picked)
    sel[...] = picked.astype(LOW)
    blk[...] = jnp.broadcast_to(jnp.sum(picked[:, block_len:], axis=1, keepdims=True), blk.shape)
    own_tok.wait()
    for cp in loads[:3]:
        cp.wait()

    def qkv_tile(r, c):
        tok_copy(r).wait_recv()
        out = dot(tok[row_tile(r), :], wqkv[...]).astype(LOW)
        for j in range(3 * pairs):
            qkv[j, row_tile(r), :] = out[:, j * LANES:(j + 1) * LANES]
        return c

    lax.fori_loop(0, tiles, qkv_tile, 0)

    low_lane = lax.broadcasted_iota(jnp.int32, (1, LANES), 1) < HEAD_DIM
    tokc[...] = dot(sel[...], tok[...]).astype(LOW)

    def keep_head(x, e):
        return jnp.where(low_lane, x, 0.0).astype(LOW) if e == 0 else jnp.where(low_lane, 0.0, x).astype(LOW)

    order = perm[...].astype(WIDE)
    head_lane = lax.broadcasted_iota(jnp.int32, order.shape, 1)

    def blocks_of(head):
        return jnp.sum(jnp.where(head_lane == head, order, 0.0), axis=1, keepdims=True)

    def second(head):
        pair = blocks_of(head)
        return (pair[:1] + blk[:, :1] * (pair[1:] - pair[:1])) > 0.5

    def masked_attention(p, c):
        q2 = dot(sel[...], qkv[p]).astype(LOW)
        qc[p] = q2
        halves = []
        for e in range(2):
            head = 2 * p + e
            late = second(head)
            qm = keep_head(q2.astype(WIDE), e)
            s = jnp.where(late, dot_nt(qm, qkv[pairs + p, block_len:, :]),
                          dot_nt(qm, qkv[pairs + p, :block_len, :])) * (scale * log2_e)
            ex = jnp.exp2(s - jnp.max(s, axis=-1, keepdims=True))
            pr = ex * (1.0 / jnp.sum(ex, axis=-1, keepdims=True))
            probs[head] = pr
            pr = pr.astype(LOW)
            halves.append(jnp.where(late, dot(pr, qkv[2 * pairs + p, block_len:, :]),
                                    dot(pr, qkv[2 * pairs + p, :block_len, :])))
        ctxc[h * pairs + p] = jnp.where(low_lane, halves[0], halves[1]).astype(LOW)
        return c

    lax.fori_loop(0, pairs, masked_attention, 0)
    mine_c = ctxc.at[pl.ds(h * pairs, pairs)]
    ctxc_copy = x_copy(mine_c, mine_c, 4)
    ctxc_copy.start()

    def attend(i, c):
        p = lax.div(i, 2)
        q_block = lax.rem(i, 2)
        q_rows = pl.ds(pl.multiple_of(q_block * block_len, block_len), block_len)
        q2 = qkv[p, q_rows, :].astype(WIDE)
        even, odd = blocks_of(2 * p), blocks_of(2 * p + 1)
        late = jnp.where(low_lane, jnp.where(q_block == 0, even[:1], even[1:]),
                         jnp.where(q_block == 0, odd[:1], odd[1:])) > 0.5

        def chosen(j):
            return jnp.where(late, qkv[j, block_len:, :].astype(WIDE), qkv[j, :block_len, :].astype(WIDE)).astype(LOW)

        k2, v2 = chosen(pairs + p), chosen(2 * pairs + p)
        halves = []
        for e in range(2):
            s = dot_nt(keep_head(q2, e), k2) * (scale * log2_e)
            ex = jnp.exp2(s - jnp.max(s, axis=-1, keepdims=True))
            inv = 1.0 / jnp.sum(ex, axis=-1, keepdims=True)
            halves.append(dot(ex.astype(LOW), v2) * inv)
        ctx[h * pairs + p, q_rows, :] = jnp.where(low_lane, halves[0], halves[1]).astype(LOW)
        return c

    attend_units = 2 * pairs
    cut = attend_units // 3
    lax.fori_loop(0, cut, attend, 0)

    ctxc_copy.wait_recv()
    for cp in loads[3:]:
        cp.wait()
    pre = tokc[...].astype(WIDE) + dot(cat([ctxc[j] for j in range(2 * pairs)]), wout[...])
    nrm_c, inv_c = normalize(pre)
    normal_one[...] = nrm_c
    inverse_one[...] = jnp.broadcast_to(inv_c, inverse_one.shape)
    nrm_c = nrm_c * gain_one[...] + shift_one[...]
    normed_one[...] = nrm_c
    low_one[...] = nrm_c.astype(LOW)
    ff_tile = 384

    def up_tile(i, c):
        cols = pl.ds(pl.multiple_of(i * ff_tile, ff_tile), ff_tile)
        u = dot(low_one[...], wup[:, cols]) + vecs[4:5, cols]
        cdf = 0.5 * (1.0 + lax.erf(u * root_half))
        hidden[:, cols] = (u * cdf).astype(LOW)
        slope[:, cols] = cdf + u * inv_root_two_pi * jnp.exp(-0.5 * u * u)
        return c

    lax.fori_loop(0, ff // ff_tile, up_tile, 0)
    part[...] = dot(hidden[...], wdown[...]).astype(LOW)
    part_copy = x_copy(part, part_got, 5)
    part_copy.start()
    lax.fori_loop(cut, attend_units, attend, 0)
    part_copy.wait_recv()

    normal_two, inv_two = normalize(normed_one[...] + (part[...].astype(WIDE) + part_got[...].astype(WIDE)))
    alive = lax.broadcasted_iota(jnp.int32, (slots, 1), 0) < count[...]
    up = jnp.where(alive, cot[...].astype(WIDE), 0.0)
    g2 = norm_backward(up, normal_two, inv_two, gain_two[...])
    gtwo[...] = g2
    gb[...] = g2.astype(LOW)
    small[2:3, :] = cat([col_sum(up * normal_two), col_sum(up)])

    def in_tile(i, c):
        cols = pl.ds(pl.multiple_of(i * ff_tile, ff_tile), ff_tile)
        g = (dot_nt(gb[...], wdown[cols, :]) * slope[:, cols]).astype(LOW)
        gin[:, cols] = g
        small[0:1, cols] = col_sum(g.astype(WIDE))
        return c

    lax.fori_loop(0, ff // ff_tile, in_tile, 0)
    back[...] = dot_nt(gin[...], wup[...]).astype(LOW)
    back_copy = x_copy(back, back_got, 6)
    back_copy.start()

    rings = ring_refs
    ring_down, ring_up, ring_out, ring_qkv = (
        Ring(peer=peer, bit_of=bit_of, **r) for r in rings)

    def put(first, unit, value):
        r = first.shape[1]
        for j in range(value.shape[0] // r):
            first[unit + j] = value[j * r:(j + 1) * r, :]

    units = f_down.shape[0]

    def down_tile(i, c):
        cols = pl.ds(pl.multiple_of(i * ff_tile, ff_tile), ff_tile)
        put(f_down, i * (ff_tile * units // ff), dot_tn(hidden[:, cols], gb[...]).astype(LOW))
        return c

    lax.fori_loop(0, ff // ff_tile, down_tile, 0)
    ring_down.start()

    def up_grad_tile(i, c):
        cols = pl.ds(pl.multiple_of(i * ff_tile, ff_tile), ff_tile)
        put(f_up, i * (ff_tile * units // width), dot_tn(low_one[:, cols], gin[...]).astype(LOW))
        return c

    lax.fori_loop(0, width // ff_tile, up_grad_tile, 0)
    ring_up.start()
    ring_down.reduce(0)
    ring_up.reduce(0)
    back_copy.wait_recv()

    gn = gtwo[...] + (back[...].astype(WIDE) + back_got[...].astype(WIDE))
    small[1:2, :] = cat([col_sum(gn * normal_one[...]), col_sum(gn)])
    g1 = norm_backward(gn, normal_one[...], inverse_one[:, :1], gain_one[...])
    gtwo[...] = g1
    gattn[...] = g1.astype(LOW)
    own_rows = pl.ds(pl.multiple_of(h * local, LANES), local)
    gc = dot_nt(gattn[...], wout[own_rows, :]).astype(LOW)
    for p in range(pairs):
        gctx[p] = gc[:, p * LANES:(p + 1) * LANES]

    def masked_backward(p, c):
        q2 = qc[p].astype(WIDE)
        g2 = gctx[p].astype(WIDE)
        k2 = cat([qkv[pairs + p, :block_len, :], qkv[pairs + p, block_len:, :]])
        dk = jnp.zeros((block_len, 2 * LANES), WIDE)
        dv = jnp.zeros((block_len, 2 * LANES), WIDE)
        dq = []
        for e in range(2):
            head = 2 * p + e
            late = second(head)
            gm = keep_head(g2, e)
            dp = jnp.where(late, dot_nt(gm, qkv[2 * pairs + p, block_len:, :]),
                           dot_nt(gm, qkv[2 * pairs + p, :block_len, :]))
            pr = probs[head]
            t = dp * pr
            ds = (t - pr * jnp.sum(t, axis=-1, keepdims=True)).astype(LOW)
            qm = keep_head(q2, e).astype(WIDE)
            gm = gm.astype(WIDE)
            dk = dk + dot_tn(ds, cat([jnp.where(late, 0.0, qm), jnp.where(late, qm, 0.0)]).astype(LOW))
            dv = dv + dot_tn(pr.astype(LOW),
                             cat([jnp.where(late, 0.0, gm), jnp.where(late, gm, 0.0)]).astype(LOW))
            both = dot(ds, k2)
            dq.append(jnp.where(late, both[:, LANES:], both[:, :LANES]))
        d = (jnp.where(low_lane, dq[0], dq[1]) * scale).astype(LOW)
        dqc[p] = d
        dall[p] = dot(sel_t[...], d).astype(LOW)
        dk = (dk * scale).astype(LOW)
        dv = dv.astype(LOW)
        dall[pairs + p, :block_len, :] = dk[:, :LANES]
        dall[pairs + p, block_len:, :] = dk[:, LANES:]
        dall[2 * pairs + p, :block_len, :] = dv[:, :LANES]
        dall[2 * pairs + p, block_len:, :] = dv[:, LANES:]
        return c

    lax.fori_loop(0, pairs, masked_backward, 0)

    small[3:8, :] = jnp.zeros((5, small.shape[1]), WIDE)

    def small_copy(k):
        return pltpu.make_async_remote_copy(
            src_ref=small.at[pl.ds(8 * k, 8)], dst_ref=small_got.at[pl.ds(8 * k, 8)],
            send_sem=xs_send.at[18 + k], recv_sem=xs_recv.at[18 + k],
            device_id=peer(bits[k]), device_id_type=MESH)

    def small_step(k):
        small_copy(k).wait_recv()
        total = small[8 * k:8 * k + 8, :] + small_got[8 * k:8 * k + 8, :]
        if k + 1 < len(bits):
            small[8 * k + 8:8 * k + 16, :] = total
            small_copy(k + 1).start()
        else:
            small_out[...] = total

    small_copy(0).start()

    put(f_out, 0, dot_tn(cat([ctxc[h * pairs + p] for p in range(pairs)]), gattn[...]).astype(LOW))
    ring_out.start()

    def qkv_grad_tile(i, c):
        cols = pl.ds(pl.multiple_of(i * ff_tile, ff_tile), ff_tile)
        gq = dot_tn(tokc[:, cols], cat([dqc[p] for p in range(pairs)]))
        gkv = dot_tn(tok[:, cols], cat([dall[pairs + j] for j in range(2 * pairs)]))
        put(f_qkv, i * (ff_tile * units // width), cat([gq, gkv]).astype(LOW))
        return c

    lax.fori_loop(0, width // ff_tile, qkv_grad_tile, 0)
    ring_qkv.start()
    small_step(0)

    def far_copy(r):
        return x_copy(far.at[row_tile(r)], far_got.at[row_tile(r)], 7 + r)

    def far_tile(r, c):
        d = cat([dall[j, row_tile(r), :] for j in range(3 * pairs)])
        far[row_tile(r), :] = dot_nt(d, wqkv[far_cols, :]).astype(LOW)
        far_copy(r).start()
        return c

    def ctx_copy():
        part_ref = ctx.at[pl.ds(h * pairs, pairs)]
        return x_copy(part_ref, part_ref, 11)

    ctx_copy().start()
    lax.fori_loop(0, tiles, far_tile, 0)
    ring_out.reduce(0)
    ring_qkv.reduce(0)
    ring_down.reduce(1)
    ring_up.reduce(1)
    for k in range(1, len(bits)):
        small_step(k)
    mine = gtwo[:, own_cols]
    high = mine.astype(LOW)
    rest = (mine - high.astype(WIDE)).astype(LOW)
    halves = cat([high, rest])

    def near_tile(r, c):
        d = cat([dall[j, row_tile(r), :] for j in range(3 * pairs)])
        spread = dot(sel_t[row_tile(r), :], halves)
        near[row_tile(r), :] = dot_nt(d, wqkv[own_cols, :]) + (spread[:, :own] + spread[:, own:])
        return c

    lax.fori_loop(0, tiles, near_tile, 0)
    ring_down.reduce(2)
    ring_up.reduce(2)
    ctx_copy().wait_recv()

    def down_copy(r):
        return x_copy(down_far.at[row_tile(r)], down_got.at[row_tile(r)], 12 + r)

    def layer_tile(r, c):
        rs = row_tile(r)
        pre_r = tok[rs, :].astype(WIDE) + dot(cat([ctx[j, rs, :] for j in range(2 * pairs)]), wout[...])
        normed = normalize(pre_r)[0] * gain_one[...] + shift_one[...]
        normed_one[...] = normed
        u = dot(normed.astype(LOW), wup[...]) + b_up[...]
        hid = (u * (0.5 * (1.0 + lax.erf(u * root_half)))).astype(LOW)
        down_far[rs, :] = dot(hid, wdown[:, far_cols]).astype(LOW)
        down_copy(r).start()
        pre_two[rs, :] = normed_one[:, own_cols] + dot(hid, wdown[:, own_cols])
        return c

    lax.fori_loop(0, tiles // 2, layer_tile, 0)
    ring_out.reduce(1)
    ring_qkv.reduce(1)
    ring_down.reduce(3)
    ring_up.reduce(3)
    lax.fori_loop(tiles // 2, tiles, layer_tile, 0)
    ring_out.reduce(2)
    ring_qkv.reduce(2)
    ring_down.gather(2)
    ring_up.gather(2)

    def grad_tile(r, c):
        far_copy(r).wait_recv()
        far_copy(r).wait_send()
        far[row_tile(r), :] = (near[row_tile(r), :] + far_got[row_tile(r), :].astype(WIDE)).astype(LOW)
        return c

    lax.fori_loop(0, tiles, grad_tile, 0)
    grad_out = pltpu.make_async_copy(far, grad_tokens, lsem.at[1])
    grad_out.start()
    ring_out.reduce(3)
    ring_qkv.reduce(3)
    ring_down.gather(1)
    ring_up.gather(1)

    first_lane = lax.broadcasted_iota(jnp.int32, (1, LANES), 1) < 1

    def stat_tile(r, c):
        rs = row_tile(r)
        down_copy(r).wait_recv()
        x = pre_two[rs, :] + down_got[rs, :].astype(WIDE)
        pre_two[rs, :] = x
        mean = jnp.mean(x, axis=-1, keepdims=True)
        dev = x - mean
        var = jnp.mean(dev * dev, axis=-1, keepdims=True)
        both = jnp.where(first_lane, mean, var)
        stats[r] = jnp.transpose(both)[:8, :]
        return c

    lax.fori_loop(0, tiles, stat_tile, 0)
    stats_copy = x_copy(stats, stats_got, 16)
    stats_copy.start()
    ring_out.gather(2)
    ring_qkv.gather(2)
    ring_down.gather(0)
    ring_up.gather(0)
    stats_copy.wait_recv()

    def result_tile(r, c):
        rs = row_tile(r)
        x = pre_two[rs, :]
        fill = jnp.zeros((LANES - 8, tile), WIDE)
        one = jnp.transpose(jnp.concatenate([stats[r], fill], axis=0))
        two = jnp.transpose(jnp.concatenate([stats_got[r], fill], axis=0))
        mean = 0.5 * (one[:, :1] + two[:, :1])
        gap = 0.5 * (one[:, :1] - two[:, :1])
        var = 0.5 * (one[:, 1:2] + two[:, 1:2]) + gap * gap
        down_copy(r).wait_send()
        down_far[rs, :] = ((x - mean) * lax.rsqrt(var + norm_eps) * vecs[2:3, own_cols]
                         + vecs[3:4, own_cols]).astype(LOW)
        return c

    lax.fori_loop(0, tiles, result_tile, 0)
    result_out = pltpu.make_async_copy(down_far, result, lsem.at[2])
    result_out.start()
    ring_out.gather(1)
    ring_qkv.gather(1)
    ring_out.gather(0)
    ring_qkv.gather(0)
    for ring in (ring_down, ring_up, ring_out, ring_qkv):
        ring.gather(-1)

    for r in range(tiles):
        tok_copy(r).wait_send()
    grad_out.wait()
    result_out.wait()
    for cp in (ctxc_copy, part_copy, back_copy, ctx_copy(), stats_copy):
        cp.wait_send()
    for k in range(len(bits)):
        small_copy(k).wait_send()
    for ring in (ring_down, ring_up, ring_out, ring_qkv):
        ring.finish()


def build(n, tokens, wqkv, wout, gain_one, shift_one, wup, b_up, wdown, gain_two, shift_two, perm, index,
          count, cot):
    rows, own = tokens.shape
    width = wout.shape[0]
    local = wqkv.shape[2]
    pairs = local // LANES
    heads = local // HEAD_DIM
    slots = index.shape[1]
    ff = wup.shape[1]
    block_len = rows // 2
    tile = 256
    steps = n.bit_length() - 1
    bits = [1 << k for k in range(steps)]
    depth = min(4, steps)
    units = 1 << depth
    halving, extra = bits[:depth], bits[depth:]

    vm = pltpu.VMEM
    groups = {"down": (ff // units, width), "up": (width // units, ff), "out": (local // units, width),
              "qkv": (width // units, 3 * local)}
    orders = {g: halving for g in groups}
    dma = pltpu.SemaphoreType.DMA

    def ring_scratch(g):
        r, c = groups[g]
        sizes = [units >> (k + 1) for k in range(depth)]
        return {
            "recv": [vm((s, r, c), LOW) for s in sizes],
            "send": [vm((s, r, c), LOW) for s in sizes[1:]],
            "keep": [vm((s, r, c), WIDE) for s in sizes[1:]],
            "fin": vm((1, r, c), LOW),
            "xsend": vm((1, r, c) if extra else (1, 8, LANES), LOW),
            "xrecv": vm((len(extra), r, c) if extra else (1, 8, LANES), LOW),
            "sems": (dma((2 * depth + len(extra),)), dma((2 * depth + len(extra),)), dma(())),
        }

    f = [vm((units,) + groups[g], LOW) for g in groups]
    scratch = [
        vm((width, 3 * local), LOW), vm(wout.shape, LOW), vm(wup.shape, LOW), vm(wdown.shape, LOW), dma((6,)),
        vm((8, ff), WIDE),
        vm((rows, width), LOW), vm((3 * pairs, rows, LANES), LOW), vm((rows, slots), LOW), vm((slots, rows), LOW),
        vm((slots, LANES), WIDE), vm((slots, width), LOW), vm((pairs, slots, LANES), LOW),
        vm((heads, slots, block_len), WIDE), vm((2 * pairs, slots, LANES), LOW), vm((slots, width), WIDE),
        vm((slots, LANES), WIDE), vm((slots, width), WIDE), vm((slots, width), LOW), vm((slots, ff), WIDE),
        vm((slots, ff), LOW), vm((slots, width), LOW), vm((slots, width), LOW), vm((slots, width), LOW),
        vm((slots, width), WIDE), vm((slots, ff), LOW), vm((slots, width), LOW), vm((slots, width), LOW),
        vm((slots, width), LOW), vm((pairs, slots, LANES), LOW),
        vm((pairs, slots, LANES), LOW), vm((3 * pairs, rows, LANES), LOW), vm((rows, own), LOW),
        vm((rows, own), LOW), vm((rows, own), WIDE),
        vm((2 * pairs, rows, LANES), LOW), vm((rows, own), WIDE), vm((rows, own), LOW),
        vm((rows, own), LOW), vm((rows // tile, 8, tile), WIDE), vm((rows // tile, 8, tile), WIDE),
        *f, vm((8 * steps, ff), WIDE), vm((8 * steps, ff), WIDE),
        dma((18 + steps,)), dma((18 + steps,)), dma((3,)),
    ]
    plain = len(scratch)
    ring_specs = [ring_scratch(g) for g in groups]
    flat, tree = jax.tree.flatten(ring_specs, is_leaf=lambda x: not isinstance(x, (dict, list, tuple)))
    n_in, n_out = 14, 7

    def run(*refs):
        head_refs = refs[:n_in + n_out + plain]
        rings = jax.tree.unflatten(tree, refs[n_in + n_out + plain:])
        firsts = head_refs[-(len(groups) + 5):-5]
        outs = refs[n_in + 2:n_in + 2 + len(groups)]
        full = []
        for g, ring, first, out in zip(groups, rings, firsts, outs):
            full.append(dict(order=orders[g], extra=extra, first=first, out=out, **ring))
        kernel(n, (*head_refs, full))

    hbm = pl.BlockSpec(memory_space=pl.ANY)
    v = pl.BlockSpec(memory_space=pltpu.VMEM)
    shape = jax.ShapeDtypeStruct
    return pl.pallas_call(
        run,
        out_shape=(shape((rows, own), LOW), shape((rows, own), LOW),
                   *(shape((units,) + groups[g], LOW) for g in groups), shape((8, ff), WIDE)),
        in_specs=[hbm, hbm, hbm, hbm, hbm, v, v, v, v, v, v, v, v, v],
        out_specs=(hbm, hbm, hbm, hbm, hbm, hbm, v),
        scratch_shapes=scratch + flat,
        compiler_params=pltpu.CompilerParams(
            collective_id=0, has_side_effects=True, vmem_limit_bytes=VMEM_BYTES),
        name="layer",
    )(tokens, wqkv, wout, wup, wdown, gain_one, shift_one, gain_two, shift_two, b_up, perm, count, index, cot)


def finish(refs):
    (f_down, f_up, f_out, f_qkv, small, res_in, tok_in,
     down, up, out, qkv, gain_one, shift_one, bias, gain_two, shift_two, res, tok,
     b_down, b_up, b_out, b_qkv, w_down, w_up, w_out, w_qkv, b_res, b_tok, isem, osem) = refs
    width = gain_one.shape[0]
    local = qkv.shape[2]
    reads, writes = [], []

    def read(src, dst):
        cp = pltpu.make_async_copy(src, dst, isem.at[len(reads)])
        cp.start()
        reads.append(cp)
        return cp

    def write(src, dst):
        cp = pltpu.make_async_copy(src, dst, osem.at[len(writes)])
        cp.start()
        writes.append(cp)

    parts = 4
    jobs = []
    for src, low, wide, dst in ((f_down, b_down, w_down, down), (f_up, b_up, w_up, up),
                                (f_out, b_out, w_out, out), (f_qkv, b_qkv, w_qkv, qkv)):
        step = src.shape[0] // parts if src.shape[0] % parts == 0 else src.shape[0]
        for u in range(0, src.shape[0], step):
            jobs.append((read(src.at[pl.ds(u, step)], low.at[pl.ds(u, step)]), u, step, low, wide, dst))
    pass_on = [(read(a, b), b, c) for a, b, c in ((res_in, b_res, res), (tok_in, b_tok, tok))]
    gain_one[...] = small[1:2, :width].reshape(width)
    shift_one[...] = small[1:2, width:].reshape(width)
    gain_two[...] = small[2:3, :width].reshape(width)
    shift_two[...] = small[2:3, width:].reshape(width)
    bias[...] = small[0:1, :].reshape(bias.shape[0])
    for cp, u, step, low, wide, dst in jobs:
        cp.wait()
        r = low.shape[1]

        def unit(j, c, u=u, low=low, wide=wide, r=r, dst=dst):
            v = low[u + j].astype(WIDE)
            rows = pl.ds(pl.multiple_of((u + j) * r, r), r)
            if dst is qkv:
                for k in range(3):
                    wide[k, rows, :] = v[:, k * local:(k + 1) * local]
            else:
                wide[rows, :] = v
            return c

        lax.fori_loop(0, step, unit, 0)
        rows = pl.ds(u * r, step * r)
        if dst is qkv:
            write(wide.at[:, rows, :], dst.at[:, rows, :])
        else:
            write(wide.at[rows, :], dst.at[rows, :])
    for cp, src, dst in pass_on:
        cp.wait()
        write(src, dst)
    for cp in writes:
        cp.wait()


def widen(g_down, g_up, g_out, g_qkv, small, result, grad_tokens):
    units, r_qkv, three = g_qkv.shape
    local, width, ff = three // 3, g_down.shape[2], g_up.shape[2]
    shape = jax.ShapeDtypeStruct
    hbm = pl.BlockSpec(memory_space=pl.ANY)
    v = pl.BlockSpec(memory_space=pltpu.VMEM)
    wide = [(ff, width), (width, ff), (local, width), (3, width, local)]
    low = [g.shape for g in (g_down, g_up, g_out, g_qkv)]
    acts = [result.shape, grad_tokens.shape]
    return pl.pallas_call(
        lambda *refs: finish(refs),
        out_shape=(*(shape(x, WIDE) for x in wide), shape((width,), WIDE), shape((width,), WIDE),
                   shape((ff,), WIDE), shape((width,), WIDE), shape((width,), WIDE),
                   *(shape(x, LOW) for x in acts)),
        in_specs=[hbm, hbm, hbm, hbm, v, hbm, hbm],
        out_specs=(hbm, hbm, hbm, hbm, v, v, v, v, v, hbm, hbm),
        scratch_shapes=[*(pltpu.VMEM(x, LOW) for x in low), *(pltpu.VMEM(x, WIDE) for x in wide),
                        *(pltpu.VMEM(x, LOW) for x in acts), pltpu.SemaphoreType.DMA((18,)),
                        pltpu.SemaphoreType.DMA((18,))],
        compiler_params=pltpu.CompilerParams(vmem_limit_bytes=VMEM_BYTES * 3 // 4),
        name="widen",
    )(g_down, g_up, g_out, g_qkv, small, result, grad_tokens)


def body(n, tokens, w_qkv, w_out, gain_one, attention_norm_bias, w_up, b_up, w_down, gain_two, shift_two,
         block_perm, mask_index, mask_count, cotangent):
    result, grad_tokens, g_down, g_up, g_out, g_qkv, small = build(
        n, tokens, w_qkv.transpose(1, 0, 2), w_out, gain_one, attention_norm_bias, w_up, b_up, w_down, gain_two,
        shift_two, block_perm.T, mask_index, mask_count.reshape(1, 1), cotangent[0])
    (g_down, g_up, g_out, g_qkv, g_gain_one, g_shift_one, g_bias, g_gain_two, g_shift_two, result,
     grad_tokens) = widen(g_down, g_up, g_out, g_qkv, small, result, grad_tokens)
    return (result, grad_tokens, g_qkv.transpose(1, 0, 2), g_out, g_gain_one, g_shift_one, g_up, g_bias, g_down,
            g_gain_two, g_shift_two)


def solution(mesh):
    return jax.shard_map(
        functools.partial(body, mesh.shape["batch"]),
        mesh=mesh,
        in_specs=(P("batch", "head"), P(None, None, "head"), P(), P(), P(), P(None, "head"), P("head"),
                  P("head", None), P(), P(), P("head", None), P("batch", None), P("batch"),
                  P("batch", None, None)),
        out_specs=(P("batch", "head"), P("batch", "head"), P(None, None, "head"), P("head", None), P(), P(),
                   P(None, "head"), P("head"), P("head", None), P(), P()),
        check_vma=False,
    )
```

```python
import functools

import jax
import jax.numpy as jnp
from jax import lax
from jax.experimental import pallas as pl
from jax.experimental.pallas import tpu as pltpu
from jax.sharding import PartitionSpec as P

HEAD_DIM = 64
norm_eps = 1e-06
root_half = 0.7071067811865476
inv_root_two_pi = 0.3989422804014327
log2_e = 1.4426950408889634
LOW = jnp.bfloat16
WIDE = jnp.float32
LANES = 128
MESH = pl.DeviceIdType.MESH
VMEM_BYTES = 67043328
CUTS = (2, 4)
CHUNKS = {"D": 2, "U": 2, "O": 1, "Q": 2}
ORDERS = {"D": [[0, 1, 2, 3], [0, 1, 2, 3]], "U": [[0, 2, 1, 3], [0, 1, 2, 3]],
          "O": [[0, 1, 2, 3]], "Q": [[0, 1, 2, 3], [0, 2, 1, 3]]}
PLAN = (
    ("D0", 0), ("D1", 0), ("U0", 0), ("attend",), ("U1", 0), ("layer", 0), ("layer", 1), ("D0", 1), ("U0", 1),
    ("norm",), ("mb", 0), ("D1", 1), ("mb", 1), ("D0", 2), ("small", 0), ("mb", 2), ("out",), ("U1", 1),
    ("D1", 2), ("qkv", 0), ("O0", 0), ("small", 1), ("qkv", 1), ("U0", 2), ("D0", 3), ("Q0", 0), ("U1", 2),
    ("far", 0), ("Q1", 0), ("D1", 3), ("small", 2), ("far", 1), ("O0", 1), ("far", 2), ("far", 3), ("layer", 2),
    ("U0", 3), ("Q0", 1), ("Q1", 1), ("D0", 4), ("small", 3), ("layer", 3), ("O0", 2), ("U1", 3), ("Q0", 2),
    ("Q1", 2), ("near", 0), ("near", 1), ("D1", 4), ("near", 2), ("D0", 5), ("near", 3), ("grad", 0),
    ("grad", 1), ("grad", 2), ("U0", 4), ("stat", 0), ("stat", 1), ("O0", 3), ("grad", 3), ("gout",), ("D1", 5),
    ("U1", 4), ("stat", 2), ("D0", 6), ("Q0", 3), ("D0", 7), ("Q1", 3), ("U1", 5), ("U0", 5), ("stat", 3),
    ("O0", 4), ("stats",), ("Q0", 4), ("result",), ("Q1", 4), ("D1", 6), ("U0", 6), ("D1", 7), ("O0", 5),
    ("U0", 7), ("Q0", 5), ("U1", 6), ("Q1", 5), ("U1", 7), ("O0", 6), ("O0", 7), ("Q1", 6), ("Q0", 6),
    ("Q1", 7), ("Q0", 7),
)


def dot(a, b):
    return lax.dot_general(a, b, (((1,), (0,)), ((), ())), preferred_element_type=WIDE)


def dot_nt(a, b):
    return lax.dot_general(a, b, (((1,), (1,)), ((), ())), preferred_element_type=WIDE)


def dot_tn(a, b):
    return lax.dot_general(a, b, (((0,), (0,)), ((), ())), preferred_element_type=WIDE)


def normalize(values):
    centered = values - jnp.mean(values, axis=-1, keepdims=True)
    inverse = lax.rsqrt(jnp.mean(centered * centered, axis=-1, keepdims=True) + norm_eps)
    return centered * inverse, inverse


def norm_backward(upstream, normal, inverse, gain_vec):
    scaled = upstream * gain_vec
    return inverse * (
        scaled
        - jnp.mean(scaled, axis=-1, keepdims=True)
        - normal * jnp.mean(scaled * normal, axis=-1, keepdims=True)
    )


def col_sum(x):
    return jnp.sum(x, axis=0, keepdims=True)


def cat(parts):
    return jnp.concatenate(parts, axis=1)


class Ring:
    def __init__(self, order, extra, first, out, recv, send, keep, fin, xsend, xrecv, sems, peer, bit_of):
        self.order, self.extra = order, extra
        self.first, self.out = first, out
        self.recv, self.send, self.keep, self.fin = recv, send, keep, fin
        self.xsend, self.xrecv = xsend, xrecv
        self.ssem, self.rsem, self.lsem = sems
        self.peer = peer
        self.mine = [bit_of(b) for b in order]
        units = first.shape[0]
        self.sizes = [units >> (k + 1) for k in range(len(order))]
        self.base = []
        base = 0
        for k in range(len(order)):
            base = base + self.mine[k] * self.sizes[k]
            self.base.append(base)

    def _copy(self, src, dst, slot, bit):
        return pltpu.make_async_remote_copy(
            src_ref=src, dst_ref=dst, send_sem=self.ssem.at[slot], recv_sem=self.rsem.at[slot],
            device_id=self.peer(bit), device_id_type=MESH)

    def _rs(self, k):
        size = self.sizes[k]
        if k == 0:
            src = self.first.at[pl.ds((1 - self.mine[0]) * size, size)]
        else:
            src = self.send[k - 1]
        return self._copy(src, self.recv[k], k, self.order[k])

    def _x(self, j):
        return self._copy(self.xsend, self.xrecv.at[pl.ds(j, 1)], len(self.order) + j, self.extra[j])

    def _ag(self, k):
        last = len(self.order) - 1
        slot = len(self.order) + len(self.extra) + k
        if k == last:
            return self._copy(self.fin, self.out.at[pl.ds(self.base[k], 1)], slot, self.order[k])
        size = self.sizes[k]
        part = self.out.at[pl.ds(self.base[k], size)]
        return self._copy(part, part, slot, self.order[k])

    def _own(self):
        return pltpu.make_async_copy(self.fin, self.out.at[pl.ds(self.base[-1], 1)], self.lsem)

    def start(self):
        self._rs(0).start()

    def _value(self, k, u):
        got = self.recv[k][u].astype(WIDE)
        if k == 0:
            return self.first[self.mine[0] * self.sizes[0] + u].astype(WIDE) + got
        return self.keep[k - 1][u] + got

    def reduce(self, k):
        self._rs(k).wait_recv()
        if k + 1 < len(self.order):
            half = self.sizes[k + 1]
            mine = self.mine[k + 1]

            def out_part(j, c):
                self.send[k][j] = self._value(k, (1 - mine) * half + j).astype(LOW)
                return c

            lax.fori_loop(0, half, out_part, 0)
            self._rs(k + 1).start()

            def own_part(j, c):
                self.keep[k][j] = self._value(k, mine * half + j)
                return c

            lax.fori_loop(0, half, own_part, 0)
        else:
            total = self._value(k, 0)
            for j in range(len(self.extra)):
                self.xsend[0] = total.astype(LOW)
                self._x(j).start()
                self._x(j).wait()
                total = self.xsend[0].astype(WIDE) + self.xrecv[j].astype(WIDE)
            self.fin[0] = total.astype(LOW)
            self._ag(k).start()
            self._own().start()

    def gather(self, k):
        self._ag(k + 1).wait_recv()
        if k + 2 == len(self.order):
            self._own().wait()
        if k >= 0:
            self._ag(k).start()

    def advance(self, stage):
        depth = len(self.order)
        if stage < depth:
            self.reduce(stage)
        else:
            self.gather(2 * depth - 2 - stage)

    def finish(self):
        for k in range(len(self.order)):
            self._rs(k).wait_send()
            self._ag(k).wait_send()


def kernel(n, refs):
    (tokens, wqkv_hbm, wout_hbm, wup_hbm, wdown_hbm, *vectors,
     perm, count, index, cot,
     result, grad_tokens, o_down, o_up, o_out, o_qkv, small_out,
     wqkv, wout, wup, wdown, wsem, vecs,
     tok, qkv, sel_t, sel, blk, tokc, qc, probs, ctxc, normal_one, inverse_one, normed_one, low_one, slope,
     hidden, part, part_got, gb, gtwo, gin, back, back_got, gattn, gctx, dqc, dall, far, far_got, near,
     ctx, pre_two, down_far, down_got, stats, stats_got,
     f_down, f_up, f_out, f_qkv, small, small_got,
     xs_send, xs_recv, lsem, rings) = refs
    rows, own = tokens.shape
    width = wout.shape[0]
    local = wqkv.shape[1] // 3
    pairs = local // LANES
    slots = index.shape[1]
    ff = wup.shape[1]
    block_len = rows // 2
    tile = 256
    tiles = rows // tile
    scale = HEAD_DIM ** (-0.5)
    b = lax.axis_index("batch")
    h = lax.axis_index("head")
    other = 1 - h
    bits = [1 << k for k in range(n.bit_length() - 1)]

    def bit_of(bit):
        return lax.rem(lax.div(b, bit), 2)

    def peer(bit):
        return (b + bit - 2 * bit * bit_of(bit), h)

    x_peer = (b, other)

    def x_copy(src, dst, slot):
        return pltpu.make_async_remote_copy(
            src_ref=src, dst_ref=dst, send_sem=xs_send.at[slot], recv_sem=xs_recv.at[slot],
            device_id=x_peer, device_id_type=MESH)

    loads = [pltpu.make_async_copy(s, d, wsem.at[i]) for i, (s, d) in enumerate(
        [(wqkv_hbm.at[j], wqkv.at[:, pl.ds(j * local, local)]) for j in range(3)]
        + [(wout_hbm, wout), (wup_hbm, wup), (wdown_hbm, wdown)])]
    for cp in loads:
        cp.start()
    barrier = pltpu.get_barrier_semaphore()
    pl.semaphore_signal(barrier, inc=1, device_id=x_peer, device_id_type=MESH)
    for bit in bits:
        pl.semaphore_signal(barrier, inc=1, device_id=peer(bit), device_id_type=MESH)
    pl.semaphore_wait(barrier, 1 + len(bits))

    own_cols = pl.ds(pl.multiple_of(h * own, LANES), own)
    far_cols = pl.ds(pl.multiple_of(other * own, LANES), own)

    def row_tile(r):
        return pl.ds(pl.multiple_of(r * tile, tile), tile)

    def tok_copy(r):
        return x_copy(tokens.at[row_tile(r)], tok.at[row_tile(r), own_cols], r)

    for r in range(tiles):
        tok_copy(r).start()
    own_tok = pltpu.make_async_copy(tokens, tok.at[:, own_cols], lsem.at[0])
    own_tok.start()

    for i, vector in enumerate(vectors):
        vecs[i:i + 1, :vector.shape[0]] = vector[...].reshape(1, -1)
    gain_one, shift_one, gain_two, shift_two = (vecs.at[i:i + 1, :width] for i in range(4))
    b_up = vecs.at[4:5, :]

    lane_slot = lax.broadcasted_iota(jnp.int32, (1, slots), 1)
    idx = jnp.where(lane_slot < count[...], index[...], -1)
    picked = jnp.where(lax.broadcasted_iota(jnp.int32, (rows, slots), 0) == idx, 1.0, 0.0)
    sel_t[...] = picked.astype(LOW)
    picked = jnp.transpose(picked)
    sel[...] = picked.astype(LOW)
    blk[...] = jnp.broadcast_to(jnp.sum(picked[:, block_len:], axis=1, keepdims=True), blk.shape)
    own_tok.wait()
    for cp in loads[:3]:
        cp.wait()

    def qkv_tile(r, c):
        tok_copy(r).wait_recv()
        out = dot(tok[row_tile(r), :], wqkv[...]).astype(LOW)
        for j in range(3 * pairs):
            qkv[j, row_tile(r), :] = out[:, j * LANES:(j + 1) * LANES]
        return c

    lax.fori_loop(0, tiles, qkv_tile, 0)

    low_lane = lax.broadcasted_iota(jnp.int32, (1, LANES), 1) < HEAD_DIM
    tokc[...] = dot(sel[...], tok[...]).astype(LOW)

    def keep_head(x, e):
        return jnp.where(low_lane, x, 0.0).astype(LOW) if e == 0 else jnp.where(low_lane, 0.0, x).astype(LOW)

    order = perm[...].astype(WIDE)
    head_lane = lax.broadcasted_iota(jnp.int32, order.shape, 1)

    def blocks_of(head):
        return jnp.sum(jnp.where(head_lane == head, order, 0.0), axis=1, keepdims=True)

    def second(head):
        pair = blocks_of(head)
        return (pair[:1] + blk[:, :1] * (pair[1:] - pair[:1])) > 0.5

    def masked_attention(p, c):
        q2 = dot(sel[...], qkv[p]).astype(LOW)
        qc[p] = q2
        halves = []
        for e in range(2):
            head = 2 * p + e
            late = second(head)
            qm = keep_head(q2.astype(WIDE), e)
            s = jnp.where(late, dot_nt(qm, qkv[pairs + p, block_len:, :]),
                          dot_nt(qm, qkv[pairs + p, :block_len, :])) * (scale * log2_e)
            ex = jnp.exp2(s - jnp.max(s, axis=-1, keepdims=True))
            pr = ex * (1.0 / jnp.sum(ex, axis=-1, keepdims=True))
            probs[head] = pr
            pr = pr.astype(LOW)
            halves.append(jnp.where(late, dot(pr, qkv[2 * pairs + p, block_len:, :]),
                                    dot(pr, qkv[2 * pairs + p, :block_len, :])))
        ctxc[h * pairs + p] = jnp.where(low_lane, halves[0], halves[1]).astype(LOW)
        ctxc_copy(p).start()
        return c

    def ctxc_copy(p):
        mine_c = ctxc.at[pl.ds(h * pairs + p, 1)]
        return x_copy(mine_c, mine_c, tiles + p)

    lax.fori_loop(0, pairs, masked_attention, 0)

    def attend(i, c):
        p = lax.rem(i, pairs)
        q_block = lax.div(i, pairs)
        q_rows = pl.ds(pl.multiple_of(q_block * block_len, block_len), block_len)
        q2 = qkv[p, q_rows, :].astype(WIDE)
        even, odd = blocks_of(2 * p), blocks_of(2 * p + 1)
        late = jnp.where(low_lane, jnp.where(q_block == 0, even[:1], even[1:]),
                         jnp.where(q_block == 0, odd[:1], odd[1:])) > 0.5

        def chosen(j):
            return jnp.where(late, qkv[j, block_len:, :].astype(WIDE), qkv[j, :block_len, :].astype(WIDE)).astype(LOW)

        k2, v2 = chosen(pairs + p), chosen(2 * pairs + p)
        halves = []
        for e in range(2):
            s = dot_nt(keep_head(q2, e), k2) * (scale * log2_e)
            ex = jnp.exp2(s - jnp.max(s, axis=-1, keepdims=True))
            inv = 1.0 / jnp.sum(ex, axis=-1, keepdims=True)
            halves.append(dot(ex.astype(LOW), v2) * inv)
        ctx[h * pairs + p, q_rows, :] = jnp.where(low_lane, halves[0], halves[1]).astype(LOW)
        ctx_copy(i).start()
        return c

    x_base = tiles + pairs

    def ctx_copy(i):
        q_rows = pl.ds(pl.multiple_of(lax.div(i, pairs) * block_len, block_len), block_len)
        part_ref = ctx.at[pl.ds(h * pairs + lax.rem(i, pairs), 1), q_rows]
        return x_copy(part_ref, part_ref, x_base + i)

    attend_units = 2 * pairs
    x_base2 = x_base + attend_units
    lax.fori_loop(0, CUTS[0], attend, 0)

    for p in range(pairs):
        ctxc_copy(p).wait_recv()
    for cp in loads[3:]:
        cp.wait()
    pre = tokc[...].astype(WIDE) + dot(cat([ctxc[j] for j in range(2 * pairs)]), wout[...])
    nrm_c, inv_c = normalize(pre)
    normal_one[...] = nrm_c
    inverse_one[...] = jnp.broadcast_to(inv_c, inverse_one.shape)
    nrm_c = nrm_c * gain_one[...] + shift_one[...]
    normed_one[...] = nrm_c
    low_one[...] = nrm_c.astype(LOW)
    ff_tile = 384

    def up_tile(i, c):
        cols = pl.ds(pl.multiple_of(i * ff_tile, ff_tile), ff_tile)
        u = dot(low_one[...], wup[:, cols]) + vecs[4:5, cols]
        cdf = 0.5 * (1.0 + lax.erf(u * root_half))
        hidden[:, cols] = (u * cdf).astype(LOW)
        slope[:, cols] = cdf + u * inv_root_two_pi * jnp.exp(-0.5 * u * u)
        return c

    lax.fori_loop(0, ff // ff_tile, up_tile, 0)
    part[...] = dot(hidden[...], wdown[...]).astype(LOW)
    part_copy = x_copy(part, part_got, x_base2)
    part_copy.start()
    lax.fori_loop(CUTS[0], CUTS[1], attend, 0)
    part_copy.wait_recv()

    normal_two, inv_two = normalize(normed_one[...] + (part[...].astype(WIDE) + part_got[...].astype(WIDE)))
    alive = lax.broadcasted_iota(jnp.int32, (slots, 1), 0) < count[...]
    up = jnp.where(alive, cot[...].astype(WIDE), 0.0)
    g2 = norm_backward(up, normal_two, inv_two, gain_two[...])
    gtwo[...] = g2
    gb[...] = g2.astype(LOW)
    small[2:3, :] = cat([col_sum(up * normal_two), col_sum(up)])

    def put(first, unit, value):
        r = first.shape[1]
        for j in range(value.shape[0] // r):
            first[unit + j] = value[j * r:(j + 1) * r, :]

    ring = {name: Ring(peer=peer, bit_of=bit_of, **r) for name, r in rings.items()}

    def down_tile(i, c):
        cols = pl.ds(pl.multiple_of(i * ff_tile, ff_tile), ff_tile)
        put(f_down, i * (ff_tile * f_down.shape[0] // ff), dot_tn(hidden[:, cols], gb[...]).astype(LOW))
        return c

    def up_grad_tile(i, c):
        cols = pl.ds(pl.multiple_of(i * ff_tile, ff_tile), ff_tile)
        put(f_up, i * (ff_tile * f_up.shape[0] // width), dot_tn(low_one[:, cols], gin[...]).astype(LOW))
        return c

    def in_tile(i, c):
        cols = pl.ds(pl.multiple_of(i * ff_tile, ff_tile), ff_tile)
        g = (dot_nt(gb[...], wdown[cols, :]) * slope[:, cols]).astype(LOW)
        gin[:, cols] = g
        small[0:1, cols] = col_sum(g.astype(WIDE))
        return c

    back_copy = x_copy(back, back_got, x_base2 + 1)
    for k in range(2):
        lax.fori_loop(k * ff // (2 * ff_tile), (k + 1) * ff // (2 * ff_tile), down_tile, 0)
        ring["D%d" % k].start()
    lax.fori_loop(0, ff // ff_tile, in_tile, 0)
    back[...] = dot_nt(gin[...], wup[...]).astype(LOW)
    back_copy.start()
    for k in range(2):
        lax.fori_loop(k * width // (2 * ff_tile), (k + 1) * width // (2 * ff_tile), up_grad_tile, 0)
        ring["U%d" % k].start()

    def attend_more():
        lax.fori_loop(CUTS[1], attend_units, attend, 0)

    own_rows = pl.ds(pl.multiple_of(h * local, LANES), local)

    def first_norm():
        back_copy.wait_recv()
        gn = gtwo[...] + (back[...].astype(WIDE) + back_got[...].astype(WIDE))
        small[1:2, :] = cat([col_sum(gn * normal_one[...]), col_sum(gn)])
        g1 = norm_backward(gn, normal_one[...], inverse_one[:, :1], gain_one[...])
        gtwo[...] = g1
        gattn[...] = g1.astype(LOW)
        gc = dot_nt(gattn[...], wout[own_rows, :]).astype(LOW)
        for p in range(pairs):
            gctx[p] = gc[:, p * LANES:(p + 1) * LANES]
        small[3:8, :] = jnp.zeros((5, small.shape[1]), WIDE)
        small_copy(0).start()

    def masked_backward(p, c):
        q2 = qc[p].astype(WIDE)
        g2 = gctx[p].astype(WIDE)
        k2 = cat([qkv[pairs + p, :block_len, :], qkv[pairs + p, block_len:, :]])
        dk = jnp.zeros((block_len, 2 * LANES), WIDE)
        dv = jnp.zeros((block_len, 2 * LANES), WIDE)
        dq = []
        for e in range(2):
            head = 2 * p + e
            late = second(head)
            gm = keep_head(g2, e)
            dp = jnp.where(late, dot_nt(gm, qkv[2 * pairs + p, block_len:, :]),
                           dot_nt(gm, qkv[2 * pairs + p, :block_len, :]))
            pr = probs[head]
            t = dp * pr
            ds = (t - pr * jnp.sum(t, axis=-1, keepdims=True)).astype(LOW)
            qm = keep_head(q2, e).astype(WIDE)
            gm = gm.astype(WIDE)
            dk = dk + dot_tn(ds, cat([jnp.where(late, 0.0, qm), jnp.where(late, qm, 0.0)]).astype(LOW))
            dv = dv + dot_tn(pr.astype(LOW),
                             cat([jnp.where(late, 0.0, gm), jnp.where(late, gm, 0.0)]).astype(LOW))
            both = dot(ds, k2)
            dq.append(jnp.where(late, both[:, LANES:], both[:, :LANES]))
        d = (jnp.where(low_lane, dq[0], dq[1]) * scale).astype(LOW)
        dqc[p] = d
        dall[p] = dot(sel_t[...], d).astype(LOW)
        dk = (dk * scale).astype(LOW)
        dv = dv.astype(LOW)
        dall[pairs + p, :block_len, :] = dk[:, :LANES]
        dall[pairs + p, block_len:, :] = dk[:, LANES:]
        dall[2 * pairs + p, :block_len, :] = dv[:, :LANES]
        dall[2 * pairs + p, block_len:, :] = dv[:, LANES:]
        return c

    def small_copy(k):
        return pltpu.make_async_remote_copy(
            src_ref=small.at[pl.ds(8 * k, 8)], dst_ref=small_got.at[pl.ds(8 * k, 8)],
            send_sem=xs_send.at[x_slots + k], recv_sem=xs_recv.at[x_slots + k],
            device_id=peer(bits[k]), device_id_type=MESH)

    def small_step(k):
        small_copy(k).wait_recv()
        total = small[8 * k:8 * k + 8, :] + small_got[8 * k:8 * k + 8, :]
        if k + 1 < len(bits):
            small[8 * k + 8:8 * k + 16, :] = total
            small_copy(k + 1).start()
        else:
            small_out[...] = total

    def out_grad():
        put(f_out, 0, dot_tn(cat([ctxc[h * pairs + p] for p in range(pairs)]), gattn[...]).astype(LOW))
        ring["O0"].start()

    def qkv_grad_tile(i, c):
        cols = pl.ds(pl.multiple_of(i * ff_tile, ff_tile), ff_tile)
        gq = dot_tn(tokc[:, cols], cat([dqc[p] for p in range(pairs)]))
        gkv = dot_tn(tok[:, cols], cat([dall[pairs + j] for j in range(2 * pairs)]))
        put(f_qkv, i * (ff_tile * f_qkv.shape[0] // width), cat([gq, gkv]).astype(LOW))
        return c

    def qkv_grad(k):
        lax.fori_loop(k * width // (2 * ff_tile), (k + 1) * width // (2 * ff_tile), qkv_grad_tile, 0)
        ring["Q%d" % k].start()

    def far_copy(r):
        return x_copy(far.at[row_tile(r)], far_got.at[row_tile(r)], x_base2 + 2 + r)

    def far_tile(r):
        d = cat([dall[j, row_tile(r), :] for j in range(3 * pairs)])
        far[row_tile(r), :] = dot_nt(d, wqkv[far_cols, :]).astype(LOW)
        far_copy(r).start()

    def near_tile(r):
        mine = gtwo[:, own_cols]
        high = mine.astype(LOW)
        rest = (mine - high.astype(WIDE)).astype(LOW)
        d = cat([dall[j, row_tile(r), :] for j in range(3 * pairs)])
        spread = dot(sel_t[row_tile(r), :], cat([high, rest]))
        near[row_tile(r), :] = dot_nt(d, wqkv[own_cols, :]) + (spread[:, :own] + spread[:, own:])

    def grad_tile(r):
        far_copy(r).wait_recv()
        far_copy(r).wait_send()
        far[row_tile(r), :] = (near[row_tile(r), :] + far_got[row_tile(r), :].astype(WIDE)).astype(LOW)

    grad_out = pltpu.make_async_copy(far, grad_tokens, lsem.at[1])

    def down_copy(r):
        return x_copy(down_far.at[row_tile(r)], down_got.at[row_tile(r)], x_base2 + 2 + tiles + r)

    def layer_tile(r):
        if r * tile % block_len == 0:
            block = r * tile // block_len
            for i in range(block * pairs, (block + 1) * pairs):
                ctx_copy(i).wait_recv()
        rs = row_tile(r)
        pre_r = tok[rs, :].astype(WIDE) + dot(cat([ctx[j, rs, :] for j in range(2 * pairs)]), wout[...])
        normed = normalize(pre_r)[0] * gain_one[...] + shift_one[...]
        normed_one[...] = normed
        u = dot(normed.astype(LOW), wup[...]) + b_up[...]
        hid = (u * (0.5 * (1.0 + lax.erf(u * root_half)))).astype(LOW)
        down_far[rs, :] = dot(hid, wdown[:, far_cols]).astype(LOW)
        down_copy(r).start()
        pre_two[rs, :] = normed_one[:, own_cols] + dot(hid, wdown[:, own_cols])

    first_lane = lax.broadcasted_iota(jnp.int32, (1, LANES), 1) < 1
    stats_copy = x_copy(stats, stats_got, x_base2 + 2 + 2 * tiles)

    def stat_tile(r):
        rs = row_tile(r)
        down_copy(r).wait_recv()
        x = pre_two[rs, :] + down_got[rs, :].astype(WIDE)
        pre_two[rs, :] = x
        mean = jnp.mean(x, axis=-1, keepdims=True)
        dev = x - mean
        var = jnp.mean(dev * dev, axis=-1, keepdims=True)
        both = jnp.where(first_lane, mean, var)
        stats[r] = jnp.transpose(both)[:8, :]

    def result_tile(r, c):
        rs = row_tile(r)
        x = pre_two[rs, :]
        fill = jnp.zeros((LANES - 8, tile), WIDE)
        one = jnp.transpose(jnp.concatenate([stats[r], fill], axis=0))
        two = jnp.transpose(jnp.concatenate([stats_got[r], fill], axis=0))
        mean = 0.5 * (one[:, :1] + two[:, :1])
        gap = 0.5 * (one[:, :1] - two[:, :1])
        var = 0.5 * (one[:, 1:2] + two[:, 1:2]) + gap * gap
        down_copy(r).wait_send()
        down_far[rs, :] = ((x - mean) * lax.rsqrt(var + norm_eps) * vecs[2:3, own_cols]
                         + vecs[3:4, own_cols]).astype(LOW)
        return c

    result_out = pltpu.make_async_copy(down_far, result, lsem.at[2])

    def write_result():
        stats_copy.wait_recv()
        lax.fori_loop(0, tiles, result_tile, 0)
        result_out.start()

    x_slots = x_base2 + 3 + 2 * tiles
    steps = {"norm": first_norm, "attend": attend_more, "mb": lambda p: masked_backward(p, 0), "out": out_grad,
             "qkv": qkv_grad, "far": far_tile, "near": near_tile, "grad": grad_tile, "layer": layer_tile,
             "stat": stat_tile, "stats": stats_copy.start, "gout": grad_out.start, "result": write_result,
             "small": small_step}
    for name, *at in PLAN:
        if name in ring:
            ring[name].advance(at[0])
        else:
            steps[name](*at)
    for k in range(min(len(bits), 4), len(bits)):
        small_step(k)

    for r in range(tiles):
        tok_copy(r).wait_send()
    grad_out.wait()
    result_out.wait()
    for i in range(attend_units):
        ctx_copy(i).wait_send()
    for p in range(pairs):
        ctxc_copy(p).wait_send()
    for cp in (part_copy, back_copy, stats_copy):
        cp.wait_send()
    for k in range(len(bits)):
        small_copy(k).wait_send()
    for one in ring.values():
        one.finish()


def build(n, tokens, wqkv, wout, gain_one, shift_one, wup, b_up, wdown, gain_two, shift_two, perm, index,
          count, cot):
    rows, own = tokens.shape
    width = wout.shape[0]
    local = wqkv.shape[2]
    pairs = local // LANES
    heads = local // HEAD_DIM
    slots = index.shape[1]
    ff = wup.shape[1]
    block_len = rows // 2
    tile = 256
    steps = n.bit_length() - 1
    bits = [1 << k for k in range(steps)]
    depth = min(4, steps)
    units = 1 << depth
    halving, extra = bits[:depth], bits[depth:]

    vm = pltpu.VMEM
    groups = {"D": (ff, width), "U": (width, ff), "O": (local, width), "Q": (width, 3 * local)}
    shapes = {g: (CHUNKS[g] * units, r // (CHUNKS[g] * units), c) for g, (r, c) in groups.items()}
    names = [(g, k) for g in groups for k in range(CHUNKS[g])]
    dma = pltpu.SemaphoreType.DMA

    def ring_scratch(g):
        _, r, c = shapes[g]
        sizes = [units >> (k + 1) for k in range(depth)]
        return {
            "recv": [vm((s, r, c), LOW) for s in sizes],
            "send": [vm((s, r, c), LOW) for s in sizes[1:]],
            "keep": [vm((s, r, c), WIDE) for s in sizes[1:]],
            "fin": vm((1, r, c), LOW),
            "xsend": vm((1, r, c) if extra else (1, 8, LANES), LOW),
            "xrecv": vm((len(extra), r, c) if extra else (1, 8, LANES), LOW),
            "sems": (dma((2 * depth + len(extra),)), dma((2 * depth + len(extra),)), dma(())),
        }

    f = [vm(shapes[g], LOW) for g in groups]
    x_slots = 3 * (rows // tile) + 3 * pairs + 3
    scratch = [
        vm((width, 3 * local), LOW), vm(wout.shape, LOW), vm(wup.shape, LOW), vm(wdown.shape, LOW), dma((6,)),
        vm((8, ff), WIDE),
        vm((rows, width), LOW), vm((3 * pairs, rows, LANES), LOW), vm((rows, slots), LOW), vm((slots, rows), LOW),
        vm((slots, LANES), WIDE), vm((slots, width), LOW), vm((pairs, slots, LANES), LOW),
        vm((heads, slots, block_len), WIDE), vm((2 * pairs, slots, LANES), LOW), vm((slots, width), WIDE),
        vm((slots, LANES), WIDE), vm((slots, width), WIDE), vm((slots, width), LOW), vm((slots, ff), WIDE),
        vm((slots, ff), LOW), vm((slots, width), LOW), vm((slots, width), LOW), vm((slots, width), LOW),
        vm((slots, width), WIDE), vm((slots, ff), LOW), vm((slots, width), LOW), vm((slots, width), LOW),
        vm((slots, width), LOW), vm((pairs, slots, LANES), LOW),
        vm((pairs, slots, LANES), LOW), vm((3 * pairs, rows, LANES), LOW), vm((rows, own), LOW),
        vm((rows, own), LOW), vm((rows, own), WIDE),
        vm((2 * pairs, rows, LANES), LOW), vm((rows, own), WIDE), vm((rows, own), LOW),
        vm((rows, own), LOW), vm((rows // tile, 8, tile), WIDE), vm((rows // tile, 8, tile), WIDE),
        *f, vm((8 * steps, ff), WIDE), vm((8 * steps, ff), WIDE),
        dma((x_slots + steps,)), dma((x_slots + steps,)), dma((3,)),
    ]
    plain = len(scratch)
    ring_specs = [ring_scratch(g) for g, _ in names]
    flat, tree = jax.tree.flatten(ring_specs, is_leaf=lambda x: not isinstance(x, (dict, list, tuple)))
    n_in, n_out = 14, 7

    def run(*refs):
        head_refs = refs[:n_in + n_out + plain]
        rings = jax.tree.unflatten(tree, refs[n_in + n_out + plain:])
        firsts = head_refs[-(len(groups) + 5):-5]
        outs = refs[n_in + 2:n_in + 2 + len(groups)]
        full = {}
        for (g, k), ring in zip(names, rings):
            i = list(groups).index(g)
            part = pl.ds(k * units, units)
            full["%s%d" % (g, k)] = dict(order=[halving[j] for j in ORDERS[g][k] if j < depth], extra=extra,
                                         first=firsts[i].at[part], out=outs[i].at[part], **ring)
        kernel(n, (*head_refs, full))

    hbm = pl.BlockSpec(memory_space=pl.ANY)
    v = pl.BlockSpec(memory_space=pltpu.VMEM)
    shape = jax.ShapeDtypeStruct
    return pl.pallas_call(
        run,
        out_shape=(shape((rows, own), LOW), shape((rows, own), LOW),
                   *(shape(shapes[g], LOW) for g in groups), shape((8, ff), WIDE)),
        in_specs=[hbm, hbm, hbm, hbm, hbm, v, v, v, v, v, v, v, v, v],
        out_specs=(hbm, hbm, hbm, hbm, hbm, hbm, v),
        scratch_shapes=scratch + flat,
        compiler_params=pltpu.CompilerParams(
            collective_id=0, has_side_effects=True, vmem_limit_bytes=VMEM_BYTES),
        name="layer",
    )(tokens, wqkv, wout, wup, wdown, gain_one, shift_one, gain_two, shift_two, b_up, perm, count, index, cot)


def finish(refs):
    (f_down, f_up, f_out, f_qkv, small, res_in, tok_in,
     down, up, out, qkv, gain_one, shift_one, bias, gain_two, shift_two, res, tok,
     b_down, b_up, b_out, b_qkv, w_down, w_up, w_out, w_qkv, b_res, b_tok, isem, osem) = refs
    width = gain_one.shape[0]
    local = qkv.shape[2]
    reads, writes = [], []

    def read(src, dst):
        cp = pltpu.make_async_copy(src, dst, isem.at[len(reads)])
        cp.start()
        reads.append(cp)
        return cp

    def write(src, dst):
        cp = pltpu.make_async_copy(src, dst, osem.at[len(writes)])
        cp.start()
        writes.append(cp)

    parts = 4
    jobs = []
    for src, low, wide, dst in ((f_down, b_down, w_down, down), (f_up, b_up, w_up, up),
                                (f_out, b_out, w_out, out), (f_qkv, b_qkv, w_qkv, qkv)):
        step = src.shape[0] // parts if src.shape[0] % parts == 0 else src.shape[0]
        for u in range(0, src.shape[0], step):
            jobs.append((read(src.at[pl.ds(u, step)], low.at[pl.ds(u, step)]), u, step, low, wide, dst))
    pass_on = [(read(a, b), b, c) for a, b, c in ((res_in, b_res, res), (tok_in, b_tok, tok))]
    gain_one[...] = small[1:2, :width].reshape(width)
    shift_one[...] = small[1:2, width:].reshape(width)
    gain_two[...] = small[2:3, :width].reshape(width)
    shift_two[...] = small[2:3, width:].reshape(width)
    bias[...] = small[0:1, :].reshape(bias.shape[0])
    for cp, u, step, low, wide, dst in jobs:
        cp.wait()
        r = low.shape[1]

        def unit(j, c, u=u, low=low, wide=wide, r=r, dst=dst):
            v = low[u + j].astype(WIDE)
            rows = pl.ds(pl.multiple_of((u + j) * r, r), r)
            if dst is qkv:
                for k in range(3):
                    wide[k, rows, :] = v[:, k * local:(k + 1) * local]
            else:
                wide[rows, :] = v
            return c

        lax.fori_loop(0, step, unit, 0)
        rows = pl.ds(u * r, step * r)
        if dst is qkv:
            write(wide.at[:, rows, :], dst.at[:, rows, :])
        else:
            write(wide.at[rows, :], dst.at[rows, :])
    for cp, src, dst in pass_on:
        cp.wait()
        write(src, dst)
    for cp in writes:
        cp.wait()


def widen(g_down, g_up, g_out, g_qkv, small, result, grad_tokens):
    units, r_qkv, three = g_qkv.shape
    local, width, ff = three // 3, g_down.shape[2], g_up.shape[2]
    shape = jax.ShapeDtypeStruct
    hbm = pl.BlockSpec(memory_space=pl.ANY)
    v = pl.BlockSpec(memory_space=pltpu.VMEM)
    wide = [(ff, width), (width, ff), (local, width), (3, width, local)]
    low = [g.shape for g in (g_down, g_up, g_out, g_qkv)]
    acts = [result.shape, grad_tokens.shape]
    return pl.pallas_call(
        lambda *refs: finish(refs),
        out_shape=(*(shape(x, WIDE) for x in wide), shape((width,), WIDE), shape((width,), WIDE),
                   shape((ff,), WIDE), shape((width,), WIDE), shape((width,), WIDE),
                   *(shape(x, LOW) for x in acts)),
        in_specs=[hbm, hbm, hbm, hbm, v, hbm, hbm],
        out_specs=(hbm, hbm, hbm, hbm, v, v, v, v, v, hbm, hbm),
        scratch_shapes=[*(pltpu.VMEM(x, LOW) for x in low), *(pltpu.VMEM(x, WIDE) for x in wide),
                        *(pltpu.VMEM(x, LOW) for x in acts), pltpu.SemaphoreType.DMA((18,)),
                        pltpu.SemaphoreType.DMA((18,))],
        compiler_params=pltpu.CompilerParams(vmem_limit_bytes=VMEM_BYTES),
        name="widen",
    )(g_down, g_up, g_out, g_qkv, small, result, grad_tokens)


def body(n, tokens, w_qkv, w_out, gain_one, attention_norm_bias, w_up, b_up, w_down, gain_two, shift_two,
         block_perm, mask_index, mask_count, cotangent):
    result, grad_tokens, g_down, g_up, g_out, g_qkv, small = build(
        n, tokens, w_qkv.transpose(1, 0, 2), w_out, gain_one, attention_norm_bias, w_up, b_up, w_down, gain_two,
        shift_two, block_perm.T, mask_index, mask_count.reshape(1, 1), cotangent[0])
    (g_down, g_up, g_out, g_qkv, g_gain_one, g_shift_one, g_bias, g_gain_two, g_shift_two, result,
     grad_tokens) = widen(g_down, g_up, g_out, g_qkv, small, result, grad_tokens)
    return (result, grad_tokens, g_qkv.transpose(1, 0, 2), g_out, g_gain_one, g_shift_one, g_up, g_bias, g_down,
            g_gain_two, g_shift_two)


def solution(mesh):
    return jax.shard_map(
        functools.partial(body, mesh.shape["batch"]),
        mesh=mesh,
        in_specs=(P("batch", "head"), P(None, None, "head"), P(), P(), P(), P(None, "head"), P("head"),
                  P("head", None), P(), P(), P("head", None), P("batch", None), P("batch"),
                  P("batch", None, None)),
        out_specs=(P("batch", "head"), P("batch", "head"), P(None, None, "head"), P("head", None), P(), P(),
                   P(None, "head"), P("head"), P("head", None), P(), P()),
        check_vma=False,
    )
```

```python
import functools

import jax
import jax.numpy as jnp
from jax import lax
from jax.experimental import pallas as pl
from jax.experimental.pallas import tpu as pltpu
from jax.sharding import PartitionSpec as P

HEAD_DIM = 64
norm_eps = 1e-06
root_half = 0.7071067811865476
inv_root_two_pi = 0.3989422804014327
log2_e = 1.4426950408889634
LOW = jnp.bfloat16
WIDE = jnp.float32
LANES = 128
MESH = pl.DeviceIdType.MESH
VMEM_BYTES = 67043328
CUTS = (2, 4)
CHUNKS = {"D": 2, "U": 2, "O": 1, "Q": 2}
ORDERS = {"D": [[0, 1, 2, 3], [0, 1, 2, 3]], "U": [[0, 2, 1, 3], [0, 1, 2, 3]],
          "O": [[0, 1, 2, 3]], "Q": [[0, 1, 2, 3], [0, 2, 1, 3]]}
PLAN = (
    ("D0", 0), ("D1", 0), ("U0", 0), ("attend",), ("U1", 0), ("layer", 0), ("layer", 1), ("D0", 1), ("U0", 1),
    ("norm",), ("mb", 0), ("D1", 1), ("mb", 1), ("D0", 2), ("small", 0), ("mb", 2), ("out",), ("U1", 1),
    ("D1", 2), ("qkv", 0), ("O0", 0), ("small", 1), ("qkv", 1), ("U0", 2), ("D0", 3), ("Q0", 0), ("U1", 2),
    ("far", 0), ("Q1", 0), ("D1", 3), ("small", 2), ("far", 1), ("O0", 1), ("far", 2), ("far", 3), ("layer", 2),
    ("U0", 3), ("Q0", 1), ("Q1", 1), ("D0", 4), ("small", 3), ("layer", 3), ("O0", 2), ("U1", 3), ("Q0", 2),
    ("Q1", 2), ("near", 0), ("near", 1), ("D1", 4), ("near", 2), ("D0", 5), ("near", 3), ("grad", 0),
    ("grad", 1), ("grad", 2), ("U0", 4), ("stat", 0), ("stat", 1), ("O0", 3), ("grad", 3), ("gout",), ("D1", 5),
    ("U1", 4), ("stat", 2), ("D0", 6), ("Q0", 3), ("D0", 7), ("Q1", 3), ("U1", 5), ("U0", 5), ("stat", 3),
    ("O0", 4), ("stats",), ("Q0", 4), ("result",), ("Q1", 4), ("D1", 6), ("U0", 6), ("D1", 7), ("O0", 5),
    ("U0", 7), ("Q0", 5), ("U1", 6), ("Q1", 5), ("U1", 7), ("O0", 6), ("O0", 7), ("Q1", 6), ("Q0", 6),
    ("Q1", 7), ("Q0", 7),
)


def dot(a, b):
    return lax.dot_general(a, b, (((1,), (0,)), ((), ())), preferred_element_type=WIDE)


def dot_nt(a, b):
    return lax.dot_general(a, b, (((1,), (1,)), ((), ())), preferred_element_type=WIDE)


def dot_tn(a, b):
    return lax.dot_general(a, b, (((0,), (0,)), ((), ())), preferred_element_type=WIDE)


def normalize(values):
    centered = values - jnp.mean(values, axis=-1, keepdims=True)
    inverse = lax.rsqrt(jnp.mean(centered * centered, axis=-1, keepdims=True) + norm_eps)
    return centered * inverse, inverse


def norm_backward(upstream, normal, inverse, gain_vec):
    scaled = upstream * gain_vec
    return inverse * (
        scaled
        - jnp.mean(scaled, axis=-1, keepdims=True)
        - normal * jnp.mean(scaled * normal, axis=-1, keepdims=True)
    )


def col_sum(x):
    return jnp.sum(x, axis=0, keepdims=True)


def cat(parts):
    return jnp.concatenate(parts, axis=1)


class Ring:
    def __init__(self, order, extra, first, out, recv, send, keep, xsend, xrecv, sems, peer, bit_of):
        self.order, self.extra = order, extra
        self.first, self.out = first, out
        self.recv, self.send, self.keep = recv, send, keep
        self.xsend, self.xrecv = xsend, xrecv
        self.ssem, self.rsem, self.lsem = sems
        self.peer = peer
        self.mine = [bit_of(b) for b in order]
        units = first.shape[0]
        self.sizes = [units >> (k + 1) for k in range(len(order))]
        self.base = []
        base = 0
        for k in range(len(order)):
            base = base + self.mine[k] * self.sizes[k]
            self.base.append(base)

    def _copy(self, src, dst, slot, bit):
        return pltpu.make_async_remote_copy(
            src_ref=src, dst_ref=dst, send_sem=self.ssem.at[slot], recv_sem=self.rsem.at[slot],
            device_id=self.peer(bit), device_id_type=MESH)

    def _rs(self, k):
        size = self.sizes[k]
        if k == 0:
            src = self.first.at[pl.ds((1 - self.mine[0]) * size, size)]
        else:
            src = self.send[k - 1]
        return self._copy(src, self.recv[k], k, self.order[k])

    def _x(self, j):
        return self._copy(self.xsend, self.xrecv.at[pl.ds(j, 1)], len(self.order) + j, self.extra[j])

    def _ag(self, k):
        slot = len(self.order) + len(self.extra) + k
        part = self.first.at[pl.ds(self.base[k], self.sizes[k])]
        return self._copy(part, part, slot, self.order[k])

    def _write(self):
        return pltpu.make_async_copy(self.first, self.out, self.lsem)

    def start(self):
        self._rs(0).start()

    def _value(self, k, u):
        got = self.recv[k][u].astype(WIDE)
        if k == 0:
            return self.first[self.mine[0] * self.sizes[0] + u].astype(WIDE) + got
        return self.keep[k - 1][u] + got

    def reduce(self, k):
        self._rs(k).wait_recv()
        if k == 0:
            self._rs(0).wait_send()
        if k + 1 < len(self.order):
            half = self.sizes[k + 1]
            mine = self.mine[k + 1]

            def out_part(j, c):
                self.send[k][j] = self._value(k, (1 - mine) * half + j).astype(LOW)
                return c

            lax.fori_loop(0, half, out_part, 0)
            self._rs(k + 1).start()

            def own_part(j, c):
                self.keep[k][j] = self._value(k, mine * half + j)
                return c

            lax.fori_loop(0, half, own_part, 0)
        else:
            total = self._value(k, 0)
            for j in range(len(self.extra)):
                self.xsend[0] = total.astype(LOW)
                self._x(j).start()
                self._x(j).wait()
                total = self.xsend[0].astype(WIDE) + self.xrecv[j].astype(WIDE)
            self.first[self.base[k]] = total.astype(LOW)
            self._ag(k).start()

    def gather(self, k):
        self._ag(k + 1).wait_recv()
        if k >= 0:
            self._ag(k).start()
        else:
            self._write().start()

    def advance(self, stage):
        depth = len(self.order)
        if stage < depth:
            self.reduce(stage)
        else:
            self.gather(2 * depth - 2 - stage)

    def finish(self):
        for k in range(len(self.order)):
            if k > 0:
                self._rs(k).wait_send()
            self._ag(k).wait_send()
        self._write().wait()


def kernel(n, refs):
    (tokens, wqkv_hbm, wout_hbm, wup_hbm, wdown_hbm, *vectors,
     perm, count, index, cot,
     result, grad_tokens, o_down, o_up, o_out, o_qkv, small_out,
     wqkv, wout, wup, wdown, wsem, vecs,
     tok, qkv, sel_t, sel, blk, tokc, qc, probs, ctxc, normal_one, inverse_one, normed_one, low_one, slope,
     hidden, part, part_got, gb, gtwo, gin, back, back_got, gattn, gctx, dqc, dall, far, far_got, near,
     ctx, pre_two, down_far, down_got, stats, stats_got,
     f_down, f_up, f_out, f_qkv, small, small_got, small_sum,
     xs_send, xs_recv, lsem, rings) = refs
    rows, own = tokens.shape
    width = wout.shape[0]
    local = wqkv.shape[1] // 3
    pairs = local // LANES
    slots = index.shape[1]
    ff = wup.shape[1]
    block_len = rows // 2
    tile = 256
    tiles = rows // tile
    scale = HEAD_DIM ** (-0.5)
    b = lax.axis_index("batch")
    h = lax.axis_index("head")
    other = 1 - h
    bits = [1 << k for k in range(n.bit_length() - 1)]

    def bit_of(bit):
        return lax.rem(lax.div(b, bit), 2)

    def peer(bit):
        return (b + bit - 2 * bit * bit_of(bit), h)

    x_peer = (b, other)

    def x_copy(src, dst, slot):
        return pltpu.make_async_remote_copy(
            src_ref=src, dst_ref=dst, send_sem=xs_send.at[slot], recv_sem=xs_recv.at[slot],
            device_id=x_peer, device_id_type=MESH)

    loads = [pltpu.make_async_copy(s, d, wsem.at[i]) for i, (s, d) in enumerate(
        [(wqkv_hbm.at[j], wqkv.at[:, pl.ds(j * local, local)]) for j in range(3)]
        + [(wout_hbm, wout), (wup_hbm, wup), (wdown_hbm, wdown)])]
    for cp in loads:
        cp.start()
    barrier = pltpu.get_barrier_semaphore()
    pl.semaphore_signal(barrier, inc=1, device_id=x_peer, device_id_type=MESH)
    for bit in bits:
        pl.semaphore_signal(barrier, inc=1, device_id=peer(bit), device_id_type=MESH)
    pl.semaphore_wait(barrier, 1 + len(bits))

    own_cols = pl.ds(pl.multiple_of(h * own, LANES), own)
    far_cols = pl.ds(pl.multiple_of(other * own, LANES), own)

    def row_tile(r):
        return pl.ds(pl.multiple_of(r * tile, tile), tile)

    def tok_copy(r):
        return x_copy(tokens.at[row_tile(r)], tok.at[row_tile(r), own_cols], r)

    for r in range(tiles):
        tok_copy(r).start()
    own_tok = pltpu.make_async_copy(tokens, tok.at[:, own_cols], lsem.at[0])
    own_tok.start()

    for i, vector in enumerate(vectors):
        vecs[i:i + 1, :vector.shape[0]] = vector[...].reshape(1, -1)
    gain_one, shift_one, gain_two, shift_two = (vecs.at[i:i + 1, :width] for i in range(4))
    b_up = vecs.at[4:5, :]

    lane_slot = lax.broadcasted_iota(jnp.int32, (1, slots), 1)
    idx = jnp.where(lane_slot < count[...], index[...], -1)
    picked = jnp.where(lax.broadcasted_iota(jnp.int32, (rows, slots), 0) == idx, 1.0, 0.0)
    sel_t[...] = picked.astype(LOW)
    picked = jnp.transpose(picked)
    sel[...] = picked.astype(LOW)
    blk[...] = jnp.broadcast_to(jnp.sum(picked[:, block_len:], axis=1, keepdims=True), blk.shape)
    own_tok.wait()
    for cp in loads[:3]:
        cp.wait()

    def qkv_tile(r, c):
        tok_copy(r).wait_recv()
        out = dot(tok[row_tile(r), :], wqkv[...]).astype(LOW)
        for j in range(3 * pairs):
            qkv[j, row_tile(r), :] = out[:, j * LANES:(j + 1) * LANES]
        return c

    lax.fori_loop(0, tiles, qkv_tile, 0)

    low_lane = lax.broadcasted_iota(jnp.int32, (1, LANES), 1) < HEAD_DIM
    def keep_head(x, e):
        return jnp.where(low_lane, x, 0.0).astype(LOW) if e == 0 else jnp.where(low_lane, 0.0, x).astype(LOW)

    order = perm[...].astype(WIDE)
    head_lane = lax.broadcasted_iota(jnp.int32, order.shape, 1)

    def blocks_of(head):
        return jnp.sum(jnp.where(head_lane == head, order, 0.0), axis=1, keepdims=True)

    def second(head):
        pair = blocks_of(head)
        return (pair[:1] + blk[:, :1] * (pair[1:] - pair[:1])) > 0.5

    def masked_attention(p, c):
        q2 = dot(sel[...], qkv[p]).astype(LOW)
        qc[p] = q2
        halves = []
        for e in range(2):
            head = 2 * p + e
            late = second(head)
            qm = keep_head(q2.astype(WIDE), e)
            s = jnp.where(late, dot_nt(qm, qkv[pairs + p, block_len:, :]),
                          dot_nt(qm, qkv[pairs + p, :block_len, :])) * (scale * log2_e)
            ex = jnp.exp2(s - jnp.max(s, axis=-1, keepdims=True))
            pr = ex * (1.0 / jnp.sum(ex, axis=-1, keepdims=True))
            probs[head] = pr
            pr = pr.astype(LOW)
            halves.append(jnp.where(late, dot(pr, qkv[2 * pairs + p, block_len:, :]),
                                    dot(pr, qkv[2 * pairs + p, :block_len, :])))
        ctxc[h * pairs + p] = jnp.where(low_lane, halves[0], halves[1]).astype(LOW)
        ctxc_copy(p).start()
        return c

    def ctxc_copy(p):
        mine_c = ctxc.at[pl.ds(h * pairs + p, 1)]
        return x_copy(mine_c, mine_c, tiles + p)

    lax.fori_loop(0, pairs, masked_attention, 0)

    def attend(i, c):
        p = lax.rem(i, pairs)
        q_block = lax.div(i, pairs)
        q_rows = pl.ds(pl.multiple_of(q_block * block_len, block_len), block_len)
        q2 = qkv[p, q_rows, :].astype(WIDE)
        even, odd = blocks_of(2 * p), blocks_of(2 * p + 1)
        late = jnp.where(low_lane, jnp.where(q_block == 0, even[:1], even[1:]),
                         jnp.where(q_block == 0, odd[:1], odd[1:])) > 0.5

        def chosen(j):
            return jnp.where(late, qkv[j, block_len:, :].astype(WIDE), qkv[j, :block_len, :].astype(WIDE)).astype(LOW)

        k2, v2 = chosen(pairs + p), chosen(2 * pairs + p)
        halves = []
        for e in range(2):
            s = dot_nt(keep_head(q2, e), k2) * (scale * log2_e)
            ex = jnp.exp2(s - jnp.max(s, axis=-1, keepdims=True))
            inv = 1.0 / jnp.sum(ex, axis=-1, keepdims=True)
            halves.append(dot(ex.astype(LOW), v2) * inv)
        ctx[h * pairs + p, q_rows, :] = jnp.where(low_lane, halves[0], halves[1]).astype(LOW)
        ctx_copy(i).start()
        return c

    x_base = tiles + pairs

    def ctx_copy(i):
        q_rows = pl.ds(pl.multiple_of(lax.div(i, pairs) * block_len, block_len), block_len)
        part_ref = ctx.at[pl.ds(h * pairs + lax.rem(i, pairs), 1), q_rows]
        return x_copy(part_ref, part_ref, x_base + i)

    tokc[...] = dot(sel[...], tok[...]).astype(LOW)
    attend_units = 2 * pairs
    x_base2 = x_base + attend_units
    lax.fori_loop(0, CUTS[0], attend, 0)

    for p in range(pairs):
        ctxc_copy(p).wait_recv()
    for cp in loads[3:]:
        cp.wait()
    pre = tokc[...].astype(WIDE) + dot(cat([ctxc[j] for j in range(2 * pairs)]), wout[...])
    nrm_c, inv_c = normalize(pre)
    normal_one[...] = nrm_c
    inverse_one[...] = jnp.broadcast_to(inv_c, inverse_one.shape)
    nrm_c = nrm_c * gain_one[...] + shift_one[...]
    normed_one[...] = nrm_c
    low_one[...] = nrm_c.astype(LOW)
    ff_tile = 384

    def up_tile(i, c):
        cols = pl.ds(pl.multiple_of(i * ff_tile, ff_tile), ff_tile)
        u = dot(low_one[...], wup[:, cols]) + vecs[4:5, cols]
        cdf = 0.5 * (1.0 + lax.erf(u * root_half))
        hidden[:, cols] = (u * cdf).astype(LOW)
        slope[:, cols] = cdf + u * inv_root_two_pi * jnp.exp(-0.5 * u * u)
        return c

    lax.fori_loop(0, ff // ff_tile, up_tile, 0)
    part[...] = dot(hidden[...], wdown[...]).astype(LOW)
    part_copy = x_copy(part, part_got, x_base2)
    part_copy.start()
    lax.fori_loop(CUTS[0], CUTS[1], attend, 0)
    part_copy.wait_recv()

    normal_two, inv_two = normalize(normed_one[...] + (part[...].astype(WIDE) + part_got[...].astype(WIDE)))
    alive = lax.broadcasted_iota(jnp.int32, (slots, 1), 0) < count[...]
    up = jnp.where(alive, cot[...].astype(WIDE), 0.0)
    g2 = norm_backward(up, normal_two, inv_two, gain_two[...])
    gtwo[...] = g2
    gb[...] = g2.astype(LOW)
    small[2:3, :] = cat([col_sum(up * normal_two), col_sum(up)])

    def put(first, unit, value):
        r = first.shape[1]
        for j in range(value.shape[0] // r):
            first[unit + j] = value[j * r:(j + 1) * r, :]

    ring = {name: Ring(peer=peer, bit_of=bit_of, **r) for name, r in rings.items()}

    def down_tile(i, c):
        cols = pl.ds(pl.multiple_of(i * ff_tile, ff_tile), ff_tile)
        put(f_down, i * (ff_tile * f_down.shape[0] // ff), dot_tn(hidden[:, cols], gb[...]).astype(LOW))
        return c

    def up_grad_tile(i, c):
        cols = pl.ds(pl.multiple_of(i * ff_tile, ff_tile), ff_tile)
        put(f_up, i * (ff_tile * f_up.shape[0] // width), dot_tn(low_one[:, cols], gin[...]).astype(LOW))
        return c

    def in_tile(i, c):
        cols = pl.ds(pl.multiple_of(i * ff_tile, ff_tile), ff_tile)
        g = (dot_nt(gb[...], wdown[cols, :]) * slope[:, cols]).astype(LOW)
        gin[:, cols] = g
        small[0:1, cols] = col_sum(g.astype(WIDE))
        return c

    back_copy = x_copy(back, back_got, x_base2 + 1)
    for k in range(2):
        lax.fori_loop(k * ff // (2 * ff_tile), (k + 1) * ff // (2 * ff_tile), down_tile, 0)
        ring["D%d" % k].start()
    lax.fori_loop(0, ff // ff_tile, in_tile, 0)
    back[...] = dot_nt(gin[...], wup[...]).astype(LOW)
    back_copy.start()
    for k in range(2):
        lax.fori_loop(k * width // (2 * ff_tile), (k + 1) * width // (2 * ff_tile), up_grad_tile, 0)
        ring["U%d" % k].start()

    def attend_more():
        lax.fori_loop(CUTS[1], attend_units, attend, 0)

    own_rows = pl.ds(pl.multiple_of(h * local, LANES), local)

    def first_norm():
        back_copy.wait_recv()
        gn = gtwo[...] + (back[...].astype(WIDE) + back_got[...].astype(WIDE))
        small[1:2, :] = cat([col_sum(gn * normal_one[...]), col_sum(gn)])
        g1 = norm_backward(gn, normal_one[...], inverse_one[:, :1], gain_one[...])
        gtwo[...] = g1
        gattn[...] = g1.astype(LOW)
        gc = dot_nt(gattn[...], wout[own_rows, :]).astype(LOW)
        for p in range(pairs):
            gctx[p] = gc[:, p * LANES:(p + 1) * LANES]
        small[3:8, :] = jnp.zeros((5, small.shape[1]), WIDE)
        small_copy(0).start()

    def masked_backward(p, c):
        q2 = qc[p].astype(WIDE)
        g2 = gctx[p].astype(WIDE)
        k2 = cat([qkv[pairs + p, :block_len, :], qkv[pairs + p, block_len:, :]])
        dk = jnp.zeros((block_len, 2 * LANES), WIDE)
        dv = jnp.zeros((block_len, 2 * LANES), WIDE)
        dq = []
        for e in range(2):
            head = 2 * p + e
            late = second(head)
            gm = keep_head(g2, e)
            dp = jnp.where(late, dot_nt(gm, qkv[2 * pairs + p, block_len:, :]),
                           dot_nt(gm, qkv[2 * pairs + p, :block_len, :]))
            pr = probs[head]
            t = dp * pr
            ds = (t - pr * jnp.sum(t, axis=-1, keepdims=True)).astype(LOW)
            qm = keep_head(q2, e).astype(WIDE)
            gm = gm.astype(WIDE)
            dk = dk + dot_tn(ds, cat([jnp.where(late, 0.0, qm), jnp.where(late, qm, 0.0)]).astype(LOW))
            dv = dv + dot_tn(pr.astype(LOW),
                             cat([jnp.where(late, 0.0, gm), jnp.where(late, gm, 0.0)]).astype(LOW))
            both = dot(ds, k2)
            dq.append(jnp.where(late, both[:, LANES:], both[:, :LANES]))
        d = (jnp.where(low_lane, dq[0], dq[1]) * scale).astype(LOW)
        dqc[p] = d
        dall[p] = dot(sel_t[...], d).astype(LOW)
        dk = (dk * scale).astype(LOW)
        dv = dv.astype(LOW)
        dall[pairs + p, :block_len, :] = dk[:, :LANES]
        dall[pairs + p, block_len:, :] = dk[:, LANES:]
        dall[2 * pairs + p, :block_len, :] = dv[:, :LANES]
        dall[2 * pairs + p, block_len:, :] = dv[:, LANES:]
        return c

    def small_copy(k):
        return pltpu.make_async_remote_copy(
            src_ref=small.at[pl.ds(8 * k, 8)], dst_ref=small_got.at[pl.ds(8 * k, 8)],
            send_sem=xs_send.at[x_slots + k], recv_sem=xs_recv.at[x_slots + k],
            device_id=peer(bits[k]), device_id_type=MESH)

    small_write = pltpu.make_async_copy(small_sum, small_out, lsem.at[3])

    def small_step(k):
        small_copy(k).wait_recv()
        total = small[8 * k:8 * k + 8, :] + small_got[8 * k:8 * k + 8, :]
        if k + 1 < len(bits):
            small[8 * k + 8:8 * k + 16, :] = total
            small_copy(k + 1).start()
        else:
            small_sum[...] = total
            small_write.start()

    def out_grad():
        put(f_out, 0, dot_tn(cat([ctxc[h * pairs + p] for p in range(pairs)]), gattn[...]).astype(LOW))
        ring["O0"].start()

    def qkv_grad_tile(i, c):
        cols = pl.ds(pl.multiple_of(i * ff_tile, ff_tile), ff_tile)
        gq = dot_tn(tokc[:, cols], cat([dqc[p] for p in range(pairs)]))
        gkv = dot_tn(tok[:, cols], cat([dall[pairs + j] for j in range(2 * pairs)]))
        put(f_qkv, i * (ff_tile * f_qkv.shape[0] // width), cat([gq, gkv]).astype(LOW))
        return c

    def qkv_grad(k):
        lax.fori_loop(k * width // (2 * ff_tile), (k + 1) * width // (2 * ff_tile), qkv_grad_tile, 0)
        ring["Q%d" % k].start()

    def far_copy(r):
        return x_copy(far.at[row_tile(r)], far_got.at[row_tile(r)], x_base2 + 2 + r)

    def far_tile(r):
        d = cat([dall[j, row_tile(r), :] for j in range(3 * pairs)])
        far[row_tile(r), :] = dot_nt(d, wqkv[far_cols, :]).astype(LOW)
        far_copy(r).start()

    def near_tile(r):
        mine = gtwo[:, own_cols]
        high = mine.astype(LOW)
        rest = (mine - high.astype(WIDE)).astype(LOW)
        d = cat([dall[j, row_tile(r), :] for j in range(3 * pairs)])
        spread = dot(sel_t[row_tile(r), :], cat([high, rest]))
        near[row_tile(r), :] = dot_nt(d, wqkv[own_cols, :]) + (spread[:, :own] + spread[:, own:])

    def grad_tile(r):
        far_copy(r).wait_recv()
        far_copy(r).wait_send()
        far[row_tile(r), :] = (near[row_tile(r), :] + far_got[row_tile(r), :].astype(WIDE)).astype(LOW)

    grad_out = pltpu.make_async_copy(far, grad_tokens, lsem.at[1])

    def down_copy(r):
        return x_copy(down_far.at[row_tile(r)], down_got.at[row_tile(r)], x_base2 + 2 + tiles + r)

    def layer_tile(r):
        if r * tile % block_len == 0:
            block = r * tile // block_len
            for i in range(block * pairs, (block + 1) * pairs):
                ctx_copy(i).wait_recv()
        rs = row_tile(r)
        pre_r = tok[rs, :].astype(WIDE) + dot(cat([ctx[j, rs, :] for j in range(2 * pairs)]), wout[...])
        normed = normalize(pre_r)[0] * gain_one[...] + shift_one[...]
        normed_one[...] = normed
        u = dot(normed.astype(LOW), wup[...]) + b_up[...]
        hid = (u * (0.5 * (1.0 + lax.erf(u * root_half)))).astype(LOW)
        down_far[rs, :] = dot(hid, wdown[:, far_cols]).astype(LOW)
        down_copy(r).start()
        pre_two[rs, :] = normed_one[:, own_cols] + dot(hid, wdown[:, own_cols])

    first_lane = lax.broadcasted_iota(jnp.int32, (1, LANES), 1) < 1
    stats_copy = x_copy(stats, stats_got, x_base2 + 2 + 2 * tiles)

    def stat_tile(r):
        rs = row_tile(r)
        down_copy(r).wait_recv()
        x = pre_two[rs, :] + down_got[rs, :].astype(WIDE)
        pre_two[rs, :] = x
        mean = jnp.mean(x, axis=-1, keepdims=True)
        dev = x - mean
        var = jnp.mean(dev * dev, axis=-1, keepdims=True)
        both = jnp.where(first_lane, mean, var)
        stats[r] = jnp.transpose(both)[:8, :]

    def result_tile(r, c):
        rs = row_tile(r)
        x = pre_two[rs, :]
        fill = jnp.zeros((LANES - 8, tile), WIDE)
        one = jnp.transpose(jnp.concatenate([stats[r], fill], axis=0))
        two = jnp.transpose(jnp.concatenate([stats_got[r], fill], axis=0))
        mean = 0.5 * (one[:, :1] + two[:, :1])
        gap = 0.5 * (one[:, :1] - two[:, :1])
        var = 0.5 * (one[:, 1:2] + two[:, 1:2]) + gap * gap
        down_copy(r).wait_send()
        down_far[rs, :] = ((x - mean) * lax.rsqrt(var + norm_eps) * vecs[2:3, own_cols]
                         + vecs[3:4, own_cols]).astype(LOW)
        return c

    result_out = pltpu.make_async_copy(down_far, result, lsem.at[2])

    def write_result():
        stats_copy.wait_recv()
        lax.fori_loop(0, tiles, result_tile, 0)
        result_out.start()

    x_slots = x_base2 + 3 + 2 * tiles
    steps = {"norm": first_norm, "attend": attend_more, "mb": lambda p: masked_backward(p, 0), "out": out_grad,
             "qkv": qkv_grad, "far": far_tile, "near": near_tile, "grad": grad_tile, "layer": layer_tile,
             "stat": stat_tile, "stats": stats_copy.start, "gout": grad_out.start, "result": write_result,
             "small": small_step}
    for name, *at in PLAN:
        if name in ring:
            ring[name].advance(at[0])
        else:
            steps[name](*at)
    for k in range(min(len(bits), 4), len(bits)):
        small_step(k)

    for r in range(tiles):
        tok_copy(r).wait_send()
    grad_out.wait()
    result_out.wait()
    small_write.wait()
    for i in range(attend_units):
        ctx_copy(i).wait_send()
    for p in range(pairs):
        ctxc_copy(p).wait_send()
    for cp in (part_copy, back_copy, stats_copy):
        cp.wait_send()
    for k in range(len(bits)):
        small_copy(k).wait_send()
    for one in ring.values():
        one.finish()


def build(n, tokens, wqkv, wout, gain_one, shift_one, wup, b_up, wdown, gain_two, shift_two, perm, index,
          count, cot):
    rows, own = tokens.shape
    width = wout.shape[0]
    local = wqkv.shape[2]
    pairs = local // LANES
    heads = local // HEAD_DIM
    slots = index.shape[1]
    ff = wup.shape[1]
    block_len = rows // 2
    tile = 256
    steps = n.bit_length() - 1
    bits = [1 << k for k in range(steps)]
    depth = min(4, steps)
    units = 1 << depth
    halving, extra = bits[:depth], bits[depth:]

    vm = pltpu.VMEM
    groups = {"D": (ff, width), "U": (width, ff), "O": (local, width), "Q": (width, 3 * local)}
    shapes = {g: (CHUNKS[g] * units, r // (CHUNKS[g] * units), c) for g, (r, c) in groups.items()}
    names = [(g, k) for g in groups for k in range(CHUNKS[g])]
    dma = pltpu.SemaphoreType.DMA

    def ring_scratch(g):
        _, r, c = shapes[g]
        sizes = [units >> (k + 1) for k in range(depth)]
        return {
            "recv": [vm((s, r, c), LOW) for s in sizes],
            "send": [vm((s, r, c), LOW) for s in sizes[1:]],
            "keep": [vm((s, r, c), WIDE) for s in sizes[1:]],
            "xsend": vm((1, r, c) if extra else (1, 8, LANES), LOW),
            "xrecv": vm((len(extra), r, c) if extra else (1, 8, LANES), LOW),
            "sems": (dma((2 * depth + len(extra),)), dma((2 * depth + len(extra),)), dma(())),
        }

    f = [vm(shapes[g], LOW) for g in groups]
    x_slots = 3 * (rows // tile) + 3 * pairs + 3
    scratch = [
        vm((width, 3 * local), LOW), vm(wout.shape, LOW), vm(wup.shape, LOW), vm(wdown.shape, LOW), dma((6,)),
        vm((8, ff), WIDE),
        vm((rows, width), LOW), vm((3 * pairs, rows, LANES), LOW), vm((rows, slots), LOW), vm((slots, rows), LOW),
        vm((slots, LANES), WIDE), vm((slots, width), LOW), vm((pairs, slots, LANES), LOW),
        vm((heads, slots, block_len), WIDE), vm((2 * pairs, slots, LANES), LOW), vm((slots, width), WIDE),
        vm((slots, LANES), WIDE), vm((slots, width), WIDE), vm((slots, width), LOW), vm((slots, ff), WIDE),
        vm((slots, ff), LOW), vm((slots, width), LOW), vm((slots, width), LOW), vm((slots, width), LOW),
        vm((slots, width), WIDE), vm((slots, ff), LOW), vm((slots, width), LOW), vm((slots, width), LOW),
        vm((slots, width), LOW), vm((pairs, slots, LANES), LOW),
        vm((pairs, slots, LANES), LOW), vm((3 * pairs, rows, LANES), LOW), vm((rows, own), LOW),
        vm((rows, own), LOW), vm((rows, own), WIDE),
        vm((2 * pairs, rows, LANES), LOW), vm((rows, own), WIDE), vm((rows, own), LOW),
        vm((rows, own), LOW), vm((rows // tile, 8, tile), WIDE), vm((rows // tile, 8, tile), WIDE),
        *f, vm((8 * steps, ff), WIDE), vm((8 * steps, ff), WIDE), vm((8, ff), WIDE),
        dma((x_slots + steps,)), dma((x_slots + steps,)), dma((4,)),
    ]
    plain = len(scratch)
    ring_specs = [ring_scratch(g) for g, _ in names]
    flat, tree = jax.tree.flatten(ring_specs, is_leaf=lambda x: not isinstance(x, (dict, list, tuple)))
    n_in, n_out = 14, 7

    def run(*refs):
        head_refs = refs[:n_in + n_out + plain]
        rings = jax.tree.unflatten(tree, refs[n_in + n_out + plain:])
        firsts = head_refs[-(len(groups) + 6):-6]
        outs = refs[n_in + 2:n_in + 2 + len(groups)]
        full = {}
        for (g, k), ring in zip(names, rings):
            i = list(groups).index(g)
            part = pl.ds(k * units, units)
            full["%s%d" % (g, k)] = dict(order=[halving[j] for j in ORDERS[g][k] if j < depth], extra=extra,
                                         first=firsts[i].at[part], out=outs[i].at[part], **ring)
        kernel(n, (*head_refs, full))

    hbm = pl.BlockSpec(memory_space=pl.ANY)
    v = pl.BlockSpec(memory_space=pltpu.VMEM)
    shape = jax.ShapeDtypeStruct
    return pl.pallas_call(
        run,
        out_shape=(shape((rows, own), LOW), shape((rows, own), LOW),
                   *(shape(shapes[g], LOW) for g in groups), shape((8, ff), WIDE)),
        in_specs=[hbm, hbm, hbm, hbm, hbm, v, v, v, v, v, v, v, v, v],
        out_specs=(hbm,) * 7,
        scratch_shapes=scratch + flat,
        compiler_params=pltpu.CompilerParams(
            collective_id=0, has_side_effects=True, vmem_limit_bytes=VMEM_BYTES),
        name="layer",
    )(tokens, wqkv, wout, wup, wdown, gain_one, shift_one, gain_two, shift_two, b_up, perm, count, index, cot)


def finish(refs):
    (f_down, f_up, f_out, f_qkv, small, res_in, tok_in,
     down, up, out, qkv, gain_one, shift_one, bias, gain_two, shift_two, res, tok,
     b_down, b_up, b_out, b_qkv, w_down, w_up, w_out, w_qkv, b_res, b_tok, b_small, v_one, v_two, v_bias, v_three,
     v_four, isem, osem) = refs
    width = gain_one.shape[0]
    local = qkv.shape[2]
    reads, writes = [], []

    def read(src, dst):
        cp = pltpu.make_async_copy(src, dst, isem.at[len(reads)])
        cp.start()
        reads.append(cp)
        return cp

    def write(src, dst):
        cp = pltpu.make_async_copy(src, dst, osem.at[len(writes)])
        cp.start()
        writes.append(cp)

    parts = 4
    jobs = []
    for src, low, wide, dst in ((f_down, b_down, w_down, down), (f_up, b_up, w_up, up),
                                (f_out, b_out, w_out, out), (f_qkv, b_qkv, w_qkv, qkv)):
        step = src.shape[0] // parts if src.shape[0] % parts == 0 else src.shape[0]
        for u in range(0, src.shape[0], step):
            jobs.append((read(src.at[pl.ds(u, step)], low.at[pl.ds(u, step)]), u, step, low, wide, dst))
    pass_on = [(read(a, b), b, c) for a, b, c in ((res_in, b_res, res), (tok_in, b_tok, tok))]
    small_read = read(small, b_small)
    for cp, u, step, low, wide, dst in jobs:
        cp.wait()
        r = low.shape[1]

        def unit(j, c, u=u, low=low, wide=wide, r=r, dst=dst):
            v = low[u + j].astype(WIDE)
            rows = pl.ds(pl.multiple_of((u + j) * r, r), r)
            if dst is qkv:
                for k in range(3):
                    wide[k, rows, :] = v[:, k * local:(k + 1) * local]
            else:
                wide[rows, :] = v
            return c

        lax.fori_loop(0, step, unit, 0)
        rows = pl.ds(u * r, step * r)
        if dst is qkv:
            write(wide.at[:, rows, :], dst.at[:, rows, :])
        else:
            write(wide.at[rows, :], dst.at[rows, :])
    for cp, src, dst in pass_on:
        cp.wait()
        write(src, dst)
    small_read.wait()
    for row, at, vec, dst in ((1, 0, v_one, gain_one), (1, width, v_two, shift_one), (0, 0, v_bias, bias),
                              (2, 0, v_three, gain_two), (2, width, v_four, shift_two)):
        size = vec.shape[0]
        vec[...] = b_small[row:row + 1, at:at + size].reshape(size)
        write(vec, dst)
    for cp in writes:
        cp.wait()


def widen(g_down, g_up, g_out, g_qkv, small, result, grad_tokens):
    units, r_qkv, three = g_qkv.shape
    local, width, ff = three // 3, g_down.shape[2], g_up.shape[2]
    shape = jax.ShapeDtypeStruct
    hbm = pl.BlockSpec(memory_space=pl.ANY)
    wide = [(ff, width), (width, ff), (local, width), (3, width, local)]
    low = [g.shape for g in (g_down, g_up, g_out, g_qkv)]
    acts = [result.shape, grad_tokens.shape]
    return pl.pallas_call(
        lambda *refs: finish(refs),
        out_shape=(*(shape(x, WIDE) for x in wide), shape((width,), WIDE), shape((width,), WIDE),
                   shape((ff,), WIDE), shape((width,), WIDE), shape((width,), WIDE),
                   *(shape(x, LOW) for x in acts)),
        in_specs=[hbm] * 7,
        out_specs=(hbm,) * 11,
        scratch_shapes=[*(pltpu.VMEM(x, LOW) for x in low), *(pltpu.VMEM(x, WIDE) for x in wide),
                        *(pltpu.VMEM(x, LOW) for x in acts), pltpu.VMEM(small.shape, WIDE),
                        *(pltpu.VMEM(x, WIDE) for x in ((width,), (width,), (ff,), (width,), (width,))),
                        pltpu.SemaphoreType.DMA((24,)), pltpu.SemaphoreType.DMA((24,))],
        compiler_params=pltpu.CompilerParams(vmem_limit_bytes=VMEM_BYTES),
        name="widen",
    )(g_down, g_up, g_out, g_qkv, small, result, grad_tokens)


def body(n, tokens, w_qkv, w_out, gain_one, attention_norm_bias, w_up, b_up, w_down, gain_two, shift_two,
         block_perm, mask_index, mask_count, cotangent):
    result, grad_tokens, g_down, g_up, g_out, g_qkv, small = build(
        n, tokens, w_qkv.transpose(1, 0, 2), w_out, gain_one, attention_norm_bias, w_up, b_up, w_down, gain_two,
        shift_two, block_perm.T, mask_index, mask_count.reshape(1, 1), cotangent[0])
    (g_down, g_up, g_out, g_qkv, g_gain_one, g_shift_one, g_bias, g_gain_two, g_shift_two, result,
     grad_tokens) = widen(g_down, g_up, g_out, g_qkv, small, result, grad_tokens)
    return (result, grad_tokens, g_qkv.transpose(1, 0, 2), g_out, g_gain_one, g_shift_one, g_up, g_bias, g_down,
            g_gain_two, g_shift_two)


def solution(mesh):
    return jax.shard_map(
        functools.partial(body, mesh.shape["batch"]),
        mesh=mesh,
        in_specs=(P("batch", "head"), P(None, None, "head"), P(), P(), P(), P(None, "head"), P("head"),
                  P("head", None), P(), P(), P("head", None), P("batch", None), P("batch"),
                  P("batch", None, None)),
        out_specs=(P("batch", "head"), P("batch", "head"), P(None, None, "head"), P("head", None), P(), P(),
                   P(None, "head"), P("head"), P("head", None), P(), P()),
        check_vma=False,
    )
```

```python
import functools

import jax
import jax.numpy as jnp
from jax import lax
from jax.experimental import pallas as pl
from jax.experimental.pallas import tpu as pltpu
from jax.sharding import PartitionSpec as P

HEAD_DIM = 64
norm_eps = 1e-06
root_half = 0.7071067811865476
inv_root_two_pi = 0.3989422804014327
log2_e = 1.4426950408889634
LOW = jnp.bfloat16
WIDE = jnp.float32
LANES = 128
MESH = pl.DeviceIdType.MESH
VMEM_BYTES = 67043328
CUTS = (2, 4)
CHUNKS = {"D": 4, "U": 3, "O": 1, "Q": 2}
ORDERS = {"D": [[0, 1, 2, 3], [0, 1, 2, 3], [0, 1, 2, 3], [0, 1, 2, 3]],
          "U": [[0, 1, 2, 3], [0, 1, 2, 3], [0, 2, 1, 3]],
          "O": [[0, 1, 2, 3]],
          "Q": [[0, 2, 1, 3], [0, 1, 2, 3]]}
PLAN = (
    ("down", 0), ("down", 1), ("in",), ("D0", 0), ("D1", 0), ("down", 2), ("down", 3), ("up", 0), ("up", 1),
    ("D2", 0), ("up", 2), ("D3", 0), ("U0", 0), ("U1", 0), ("D0", 1), ("U2", 0), ("attend",), ("ctx", 0),
    ("layer", 0, 1), ("D1", 1), ("D0", 2), ("D2", 1), ("norm",), ("U2", 1), ("mb", 0), ("D3", 1), ("D1", 2),
    ("D0", 3), ("mb", 1), ("D2", 2), ("small", 0), ("U0", 1), ("D3", 2), ("mb", 2), ("D1", 3), ("out",),
    ("D0", 4), ("small", 1), ("qkv", 0), ("U1", 1), ("D2", 3), ("U0", 2), ("O0", 0), ("U2", 2), ("D3", 3),
    ("Q0", 0), ("small", 2), ("D1", 4), ("qkv", 1), ("D0", 5), ("far", 0, 2), ("U1", 2), ("far", 2, 3),
    ("Q1", 0), ("O0", 1), ("D2", 4), ("small", 3), ("far", 3, 4), ("U0", 3), ("layer", 1, 2), ("U2", 3),
    ("D0", 6), ("D3", 4), ("ctx", 1), ("layer", 2, 3), ("Q0", 1), ("D0", 7), ("Q1", 1), ("D1", 5),
    ("layer", 3, 4), ("U1", 3), ("O0", 2), ("D2", 5), ("Q0", 2), ("near", 0, 1), ("U0", 4), ("near", 1, 2),
    ("U2", 4), ("near", 2, 3), ("D1", 6), ("D3", 5), ("near", 3, 4), ("grad", 0, 2), ("D1", 7), ("grad", 2, 4),
    ("Q1", 2), ("gout",), ("stat", 0, 1), ("D2", 6), ("stat", 1, 2), ("U1", 4), ("O0", 3), ("D2", 7), ("U2", 5),
    ("Q0", 3), ("U0", 5), ("stat", 2, 3), ("D3", 6), ("Q1", 3), ("D3", 7), ("U1", 5), ("stat", 3, 4), ("O0", 4),
    ("stats",), ("U0", 6), ("U0", 7), ("result",), ("U2", 6), ("U1", 6), ("Q0", 4), ("U2", 7), ("Q1", 4),
    ("U1", 7), ("O0", 5), ("Q0", 5), ("Q1", 5), ("O0", 6), ("O0", 7), ("Q0", 6), ("Q1", 6), ("Q0", 7),
    ("Q1", 7),
)


def dot(a, b):
    return lax.dot_general(a, b, (((1,), (0,)), ((), ())), preferred_element_type=WIDE)


def dot_nt(a, b):
    return lax.dot_general(a, b, (((1,), (1,)), ((), ())), preferred_element_type=WIDE)


def dot_tn(a, b):
    return lax.dot_general(a, b, (((0,), (0,)), ((), ())), preferred_element_type=WIDE)


def normalize(values):
    centered = values - jnp.mean(values, axis=-1, keepdims=True)
    inverse = lax.rsqrt(jnp.mean(centered * centered, axis=-1, keepdims=True) + norm_eps)
    return centered * inverse, inverse


def norm_backward(upstream, normal, inverse, gain_vec):
    scaled = upstream * gain_vec
    return inverse * (
        scaled
        - jnp.mean(scaled, axis=-1, keepdims=True)
        - normal * jnp.mean(scaled * normal, axis=-1, keepdims=True)
    )


def col_sum(x):
    return jnp.sum(x, axis=0, keepdims=True)


def cat(parts):
    return jnp.concatenate(parts, axis=1)


class Ring:
    def __init__(self, order, extra, first, out, recv, send, keep, xsend, xrecv, sems, peer, bit_of):
        self.order, self.extra = order, extra
        self.first, self.out = first, out
        self.recv, self.send, self.keep = recv, send, keep
        self.xsend, self.xrecv = xsend, xrecv
        self.ssem, self.rsem, self.lsem = sems
        self.peer = peer
        self.mine = [bit_of(b) for b in order]
        units = first.shape[0]
        self.sizes = [units >> (k + 1) for k in range(len(order))]
        self.base = []
        base = 0
        for k in range(len(order)):
            base = base + self.mine[k] * self.sizes[k]
            self.base.append(base)

    def _copy(self, src, dst, slot, bit):
        return pltpu.make_async_remote_copy(
            src_ref=src, dst_ref=dst, send_sem=self.ssem.at[slot], recv_sem=self.rsem.at[slot],
            device_id=self.peer(bit), device_id_type=MESH)

    def _rs(self, k):
        size = self.sizes[k]
        if k == 0:
            src = self.first.at[pl.ds((1 - self.mine[0]) * size, size)]
        else:
            src = self.send[k - 1]
        return self._copy(src, self.recv[k], k, self.order[k])

    def _x(self, j):
        return self._copy(self.xsend, self.xrecv.at[pl.ds(j, 1)], len(self.order) + j, self.extra[j])

    def _ag(self, k):
        slot = len(self.order) + len(self.extra) + k
        part = self.first.at[pl.ds(self.base[k], self.sizes[k])]
        return self._copy(part, part, slot, self.order[k])

    def _write(self):
        return pltpu.make_async_copy(self.first, self.out, self.lsem)

    def start(self):
        self._rs(0).start()

    def _value(self, k, u):
        got = self.recv[k][u].astype(WIDE)
        if k == 0:
            return self.first[self.mine[0] * self.sizes[0] + u].astype(WIDE) + got
        return self.keep[k - 1][u] + got

    def reduce(self, k):
        self._rs(k).wait_recv()
        if k == 0:
            self._rs(0).wait_send()
        if k + 1 < len(self.order):
            half = self.sizes[k + 1]
            mine = self.mine[k + 1]

            def out_part(j, c):
                self.send[k][j] = self._value(k, (1 - mine) * half + j).astype(LOW)
                return c

            lax.fori_loop(0, half, out_part, 0)
            self._rs(k + 1).start()

            def own_part(j, c):
                self.keep[k][j] = self._value(k, mine * half + j)
                return c

            lax.fori_loop(0, half, own_part, 0)
        else:
            total = self._value(k, 0)
            for j in range(len(self.extra)):
                self.xsend[0] = total.astype(LOW)
                self._x(j).start()
                self._x(j).wait()
                total = self.xsend[0].astype(WIDE) + self.xrecv[j].astype(WIDE)
            self.first[self.base[k]] = total.astype(LOW)
            self._ag(k).start()

    def gather(self, k):
        self._ag(k + 1).wait_recv()
        if k >= 0:
            self._ag(k).start()
        else:
            self._write().start()

    def advance(self, stage):
        depth = len(self.order)
        if stage < depth:
            self.reduce(stage)
        else:
            self.gather(2 * depth - 2 - stage)

    def finish(self):
        for k in range(len(self.order)):
            if k > 0:
                self._rs(k).wait_send()
            self._ag(k).wait_send()
        self._write().wait()


def kernel(n, refs):
    (tokens, wqkv_hbm, wout_hbm, wup_hbm, wdown_hbm, *vectors,
     perm, count, index, cot,
     result, grad_tokens, o_down, o_up, o_out, o_qkv, small_out,
     wqkv, wout, wup, wdown, wsem, vecs,
     tok, qkv, sel_t, sel, blk, tokc, qc, probs, ctxc, normal_one, inverse_one, normed_one, low_one, slope,
     hidden, part, part_got, gb, gtwo, gin, back, back_got, gattn, gctx, dqc, dall, far, far_got, near,
     ctx, pre_two, down_far, down_got, stats, stats_got,
     f_down, f_up, f_out, f_qkv, small, small_got, small_sum,
     xs_send, xs_recv, lsem, rings) = refs
    rows, own = tokens.shape
    width = wout.shape[0]
    local = wqkv.shape[1] // 3
    pairs = local // LANES
    slots = index.shape[1]
    ff = wup.shape[1]
    block_len = rows // 2
    tile = 256
    tiles = rows // tile
    scale = HEAD_DIM ** (-0.5)
    b = lax.axis_index("batch")
    h = lax.axis_index("head")
    other = 1 - h
    bits = [1 << k for k in range(n.bit_length() - 1)]

    def bit_of(bit):
        return lax.rem(lax.div(b, bit), 2)

    def peer(bit):
        return (b + bit - 2 * bit * bit_of(bit), h)

    x_peer = (b, other)

    def x_copy(src, dst, slot):
        return pltpu.make_async_remote_copy(
            src_ref=src, dst_ref=dst, send_sem=xs_send.at[slot], recv_sem=xs_recv.at[slot],
            device_id=x_peer, device_id_type=MESH)

    loads = [pltpu.make_async_copy(s, d, wsem.at[i]) for i, (s, d) in enumerate(
        [(wqkv_hbm.at[j], wqkv.at[:, pl.ds(j * local, local)]) for j in range(3)]
        + [(wout_hbm, wout), (wup_hbm, wup), (wdown_hbm, wdown)])]
    for cp in loads:
        cp.start()
    barrier = pltpu.get_barrier_semaphore()
    pl.semaphore_signal(barrier, inc=1, device_id=x_peer, device_id_type=MESH)
    for bit in bits:
        pl.semaphore_signal(barrier, inc=1, device_id=peer(bit), device_id_type=MESH)
    pl.semaphore_wait(barrier, 1 + len(bits))

    own_cols = pl.ds(pl.multiple_of(h * own, LANES), own)
    far_cols = pl.ds(pl.multiple_of(other * own, LANES), own)

    def row_tile(r):
        return pl.ds(pl.multiple_of(r * tile, tile), tile)

    def tok_copy(r):
        return x_copy(tokens.at[row_tile(r)], tok.at[row_tile(r), own_cols], r)

    for r in range(tiles):
        tok_copy(r).start()
    own_tok = pltpu.make_async_copy(tokens, tok.at[:, own_cols], lsem.at[0])
    own_tok.start()

    for i, vector in enumerate(vectors):
        vecs[i:i + 1, :vector.shape[0]] = vector[...].reshape(1, -1)
    gain_one, shift_one, gain_two, shift_two = (vecs.at[i:i + 1, :width] for i in range(4))
    b_up = vecs.at[4:5, :]

    lane_slot = lax.broadcasted_iota(jnp.int32, (1, slots), 1)
    idx = jnp.where(lane_slot < count[...], index[...], -1)
    picked = jnp.where(lax.broadcasted_iota(jnp.int32, (rows, slots), 0) == idx, 1.0, 0.0)
    sel_t[...] = picked.astype(LOW)
    picked = jnp.transpose(picked)
    sel[...] = picked.astype(LOW)
    blk[...] = jnp.broadcast_to(jnp.sum(picked[:, block_len:], axis=1, keepdims=True), blk.shape)
    own_tok.wait()
    for cp in loads[:3]:
        cp.wait()

    def qkv_tile(r, c):
        tok_copy(r).wait_recv()
        out = dot(tok[row_tile(r), :], wqkv[...]).astype(LOW)
        for j in range(3 * pairs):
            qkv[j, row_tile(r), :] = out[:, j * LANES:(j + 1) * LANES]
        return c

    lax.fori_loop(0, tiles, qkv_tile, 0)

    low_lane = lax.broadcasted_iota(jnp.int32, (1, LANES), 1) < HEAD_DIM
    def keep_head(x, e):
        return jnp.where(low_lane, x, 0.0).astype(LOW) if e == 0 else jnp.where(low_lane, 0.0, x).astype(LOW)

    order = perm[...].astype(WIDE)
    head_lane = lax.broadcasted_iota(jnp.int32, order.shape, 1)

    def blocks_of(head):
        return jnp.sum(jnp.where(head_lane == head, order, 0.0), axis=1, keepdims=True)

    def second(head):
        pair = blocks_of(head)
        return (pair[:1] + blk[:, :1] * (pair[1:] - pair[:1])) > 0.5

    def masked_attention(p, c):
        q2 = dot(sel[...], qkv[p]).astype(LOW)
        qc[p] = q2
        halves = []
        for e in range(2):
            head = 2 * p + e
            late = second(head)
            qm = keep_head(q2.astype(WIDE), e)
            s = jnp.where(late, dot_nt(qm, qkv[pairs + p, block_len:, :]),
                          dot_nt(qm, qkv[pairs + p, :block_len, :])) * (scale * log2_e)
            ex = jnp.exp2(s - jnp.max(s, axis=-1, keepdims=True))
            pr = ex * (1.0 / jnp.sum(ex, axis=-1, keepdims=True))
            probs[head] = pr
            pr = pr.astype(LOW)
            halves.append(jnp.where(late, dot(pr, qkv[2 * pairs + p, block_len:, :]),
                                    dot(pr, qkv[2 * pairs + p, :block_len, :])))
        ctxc[h * pairs + p] = jnp.where(low_lane, halves[0], halves[1]).astype(LOW)
        ctxc_copy(p).start()
        return c

    def ctxc_copy(p):
        mine_c = ctxc.at[pl.ds(h * pairs + p, 1)]
        return x_copy(mine_c, mine_c, tiles + p)

    lax.fori_loop(0, pairs, masked_attention, 0)

    def attend(i, c):
        p = lax.rem(i, pairs)
        q_block = lax.div(i, pairs)
        q_rows = pl.ds(pl.multiple_of(q_block * block_len, block_len), block_len)
        q2 = qkv[p, q_rows, :].astype(WIDE)
        even, odd = blocks_of(2 * p), blocks_of(2 * p + 1)
        late = jnp.where(low_lane, jnp.where(q_block == 0, even[:1], even[1:]),
                         jnp.where(q_block == 0, odd[:1], odd[1:])) > 0.5

        def chosen(j):
            return jnp.where(late, qkv[j, block_len:, :].astype(WIDE), qkv[j, :block_len, :].astype(WIDE)).astype(LOW)

        k2, v2 = chosen(pairs + p), chosen(2 * pairs + p)
        halves = []
        for e in range(2):
            s = dot_nt(keep_head(q2, e), k2) * (scale * log2_e)
            ex = jnp.exp2(s - jnp.max(s, axis=-1, keepdims=True))
            inv = 1.0 / jnp.sum(ex, axis=-1, keepdims=True)
            halves.append(dot(ex.astype(LOW), v2) * inv)
        ctx[h * pairs + p, q_rows, :] = jnp.where(low_lane, halves[0], halves[1]).astype(LOW)
        ctx_copy(i).start()
        return c

    x_base = tiles + pairs

    def ctx_copy(i):
        q_rows = pl.ds(pl.multiple_of(lax.div(i, pairs) * block_len, block_len), block_len)
        part_ref = ctx.at[pl.ds(h * pairs + lax.rem(i, pairs), 1), q_rows]
        return x_copy(part_ref, part_ref, x_base + i)

    tokc[...] = dot(sel[...], tok[...]).astype(LOW)
    attend_units = 2 * pairs
    x_base2 = x_base + attend_units
    lax.fori_loop(0, CUTS[0], attend, 0)

    for p in range(pairs):
        ctxc_copy(p).wait_recv()
    for cp in loads[3:]:
        cp.wait()
    pre = tokc[...].astype(WIDE) + dot(cat([ctxc[j] for j in range(2 * pairs)]), wout[...])
    nrm_c, inv_c = normalize(pre)
    normal_one[...] = nrm_c
    inverse_one[...] = jnp.broadcast_to(inv_c, inverse_one.shape)
    nrm_c = nrm_c * gain_one[...] + shift_one[...]
    normed_one[...] = nrm_c
    low_one[...] = nrm_c.astype(LOW)
    ff_tile = 384

    def up_tile(i, c):
        cols = pl.ds(pl.multiple_of(i * ff_tile, ff_tile), ff_tile)
        u = dot(low_one[...], wup[:, cols]) + vecs[4:5, cols]
        cdf = 0.5 * (1.0 + lax.erf(u * root_half))
        hidden[:, cols] = (u * cdf).astype(LOW)
        slope[:, cols] = cdf + u * inv_root_two_pi * jnp.exp(-0.5 * u * u)
        return c

    lax.fori_loop(0, ff // ff_tile, up_tile, 0)
    part[...] = dot(hidden[...], wdown[...]).astype(LOW)
    part_copy = x_copy(part, part_got, x_base2)
    part_copy.start()
    lax.fori_loop(CUTS[0], CUTS[1], attend, 0)
    part_copy.wait_recv()

    normal_two, inv_two = normalize(normed_one[...] + (part[...].astype(WIDE) + part_got[...].astype(WIDE)))
    alive = lax.broadcasted_iota(jnp.int32, (slots, 1), 0) < count[...]
    up = jnp.where(alive, cot[...].astype(WIDE), 0.0)
    g2 = norm_backward(up, normal_two, inv_two, gain_two[...])
    gtwo[...] = g2
    gb[...] = g2.astype(LOW)
    small[2:3, :] = cat([col_sum(up * normal_two), col_sum(up)])

    def put(first, unit, value):
        r = first.shape[1]
        for j in range(value.shape[0] // r):
            first[unit + j] = value[j * r:(j + 1) * r, :]

    ring = {name: Ring(peer=peer, bit_of=bit_of, **r) for name, r in rings.items()}

    def by_tiles(group, k, first, grad):
        units = first.shape[0] // CHUNKS[group]
        size = units * first.shape[1]
        step = 256 if size % 256 == 0 else 384

        def one_tile(i, c):
            at = k * size + i * step
            put(first, k * units + i * (step * units // size), grad(pl.ds(pl.multiple_of(at, LANES), step)))
            return c

        lax.fori_loop(0, size // step, one_tile, 0)
        ring["%s%d" % (group, k)].start()

    def down_grad(k):
        by_tiles("D", k, f_down, lambda cols: dot_tn(hidden[:, cols], gb[...]).astype(LOW))

    def up_grad(k):
        by_tiles("U", k, f_up, lambda cols: dot_tn(low_one[:, cols], gin[...]).astype(LOW))

    def in_tile(i, c):
        cols = pl.ds(pl.multiple_of(i * ff_tile, ff_tile), ff_tile)
        g = (dot_nt(gb[...], wdown[cols, :]) * slope[:, cols]).astype(LOW)
        gin[:, cols] = g
        small[0:1, cols] = col_sum(g.astype(WIDE))
        return c

    back_copy = x_copy(back, back_got, x_base2 + 1)

    def input_grad():
        lax.fori_loop(0, ff // ff_tile, in_tile, 0)
        back[...] = dot_nt(gin[...], wup[...]).astype(LOW)
        back_copy.start()

    def attend_more():
        lax.fori_loop(CUTS[1], attend_units, attend, 0)

    own_rows = pl.ds(pl.multiple_of(h * local, LANES), local)

    def first_norm():
        back_copy.wait_recv()
        gn = gtwo[...] + (back[...].astype(WIDE) + back_got[...].astype(WIDE))
        small[1:2, :] = cat([col_sum(gn * normal_one[...]), col_sum(gn)])
        g1 = norm_backward(gn, normal_one[...], inverse_one[:, :1], gain_one[...])
        gtwo[...] = g1
        gattn[...] = g1.astype(LOW)
        gc = dot_nt(gattn[...], wout[own_rows, :]).astype(LOW)
        for p in range(pairs):
            gctx[p] = gc[:, p * LANES:(p + 1) * LANES]
        small[3:8, :] = jnp.zeros((5, small.shape[1]), WIDE)
        small_copy(0).start()

    def masked_backward(p, c):
        q2 = qc[p].astype(WIDE)
        g2 = gctx[p].astype(WIDE)
        k2 = cat([qkv[pairs + p, :block_len, :], qkv[pairs + p, block_len:, :]])
        dk = jnp.zeros((block_len, 2 * LANES), WIDE)
        dv = jnp.zeros((block_len, 2 * LANES), WIDE)
        dq = []
        for e in range(2):
            head = 2 * p + e
            late = second(head)
            gm = keep_head(g2, e)
            dp = jnp.where(late, dot_nt(gm, qkv[2 * pairs + p, block_len:, :]),
                           dot_nt(gm, qkv[2 * pairs + p, :block_len, :]))
            pr = probs[head]
            t = dp * pr
            ds = (t - pr * jnp.sum(t, axis=-1, keepdims=True)).astype(LOW)
            qm = keep_head(q2, e).astype(WIDE)
            gm = gm.astype(WIDE)
            dk = dk + dot_tn(ds, cat([jnp.where(late, 0.0, qm), jnp.where(late, qm, 0.0)]).astype(LOW))
            dv = dv + dot_tn(pr.astype(LOW),
                             cat([jnp.where(late, 0.0, gm), jnp.where(late, gm, 0.0)]).astype(LOW))
            both = dot(ds, k2)
            dq.append(jnp.where(late, both[:, LANES:], both[:, :LANES]))
        d = (jnp.where(low_lane, dq[0], dq[1]) * scale).astype(LOW)
        dqc[p] = d
        dall[p] = dot(sel_t[...], d).astype(LOW)
        dk = (dk * scale).astype(LOW)
        dv = dv.astype(LOW)
        dall[pairs + p, :block_len, :] = dk[:, :LANES]
        dall[pairs + p, block_len:, :] = dk[:, LANES:]
        dall[2 * pairs + p, :block_len, :] = dv[:, :LANES]
        dall[2 * pairs + p, block_len:, :] = dv[:, LANES:]
        return c

    def small_copy(k):
        return pltpu.make_async_remote_copy(
            src_ref=small.at[pl.ds(8 * k, 8)], dst_ref=small_got.at[pl.ds(8 * k, 8)],
            send_sem=xs_send.at[x_slots + k], recv_sem=xs_recv.at[x_slots + k],
            device_id=peer(bits[k]), device_id_type=MESH)

    small_write = pltpu.make_async_copy(small_sum, small_out, lsem.at[3])

    def small_step(k):
        small_copy(k).wait_recv()
        total = small[8 * k:8 * k + 8, :] + small_got[8 * k:8 * k + 8, :]
        if k + 1 < len(bits):
            small[8 * k + 8:8 * k + 16, :] = total
            small_copy(k + 1).start()
        else:
            small_sum[...] = total
            small_write.start()

    def out_grad():
        put(f_out, 0, dot_tn(cat([ctxc[h * pairs + p] for p in range(pairs)]), gattn[...]).astype(LOW))
        ring["O0"].start()

    def qkv_grad(k):
        def grad(cols):
            gq = dot_tn(tokc[:, cols], cat([dqc[p] for p in range(pairs)]))
            gkv = dot_tn(tok[:, cols], cat([dall[pairs + j] for j in range(2 * pairs)]))
            return cat([gq, gkv]).astype(LOW)

        by_tiles("Q", k, f_qkv, grad)

    def far_copy(r):
        return x_copy(far.at[row_tile(r)], far_got.at[row_tile(r)], x_base2 + 2 + r)

    def far_tile(r):
        d = cat([dall[j, row_tile(r), :] for j in range(3 * pairs)])
        far[row_tile(r), :] = dot_nt(d, wqkv[far_cols, :]).astype(LOW)
        far_copy(r).start()

    def near_tile(r):
        mine = gtwo[:, own_cols]
        high = mine.astype(LOW)
        rest = (mine - high.astype(WIDE)).astype(LOW)
        d = cat([dall[j, row_tile(r), :] for j in range(3 * pairs)])
        spread = dot(sel_t[row_tile(r), :], cat([high, rest]))
        near[row_tile(r), :] = dot_nt(d, wqkv[own_cols, :]) + (spread[:, :own] + spread[:, own:])

    def grad_tile(r):
        far_copy(r).wait_recv()
        far_copy(r).wait_send()
        far[row_tile(r), :] = (near[row_tile(r), :] + far_got[row_tile(r), :].astype(WIDE)).astype(LOW)

    grad_out = pltpu.make_async_copy(far, grad_tokens, lsem.at[1])

    def down_copy(r):
        return x_copy(down_far.at[row_tile(r)], down_got.at[row_tile(r)], x_base2 + 2 + tiles + r)

    def ctx_wait(block):
        for i in range(block * pairs, (block + 1) * pairs):
            ctx_copy(i).wait_recv()

    def layer_tile(r):
        rs = row_tile(r)
        pre_r = tok[rs, :].astype(WIDE) + dot(cat([ctx[j, rs, :] for j in range(2 * pairs)]), wout[...])
        normed = normalize(pre_r)[0] * gain_one[...] + shift_one[...]
        normed_one[...] = normed
        u = dot(normed.astype(LOW), wup[...]) + b_up[...]
        hid = (u * (0.5 * (1.0 + lax.erf(u * root_half)))).astype(LOW)
        down_far[rs, :] = dot(hid, wdown[:, far_cols]).astype(LOW)
        down_copy(r).start()
        pre_two[rs, :] = normed_one[:, own_cols] + dot(hid, wdown[:, own_cols])

    first_lane = lax.broadcasted_iota(jnp.int32, (1, LANES), 1) < 1
    stats_copy = x_copy(stats, stats_got, x_base2 + 2 + 2 * tiles)

    def stat_tile(r):
        rs = row_tile(r)
        down_copy(r).wait_recv()
        x = pre_two[rs, :] + down_got[rs, :].astype(WIDE)
        pre_two[rs, :] = x
        mean = jnp.mean(x, axis=-1, keepdims=True)
        dev = x - mean
        var = jnp.mean(dev * dev, axis=-1, keepdims=True)
        both = jnp.where(first_lane, mean, var)
        stats[r] = jnp.transpose(both)[:8, :]

    def result_tile(r, c):
        rs = row_tile(r)
        x = pre_two[rs, :]
        fill = jnp.zeros((LANES - 8, tile), WIDE)
        one = jnp.transpose(jnp.concatenate([stats[r], fill], axis=0))
        two = jnp.transpose(jnp.concatenate([stats_got[r], fill], axis=0))
        mean = 0.5 * (one[:, :1] + two[:, :1])
        gap = 0.5 * (one[:, :1] - two[:, :1])
        var = 0.5 * (one[:, 1:2] + two[:, 1:2]) + gap * gap
        down_copy(r).wait_send()
        down_far[rs, :] = ((x - mean) * lax.rsqrt(var + norm_eps) * vecs[2:3, own_cols]
                         + vecs[3:4, own_cols]).astype(LOW)
        return c

    result_out = pltpu.make_async_copy(down_far, result, lsem.at[2])

    def write_result():
        stats_copy.wait_recv()
        lax.fori_loop(0, tiles, result_tile, 0)
        result_out.start()

    x_slots = x_base2 + 3 + 2 * tiles
    steps = {"down": down_grad, "in": input_grad, "up": up_grad, "norm": first_norm, "attend": attend_more,
             "mb": lambda p: masked_backward(p, 0), "out": out_grad, "qkv": qkv_grad, "gout": grad_out.start,
             "stats": stats_copy.start, "result": write_result, "small": small_step, "ctx": ctx_wait}
    looped = {"far": far_tile, "near": near_tile, "grad": grad_tile, "layer": layer_tile, "stat": stat_tile}
    for name, *at in PLAN:
        if name in ring:
            ring[name].advance(at[0])
        elif name in looped:
            lax.fori_loop(at[0], at[1], lambda r, c, name=name: looped[name](r) or c, 0)
        else:
            steps[name](*at)
    for k in range(min(len(bits), 4), len(bits)):
        small_step(k)

    for r in range(tiles):
        tok_copy(r).wait_send()
    grad_out.wait()
    result_out.wait()
    small_write.wait()
    for i in range(attend_units):
        ctx_copy(i).wait_send()
    for p in range(pairs):
        ctxc_copy(p).wait_send()
    for cp in (part_copy, back_copy, stats_copy):
        cp.wait_send()
    for k in range(len(bits)):
        small_copy(k).wait_send()
    for one in ring.values():
        one.finish()


def build(n, tokens, wqkv, wout, gain_one, shift_one, wup, b_up, wdown, gain_two, shift_two, perm, index,
          count, cot):
    rows, own = tokens.shape
    width = wout.shape[0]
    local = wqkv.shape[2]
    pairs = local // LANES
    heads = local // HEAD_DIM
    slots = index.shape[1]
    ff = wup.shape[1]
    block_len = rows // 2
    tile = 256
    steps = n.bit_length() - 1
    bits = [1 << k for k in range(steps)]
    depth = min(4, steps)
    units = 1 << depth
    halving, extra = bits[:depth], bits[depth:]

    vm = pltpu.VMEM
    groups = {"D": (ff, width), "U": (width, ff), "O": (local, width), "Q": (width, 3 * local)}
    shapes = {g: (CHUNKS[g] * units, r // (CHUNKS[g] * units), c) for g, (r, c) in groups.items()}
    names = [(g, k) for g in groups for k in range(CHUNKS[g])]
    dma = pltpu.SemaphoreType.DMA

    def ring_scratch(g):
        _, r, c = shapes[g]
        sizes = [units >> (k + 1) for k in range(depth)]
        return {
            "recv": [vm((s, r, c), LOW) for s in sizes],
            "send": [vm((s, r, c), LOW) for s in sizes[1:]],
            "keep": [vm((s, r, c), WIDE) for s in sizes[1:]],
            "xsend": vm((1, r, c) if extra else (1, 8, LANES), LOW),
            "xrecv": vm((len(extra), r, c) if extra else (1, 8, LANES), LOW),
            "sems": (dma((2 * depth + len(extra),)), dma((2 * depth + len(extra),)), dma(())),
        }

    f = [vm(shapes[g], LOW) for g in groups]
    x_slots = 3 * (rows // tile) + 3 * pairs + 3
    scratch = [
        vm((width, 3 * local), LOW), vm(wout.shape, LOW), vm(wup.shape, LOW), vm(wdown.shape, LOW), dma((6,)),
        vm((8, ff), WIDE),
        vm((rows, width), LOW), vm((3 * pairs, rows, LANES), LOW), vm((rows, slots), LOW), vm((slots, rows), LOW),
        vm((slots, LANES), WIDE), vm((slots, width), LOW), vm((pairs, slots, LANES), LOW),
        vm((heads, slots, block_len), WIDE), vm((2 * pairs, slots, LANES), LOW), vm((slots, width), WIDE),
        vm((slots, LANES), WIDE), vm((slots, width), WIDE), vm((slots, width), LOW), vm((slots, ff), WIDE),
        vm((slots, ff), LOW), vm((slots, width), LOW), vm((slots, width), LOW), vm((slots, width), LOW),
        vm((slots, width), WIDE), vm((slots, ff), LOW), vm((slots, width), LOW), vm((slots, width), LOW),
        vm((slots, width), LOW), vm((pairs, slots, LANES), LOW),
        vm((pairs, slots, LANES), LOW), vm((3 * pairs, rows, LANES), LOW), vm((rows, own), LOW),
        vm((rows, own), LOW), vm((rows, own), WIDE),
        vm((2 * pairs, rows, LANES), LOW), vm((rows, own), WIDE), vm((rows, own), LOW),
        vm((rows, own), LOW), vm((rows // tile, 8, tile), WIDE), vm((rows // tile, 8, tile), WIDE),
        *f, vm((8 * steps, ff), WIDE), vm((8 * steps, ff), WIDE), vm((8, ff), WIDE),
        dma((x_slots + steps,)), dma((x_slots + steps,)), dma((4,)),
    ]
    plain = len(scratch)
    ring_specs = [ring_scratch(g) for g, _ in names]
    flat, tree = jax.tree.flatten(ring_specs, is_leaf=lambda x: not isinstance(x, (dict, list, tuple)))
    n_in, n_out = 14, 7

    def run(*refs):
        head_refs = refs[:n_in + n_out + plain]
        rings = jax.tree.unflatten(tree, refs[n_in + n_out + plain:])
        firsts = head_refs[-(len(groups) + 6):-6]
        outs = refs[n_in + 2:n_in + 2 + len(groups)]
        full = {}
        for (g, k), ring in zip(names, rings):
            i = list(groups).index(g)
            part = pl.ds(k * units, units)
            full["%s%d" % (g, k)] = dict(order=[halving[j] for j in ORDERS[g][k] if j < depth], extra=extra,
                                         first=firsts[i].at[part], out=outs[i].at[part], **ring)
        kernel(n, (*head_refs, full))

    hbm = pl.BlockSpec(memory_space=pl.ANY)
    v = pl.BlockSpec(memory_space=pltpu.VMEM)
    shape = jax.ShapeDtypeStruct
    return pl.pallas_call(
        run,
        out_shape=(shape((rows, own), LOW), shape((rows, own), LOW),
                   *(shape(shapes[g], LOW) for g in groups), shape((8, ff), WIDE)),
        in_specs=[hbm, hbm, hbm, hbm, hbm, v, v, v, v, v, v, v, v, v],
        out_specs=(hbm,) * 7,
        scratch_shapes=scratch + flat,
        compiler_params=pltpu.CompilerParams(
            collective_id=0, has_side_effects=True, vmem_limit_bytes=VMEM_BYTES),
        name="layer",
    )(tokens, wqkv, wout, wup, wdown, gain_one, shift_one, gain_two, shift_two, b_up, perm, count, index, cot)


def finish(refs):
    (f_down, f_up, f_out, f_qkv, small, res_in, tok_in,
     down, up, out, qkv, gain_one, shift_one, bias, gain_two, shift_two, res, tok,
     b_down, b_up, b_out, b_qkv, w_down, w_up, w_out, w_qkv, b_res, b_tok, b_small, v_one, v_two, v_bias, v_three,
     v_four, isem, osem) = refs
    width = gain_one.shape[0]
    local = qkv.shape[2]
    reads, writes = [], []

    def read(src, dst):
        cp = pltpu.make_async_copy(src, dst, isem.at[len(reads)])
        cp.start()
        reads.append(cp)
        return cp

    def write(src, dst):
        cp = pltpu.make_async_copy(src, dst, osem.at[len(writes)])
        cp.start()
        writes.append(cp)

    parts = 4
    jobs = []
    for src, low, wide, dst in ((f_down, b_down, w_down, down), (f_up, b_up, w_up, up),
                                (f_out, b_out, w_out, out), (f_qkv, b_qkv, w_qkv, qkv)):
        step = src.shape[0] // parts if src.shape[0] % parts == 0 else src.shape[0]
        for u in range(0, src.shape[0], step):
            jobs.append((read(src.at[pl.ds(u, step)], low.at[pl.ds(u, step)]), u, step, low, wide, dst))
    pass_on = [(read(a, b), b, c) for a, b, c in ((res_in, b_res, res), (tok_in, b_tok, tok))]
    small_read = read(small, b_small)
    for cp, u, step, low, wide, dst in jobs:
        cp.wait()
        r = low.shape[1]

        def unit(j, c, u=u, low=low, wide=wide, r=r, dst=dst):
            v = low[u + j].astype(WIDE)
            rows = pl.ds(pl.multiple_of((u + j) * r, r), r)
            if dst is qkv:
                for k in range(3):
                    wide[k, rows, :] = v[:, k * local:(k + 1) * local]
            else:
                wide[rows, :] = v
            return c

        lax.fori_loop(0, step, unit, 0)
        rows = pl.ds(u * r, step * r)
        if dst is qkv:
            write(wide.at[:, rows, :], dst.at[:, rows, :])
        else:
            write(wide.at[rows, :], dst.at[rows, :])
    for cp, src, dst in pass_on:
        cp.wait()
        write(src, dst)
    small_read.wait()
    for row, at, vec, dst in ((1, 0, v_one, gain_one), (1, width, v_two, shift_one), (0, 0, v_bias, bias),
                              (2, 0, v_three, gain_two), (2, width, v_four, shift_two)):
        size = vec.shape[0]
        vec[...] = b_small[row:row + 1, at:at + size].reshape(size)
        write(vec, dst)
    for cp in writes:
        cp.wait()


def widen(g_down, g_up, g_out, g_qkv, small, result, grad_tokens):
    units, r_qkv, three = g_qkv.shape
    local, width, ff = three // 3, g_down.shape[2], g_up.shape[2]
    shape = jax.ShapeDtypeStruct
    hbm = pl.BlockSpec(memory_space=pl.ANY)
    wide = [(ff, width), (width, ff), (local, width), (3, width, local)]
    low = [g.shape for g in (g_down, g_up, g_out, g_qkv)]
    acts = [result.shape, grad_tokens.shape]
    return pl.pallas_call(
        lambda *refs: finish(refs),
        out_shape=(*(shape(x, WIDE) for x in wide), shape((width,), WIDE), shape((width,), WIDE),
                   shape((ff,), WIDE), shape((width,), WIDE), shape((width,), WIDE),
                   *(shape(x, LOW) for x in acts)),
        in_specs=[hbm] * 7,
        out_specs=(hbm,) * 11,
        scratch_shapes=[*(pltpu.VMEM(x, LOW) for x in low), *(pltpu.VMEM(x, WIDE) for x in wide),
                        *(pltpu.VMEM(x, LOW) for x in acts), pltpu.VMEM(small.shape, WIDE),
                        *(pltpu.VMEM(x, WIDE) for x in ((width,), (width,), (ff,), (width,), (width,))),
                        pltpu.SemaphoreType.DMA((24,)), pltpu.SemaphoreType.DMA((24,))],
        compiler_params=pltpu.CompilerParams(vmem_limit_bytes=VMEM_BYTES),
        name="widen",
    )(g_down, g_up, g_out, g_qkv, small, result, grad_tokens)


def body(n, tokens, w_qkv, w_out, gain_one, attention_norm_bias, w_up, b_up, w_down, gain_two, shift_two,
         block_perm, mask_index, mask_count, cotangent):
    result, grad_tokens, g_down, g_up, g_out, g_qkv, small = build(
        n, tokens, w_qkv.transpose(1, 0, 2), w_out, gain_one, attention_norm_bias, w_up, b_up, w_down, gain_two,
        shift_two, block_perm.T, mask_index, mask_count.reshape(1, 1), cotangent[0])
    (g_down, g_up, g_out, g_qkv, g_gain_one, g_shift_one, g_bias, g_gain_two, g_shift_two, result,
     grad_tokens) = widen(g_down, g_up, g_out, g_qkv, small, result, grad_tokens)
    return (result, grad_tokens, g_qkv.transpose(1, 0, 2), g_out, g_gain_one, g_shift_one, g_up, g_bias, g_down,
            g_gain_two, g_shift_two)


def solution(mesh):
    return jax.shard_map(
        functools.partial(body, mesh.shape["batch"]),
        mesh=mesh,
        in_specs=(P("batch", "head"), P(None, None, "head"), P(), P(), P(), P(None, "head"), P("head"),
                  P("head", None), P(), P(), P("head", None), P("batch", None), P("batch"),
                  P("batch", None, None)),
        out_specs=(P("batch", "head"), P("batch", "head"), P(None, None, "head"), P("head", None), P(), P(),
                   P(None, "head"), P("head"), P("head", None), P(), P()),
        check_vma=False,
    )
```

```python
import functools

import jax
import jax.numpy as jnp
from jax import lax
from jax.experimental import pallas as pl
from jax.experimental.pallas import tpu as pltpu
from jax.sharding import PartitionSpec as P

HEAD_DIM = 64
norm_eps = 1e-06
root_half = 0.7071067811865476
inv_root_two_pi = 0.3989422804014327
log2_e = 1.4426950408889634
LOW = jnp.bfloat16
WIDE = jnp.float32
LANES = 128
MESH = pl.DeviceIdType.MESH
VMEM_BYTES = 67043328
CUTS = (2, 4)
CHUNKS = {"D": 3, "U": 3, "O": 1, "Q": 2}
ORDERS = {"D": [[0, 1, 2, 3], [0, 2, 3, 1], [0, 2, 1, 3]],
          "U": [[0, 1, 2, 3], [0, 1, 2, 3], [0, 1, 2, 3]],
          "O": [[0, 1, 2, 3]],
          "Q": [[0, 1, 2, 3], [0, 1, 3, 2]]}
PLAN = (
    ("down", 0), ("down", 1), ("in",), ("D0", 0), ("D1", 0), ("down", 2), ("up", 0), ("up", 1), ("up", 2),
    ("D2", 0), ("attend",), ("U0", 0), ("U1", 0), ("U2", 0), ("D0", 1), ("D1", 1), ("ctx", 0), ("layer", 0, 1),
    ("D2", 1), ("norm",), ("U0", 1), ("D0", 2), ("mb", 0), ("mb", 1), ("D1", 2), ("U1", 1), ("U0", 2),
    ("small", 0), ("mb", 2), ("D0", 3), ("U2", 1), ("out",), ("U1", 2), ("qkv", 0), ("O0", 0), ("U0", 3),
    ("small", 1), ("far", 0, 1), ("qkv", 1), ("Q0", 0), ("D0", 4), ("U2", 2), ("far", 1, 2), ("D2", 2),
    ("U1", 3), ("Q1", 0), ("O0", 1), ("small", 2), ("far", 2, 3), ("U0", 4), ("ctx", 1), ("layer", 2, 3),
    ("D0", 5), ("U2", 3), ("Q0", 1), ("D2", 3), ("small", 3), ("far", 3, 4), ("layer", 3, 4), ("O0", 2),
    ("Q1", 1), ("near", 0, 1), ("U2", 4), ("near", 1, 2), ("U0", 5), ("Q0", 2), ("near", 2, 3), ("U1", 4),
    ("D0", 6), ("near", 3, 4), ("D2", 4), ("grad", 0, 1), ("layer", 1, 2), ("D1", 3), ("O0", 3), ("D0", 7),
    ("U0", 6), ("U2", 5), ("Q1", 2), ("grad", 1, 4), ("gout",), ("stat", 0, 1), ("U0", 7), ("stat", 2, 3),
    ("Q0", 3), ("D1", 4), ("U1", 5), ("stat", 3, 4), ("O0", 4), ("Q1", 3), ("U2", 6), ("Q0", 4),
    ("stat", 1, 2), ("stats",), ("U2", 7), ("O0", 5), ("U1", 6), ("Q1", 4), ("result",), ("D1", 5), ("U1", 7), ("D2", 5),
    ("Q0", 5), ("O0", 6), ("O0", 7), ("Q1", 5), ("Q0", 6), ("D1", 6), ("Q0", 7), ("D1", 7), ("D2", 6),
    ("Q1", 6), ("D2", 7), ("Q1", 7),
)


def dot(a, b):
    return lax.dot_general(a, b, (((1,), (0,)), ((), ())), preferred_element_type=WIDE)


def dot_nt(a, b):
    return lax.dot_general(a, b, (((1,), (1,)), ((), ())), preferred_element_type=WIDE)


def dot_tn(a, b):
    return lax.dot_general(a, b, (((0,), (0,)), ((), ())), preferred_element_type=WIDE)


def normalize(values):
    centered = values - jnp.mean(values, axis=-1, keepdims=True)
    inverse = lax.rsqrt(jnp.mean(centered * centered, axis=-1, keepdims=True) + norm_eps)
    return centered * inverse, inverse


def norm_backward(upstream, normal, inverse, gain_vec):
    scaled = upstream * gain_vec
    return inverse * (
        scaled
        - jnp.mean(scaled, axis=-1, keepdims=True)
        - normal * jnp.mean(scaled * normal, axis=-1, keepdims=True)
    )


def col_sum(x):
    return jnp.sum(x, axis=0, keepdims=True)


def cat(parts):
    return jnp.concatenate(parts, axis=1)


class Ring:
    def __init__(self, order, extra, first, out, recv, send, keep, xsend, xrecv, sems, peer, bit_of):
        self.order, self.extra = order, extra
        self.first, self.out = first, out
        self.recv, self.send, self.keep = recv, send, keep
        self.xsend, self.xrecv = xsend, xrecv
        self.ssem, self.rsem, self.lsem = sems
        self.peer = peer
        self.mine = [bit_of(b) for b in order]
        units = first.shape[0]
        self.sizes = [units >> (k + 1) for k in range(len(order))]
        self.base = []
        base = 0
        for k in range(len(order)):
            base = base + self.mine[k] * self.sizes[k]
            self.base.append(base)

    def _copy(self, src, dst, slot, bit):
        return pltpu.make_async_remote_copy(
            src_ref=src, dst_ref=dst, send_sem=self.ssem.at[slot], recv_sem=self.rsem.at[slot],
            device_id=self.peer(bit), device_id_type=MESH)

    def _rs(self, k):
        size = self.sizes[k]
        if k == 0:
            src = self.first.at[pl.ds((1 - self.mine[0]) * size, size)]
        else:
            src = self.send[k - 1]
        return self._copy(src, self.recv[k], k, self.order[k])

    def _x(self, j):
        return self._copy(self.xsend, self.xrecv.at[pl.ds(j, 1)], len(self.order) + j, self.extra[j])

    def _ag(self, k):
        slot = len(self.order) + len(self.extra) + k
        part = self.first.at[pl.ds(self.base[k], self.sizes[k])]
        return self._copy(part, part, slot, self.order[k])

    def _write(self):
        return pltpu.make_async_copy(self.first, self.out, self.lsem)

    def start(self):
        self._rs(0).start()

    def _value(self, k, u):
        got = self.recv[k][u].astype(WIDE)
        if k == 0:
            return self.first[self.mine[0] * self.sizes[0] + u].astype(WIDE) + got
        return self.keep[k - 1][u] + got

    def reduce(self, k):
        self._rs(k).wait_recv()
        if k == 0:
            self._rs(0).wait_send()
        if k + 1 < len(self.order):
            half = self.sizes[k + 1]
            mine = self.mine[k + 1]

            def out_part(j, c):
                self.send[k][j] = self._value(k, (1 - mine) * half + j).astype(LOW)
                return c

            lax.fori_loop(0, half, out_part, 0)
            self._rs(k + 1).start()

            def own_part(j, c):
                self.keep[k][j] = self._value(k, mine * half + j)
                return c

            lax.fori_loop(0, half, own_part, 0)
        else:
            total = self._value(k, 0)
            for j in range(len(self.extra)):
                self.xsend[0] = total.astype(LOW)
                self._x(j).start()
                self._x(j).wait()
                total = self.xsend[0].astype(WIDE) + self.xrecv[j].astype(WIDE)
            self.first[self.base[k]] = total.astype(LOW)
            self._ag(k).start()

    def gather(self, k):
        self._ag(k + 1).wait_recv()
        if k >= 0:
            self._ag(k).start()
        else:
            self._write().start()

    def advance(self, stage):
        depth = len(self.order)
        if stage < depth:
            self.reduce(stage)
        else:
            self.gather(2 * depth - 2 - stage)

    def finish(self):
        for k in range(len(self.order)):
            if k > 0:
                self._rs(k).wait_send()
            self._ag(k).wait_send()
        self._write().wait()


def kernel(n, refs):
    (tokens, wqkv_hbm, wout_hbm, wup_hbm, wdown_hbm, *vectors,
     perm, count, index, cot,
     result, grad_tokens, o_down, o_up, o_out, o_qkv, small_out,
     wqkv, wout, wup, wdown, wsem, vecs,
     tok, qkv, sel_t, sel, blk, tokc, qc, probs, ctxc, normal_one, inverse_one, normed_one, low_one, slope,
     hidden, part, part_got, gb, gtwo, gin, back, back_got, gattn, gctx, dqc, dall, far, far_got, near,
     ctx, pre_two, down_far, down_got, stats, stats_got,
     f_down, f_up, f_out, f_qkv, small, small_got, small_sum,
     xs_send, xs_recv, lsem, rings) = refs
    rows, own = tokens.shape
    width = wout.shape[0]
    local = wqkv.shape[1] // 3
    pairs = local // LANES
    slots = index.shape[1]
    ff = wup.shape[1]
    block_len = rows // 2
    tile = 256
    tiles = rows // tile
    scale = HEAD_DIM ** (-0.5)
    b = lax.axis_index("batch")
    h = lax.axis_index("head")
    other = 1 - h
    bits = [1 << k for k in range(n.bit_length() - 1)]

    def bit_of(bit):
        return lax.rem(lax.div(b, bit), 2)

    def peer(bit):
        return (b + bit - 2 * bit * bit_of(bit), h)

    x_peer = (b, other)

    def x_copy(src, dst, slot):
        return pltpu.make_async_remote_copy(
            src_ref=src, dst_ref=dst, send_sem=xs_send.at[slot], recv_sem=xs_recv.at[slot],
            device_id=x_peer, device_id_type=MESH)

    loads = [pltpu.make_async_copy(s, d, wsem.at[i]) for i, (s, d) in enumerate(
        [(wqkv_hbm.at[j], wqkv.at[:, pl.ds(j * local, local)]) for j in range(3)]
        + [(wout_hbm, wout), (wup_hbm, wup), (wdown_hbm, wdown)])]
    for cp in loads:
        cp.start()
    barrier = pltpu.get_barrier_semaphore()
    pl.semaphore_signal(barrier, inc=1, device_id=x_peer, device_id_type=MESH)
    for bit in bits:
        pl.semaphore_signal(barrier, inc=1, device_id=peer(bit), device_id_type=MESH)
    pl.semaphore_wait(barrier, 1 + len(bits))

    own_cols = pl.ds(pl.multiple_of(h * own, LANES), own)
    far_cols = pl.ds(pl.multiple_of(other * own, LANES), own)

    def row_tile(r):
        return pl.ds(pl.multiple_of(r * tile, tile), tile)

    def tok_copy(r):
        return x_copy(tokens.at[row_tile(r)], tok.at[row_tile(r), own_cols], r)

    for r in range(tiles):
        tok_copy(r).start()
    own_tok = pltpu.make_async_copy(tokens, tok.at[:, own_cols], lsem.at[0])
    own_tok.start()

    for i, vector in enumerate(vectors):
        vecs[i:i + 1, :vector.shape[0]] = vector[...].reshape(1, -1)
    gain_one, shift_one, gain_two, shift_two = (vecs.at[i:i + 1, :width] for i in range(4))
    b_up = vecs.at[4:5, :]

    lane_slot = lax.broadcasted_iota(jnp.int32, (1, slots), 1)
    idx = jnp.where(lane_slot < count[...], index[...], -1)
    picked = jnp.where(lax.broadcasted_iota(jnp.int32, (rows, slots), 0) == idx, 1.0, 0.0)
    sel_t[...] = picked.astype(LOW)
    picked = jnp.transpose(picked)
    sel[...] = picked.astype(LOW)
    blk[...] = jnp.broadcast_to(jnp.sum(picked[:, block_len:], axis=1, keepdims=True), blk.shape)
    own_tok.wait()
    for cp in loads[:3]:
        cp.wait()

    def qkv_tile(r, c):
        tok_copy(r).wait_recv()
        out = dot(tok[row_tile(r), :], wqkv[...]).astype(LOW)
        for j in range(3 * pairs):
            qkv[j, row_tile(r), :] = out[:, j * LANES:(j + 1) * LANES]
        return c

    lax.fori_loop(0, tiles, qkv_tile, 0)

    low_lane = lax.broadcasted_iota(jnp.int32, (1, LANES), 1) < HEAD_DIM
    def keep_head(x, e):
        return jnp.where(low_lane, x, 0.0).astype(LOW) if e == 0 else jnp.where(low_lane, 0.0, x).astype(LOW)

    order = perm[...].astype(WIDE)
    head_lane = lax.broadcasted_iota(jnp.int32, order.shape, 1)

    def blocks_of(head):
        return jnp.sum(jnp.where(head_lane == head, order, 0.0), axis=1, keepdims=True)

    def second(head):
        pair = blocks_of(head)
        return (pair[:1] + blk[:, :1] * (pair[1:] - pair[:1])) > 0.5

    def masked_attention(p, c):
        q2 = dot(sel[...], qkv[p]).astype(LOW)
        qc[p] = q2
        halves = []
        for e in range(2):
            head = 2 * p + e
            late = second(head)
            qm = keep_head(q2.astype(WIDE), e)
            s = jnp.where(late, dot_nt(qm, qkv[pairs + p, block_len:, :]),
                          dot_nt(qm, qkv[pairs + p, :block_len, :])) * (scale * log2_e)
            ex = jnp.exp2(s - jnp.max(s, axis=-1, keepdims=True))
            pr = ex * (1.0 / jnp.sum(ex, axis=-1, keepdims=True))
            probs[head] = pr
            pr = pr.astype(LOW)
            halves.append(jnp.where(late, dot(pr, qkv[2 * pairs + p, block_len:, :]),
                                    dot(pr, qkv[2 * pairs + p, :block_len, :])))
        ctxc[h * pairs + p] = jnp.where(low_lane, halves[0], halves[1]).astype(LOW)
        ctxc_copy(p).start()
        return c

    def ctxc_copy(p):
        mine_c = ctxc.at[pl.ds(h * pairs + p, 1)]
        return x_copy(mine_c, mine_c, tiles + p)

    lax.fori_loop(0, pairs, masked_attention, 0)

    def attend(i, c):
        p = lax.rem(i, pairs)
        q_block = lax.div(i, pairs)
        q_rows = pl.ds(pl.multiple_of(q_block * block_len, block_len), block_len)
        q2 = qkv[p, q_rows, :].astype(WIDE)
        even, odd = blocks_of(2 * p), blocks_of(2 * p + 1)
        late = jnp.where(low_lane, jnp.where(q_block == 0, even[:1], even[1:]),
                         jnp.where(q_block == 0, odd[:1], odd[1:])) > 0.5

        def chosen(j):
            return jnp.where(late, qkv[j, block_len:, :].astype(WIDE), qkv[j, :block_len, :].astype(WIDE)).astype(LOW)

        k2, v2 = chosen(pairs + p), chosen(2 * pairs + p)
        halves = []
        for e in range(2):
            s = dot_nt(keep_head(q2, e), k2) * (scale * log2_e)
            ex = jnp.exp2(s - jnp.max(s, axis=-1, keepdims=True))
            inv = 1.0 / jnp.sum(ex, axis=-1, keepdims=True)
            halves.append(dot(ex.astype(LOW), v2) * inv)
        ctx[h * pairs + p, q_rows, :] = jnp.where(low_lane, halves[0], halves[1]).astype(LOW)
        ctx_copy(i).start()
        return c

    x_base = tiles + pairs

    def ctx_copy(i):
        q_rows = pl.ds(pl.multiple_of(lax.div(i, pairs) * block_len, block_len), block_len)
        part_ref = ctx.at[pl.ds(h * pairs + lax.rem(i, pairs), 1), q_rows]
        return x_copy(part_ref, part_ref, x_base + i)

    tokc[...] = dot(sel[...], tok[...]).astype(LOW)
    attend_units = 2 * pairs
    x_base2 = x_base + attend_units
    lax.fori_loop(0, CUTS[0], attend, 0)

    for p in range(pairs):
        ctxc_copy(p).wait_recv()
    for cp in loads[3:]:
        cp.wait()
    pre = tokc[...].astype(WIDE) + dot(cat([ctxc[j] for j in range(2 * pairs)]), wout[...])
    nrm_c, inv_c = normalize(pre)
    normal_one[...] = nrm_c
    inverse_one[...] = jnp.broadcast_to(inv_c, inverse_one.shape)
    nrm_c = nrm_c * gain_one[...] + shift_one[...]
    normed_one[...] = nrm_c
    low_one[...] = nrm_c.astype(LOW)
    ff_tile = 384

    def up_tile(i, c):
        cols = pl.ds(pl.multiple_of(i * ff_tile, ff_tile), ff_tile)
        u = dot(low_one[...], wup[:, cols]) + vecs[4:5, cols]
        cdf = 0.5 * (1.0 + lax.erf(u * root_half))
        hidden[:, cols] = (u * cdf).astype(LOW)
        slope[:, cols] = cdf + u * inv_root_two_pi * jnp.exp(-0.5 * u * u)
        return c

    lax.fori_loop(0, ff // ff_tile, up_tile, 0)
    part[...] = dot(hidden[...], wdown[...]).astype(LOW)
    part_copy = x_copy(part, part_got, x_base2)
    part_copy.start()
    lax.fori_loop(CUTS[0], CUTS[1], attend, 0)
    part_copy.wait_recv()

    normal_two, inv_two = normalize(normed_one[...] + (part[...].astype(WIDE) + part_got[...].astype(WIDE)))
    alive = lax.broadcasted_iota(jnp.int32, (slots, 1), 0) < count[...]
    up = jnp.where(alive, cot[...].astype(WIDE), 0.0)
    g2 = norm_backward(up, normal_two, inv_two, gain_two[...])
    gtwo[...] = g2
    gb[...] = g2.astype(LOW)
    small[2:3, :] = cat([col_sum(up * normal_two), col_sum(up)])

    def put(first, unit, value):
        r = first.shape[1]
        for j in range(value.shape[0] // r):
            first[unit + j] = value[j * r:(j + 1) * r, :]

    ring = {name: Ring(peer=peer, bit_of=bit_of, **r) for name, r in rings.items()}

    def by_tiles(group, k, first, grad):
        units = first.shape[0] // CHUNKS[group]
        size = units * first.shape[1]
        step = 256 if size % 256 == 0 else 384

        def one_tile(i, c):
            at = k * size + i * step
            put(first, k * units + i * (step * units // size), grad(pl.ds(pl.multiple_of(at, LANES), step)))
            return c

        lax.fori_loop(0, size // step, one_tile, 0)
        ring["%s%d" % (group, k)].start()

    def down_grad(k):
        by_tiles("D", k, f_down, lambda cols: dot_tn(hidden[:, cols], gb[...]).astype(LOW))

    def up_grad(k):
        by_tiles("U", k, f_up, lambda cols: dot_tn(low_one[:, cols], gin[...]).astype(LOW))

    def in_tile(i, c):
        cols = pl.ds(pl.multiple_of(i * ff_tile, ff_tile), ff_tile)
        g = (dot_nt(gb[...], wdown[cols, :]) * slope[:, cols]).astype(LOW)
        gin[:, cols] = g
        small[0:1, cols] = col_sum(g.astype(WIDE))
        return c

    back_copy = x_copy(back, back_got, x_base2 + 1)

    def input_grad():
        lax.fori_loop(0, ff // ff_tile, in_tile, 0)
        back[...] = dot_nt(gin[...], wup[...]).astype(LOW)
        back_copy.start()

    def attend_more():
        lax.fori_loop(CUTS[1], attend_units, attend, 0)

    own_rows = pl.ds(pl.multiple_of(h * local, LANES), local)

    def first_norm():
        back_copy.wait_recv()
        gn = gtwo[...] + (back[...].astype(WIDE) + back_got[...].astype(WIDE))
        small[1:2, :] = cat([col_sum(gn * normal_one[...]), col_sum(gn)])
        g1 = norm_backward(gn, normal_one[...], inverse_one[:, :1], gain_one[...])
        gtwo[...] = g1
        gattn[...] = g1.astype(LOW)
        gc = dot_nt(gattn[...], wout[own_rows, :]).astype(LOW)
        for p in range(pairs):
            gctx[p] = gc[:, p * LANES:(p + 1) * LANES]
        small[3:8, :] = jnp.zeros((5, small.shape[1]), WIDE)
        small_copy(0).start()

    def masked_backward(p, c):
        q2 = qc[p].astype(WIDE)
        g2 = gctx[p].astype(WIDE)
        k2 = cat([qkv[pairs + p, :block_len, :], qkv[pairs + p, block_len:, :]])
        dk = jnp.zeros((block_len, 2 * LANES), WIDE)
        dv = jnp.zeros((block_len, 2 * LANES), WIDE)
        dq = []
        for e in range(2):
            head = 2 * p + e
            late = second(head)
            gm = keep_head(g2, e)
            dp = jnp.where(late, dot_nt(gm, qkv[2 * pairs + p, block_len:, :]),
                           dot_nt(gm, qkv[2 * pairs + p, :block_len, :]))
            pr = probs[head]
            t = dp * pr
            ds = (t - pr * jnp.sum(t, axis=-1, keepdims=True)).astype(LOW)
            qm = keep_head(q2, e).astype(WIDE)
            gm = gm.astype(WIDE)
            dk = dk + dot_tn(ds, cat([jnp.where(late, 0.0, qm), jnp.where(late, qm, 0.0)]).astype(LOW))
            dv = dv + dot_tn(pr.astype(LOW),
                             cat([jnp.where(late, 0.0, gm), jnp.where(late, gm, 0.0)]).astype(LOW))
            both = dot(ds, k2)
            dq.append(jnp.where(late, both[:, LANES:], both[:, :LANES]))
        d = (jnp.where(low_lane, dq[0], dq[1]) * scale).astype(LOW)
        dqc[p] = d
        dall[p] = dot(sel_t[...], d).astype(LOW)
        dk = (dk * scale).astype(LOW)
        dv = dv.astype(LOW)
        dall[pairs + p, :block_len, :] = dk[:, :LANES]
        dall[pairs + p, block_len:, :] = dk[:, LANES:]
        dall[2 * pairs + p, :block_len, :] = dv[:, :LANES]
        dall[2 * pairs + p, block_len:, :] = dv[:, LANES:]
        return c

    def small_copy(k):
        return pltpu.make_async_remote_copy(
            src_ref=small.at[pl.ds(8 * k, 8)], dst_ref=small_got.at[pl.ds(8 * k, 8)],
            send_sem=xs_send.at[x_slots + k], recv_sem=xs_recv.at[x_slots + k],
            device_id=peer(bits[k]), device_id_type=MESH)

    small_write = pltpu.make_async_copy(small_sum, small_out, lsem.at[3])

    def small_step(k):
        small_copy(k).wait_recv()
        total = small[8 * k:8 * k + 8, :] + small_got[8 * k:8 * k + 8, :]
        if k + 1 < len(bits):
            small[8 * k + 8:8 * k + 16, :] = total
            small_copy(k + 1).start()
        else:
            small_sum[...] = total
            small_write.start()

    def out_grad():
        put(f_out, 0, dot_tn(cat([ctxc[h * pairs + p] for p in range(pairs)]), gattn[...]).astype(LOW))
        ring["O0"].start()

    def qkv_grad(k):
        def grad(cols):
            gq = dot_tn(tokc[:, cols], cat([dqc[p] for p in range(pairs)]))
            gkv = dot_tn(tok[:, cols], cat([dall[pairs + j] for j in range(2 * pairs)]))
            return cat([gq, gkv]).astype(LOW)

        by_tiles("Q", k, f_qkv, grad)

    def far_copy(r):
        return x_copy(far.at[row_tile(r)], far_got.at[row_tile(r)], x_base2 + 2 + r)

    def far_tile(r):
        d = cat([dall[j, row_tile(r), :] for j in range(3 * pairs)])
        far[row_tile(r), :] = dot_nt(d, wqkv[far_cols, :]).astype(LOW)
        far_copy(r).start()

    def near_tile(r):
        mine = gtwo[:, own_cols]
        high = mine.astype(LOW)
        rest = (mine - high.astype(WIDE)).astype(LOW)
        d = cat([dall[j, row_tile(r), :] for j in range(3 * pairs)])
        spread = dot(sel_t[row_tile(r), :], cat([high, rest]))
        near[row_tile(r), :] = dot_nt(d, wqkv[own_cols, :]) + (spread[:, :own] + spread[:, own:])

    def grad_tile(r):
        far_copy(r).wait_recv()
        far_copy(r).wait_send()
        far[row_tile(r), :] = (near[row_tile(r), :] + far_got[row_tile(r), :].astype(WIDE)).astype(LOW)

    grad_out = pltpu.make_async_copy(far, grad_tokens, lsem.at[1])

    def down_copy(r):
        return x_copy(down_far.at[row_tile(r)], down_got.at[row_tile(r)], x_base2 + 2 + tiles + r)

    def ctx_wait(block):
        for i in range(block * pairs, (block + 1) * pairs):
            ctx_copy(i).wait_recv()

    def layer_tile(r):
        rs = row_tile(r)
        pre_r = tok[rs, :].astype(WIDE) + dot(cat([ctx[j, rs, :] for j in range(2 * pairs)]), wout[...])
        normed = normalize(pre_r)[0] * gain_one[...] + shift_one[...]
        normed_one[...] = normed
        u = dot(normed.astype(LOW), wup[...]) + b_up[...]
        hid = (u * (0.5 * (1.0 + lax.erf(u * root_half)))).astype(LOW)
        down_far[rs, :] = dot(hid, wdown[:, far_cols]).astype(LOW)
        down_copy(r).start()
        pre_two[rs, :] = normed_one[:, own_cols] + dot(hid, wdown[:, own_cols])

    first_lane = lax.broadcasted_iota(jnp.int32, (1, LANES), 1) < 1
    stats_copy = x_copy(stats, stats_got, x_base2 + 2 + 2 * tiles)

    def stat_tile(r):
        rs = row_tile(r)
        down_copy(r).wait_recv()
        x = pre_two[rs, :] + down_got[rs, :].astype(WIDE)
        pre_two[rs, :] = x
        mean = jnp.mean(x, axis=-1, keepdims=True)
        dev = x - mean
        var = jnp.mean(dev * dev, axis=-1, keepdims=True)
        both = jnp.where(first_lane, mean, var)
        stats[r] = jnp.transpose(both)[:8, :]

    def result_tile(r, c):
        rs = row_tile(r)
        x = pre_two[rs, :]
        fill = jnp.zeros((LANES - 8, tile), WIDE)
        one = jnp.transpose(jnp.concatenate([stats[r], fill], axis=0))
        two = jnp.transpose(jnp.concatenate([stats_got[r], fill], axis=0))
        mean = 0.5 * (one[:, :1] + two[:, :1])
        gap = 0.5 * (one[:, :1] - two[:, :1])
        var = 0.5 * (one[:, 1:2] + two[:, 1:2]) + gap * gap
        down_copy(r).wait_send()
        down_far[rs, :] = ((x - mean) * lax.rsqrt(var + norm_eps) * vecs[2:3, own_cols]
                         + vecs[3:4, own_cols]).astype(LOW)
        return c

    result_out = pltpu.make_async_copy(down_far, result, lsem.at[2])

    def write_result():
        stats_copy.wait_recv()
        lax.fori_loop(0, tiles, result_tile, 0)
        result_out.start()

    x_slots = x_base2 + 3 + 2 * tiles
    steps = {"down": down_grad, "in": input_grad, "up": up_grad, "norm": first_norm, "attend": attend_more,
             "mb": lambda p: masked_backward(p, 0), "out": out_grad, "qkv": qkv_grad, "gout": grad_out.start,
             "stats": stats_copy.start, "result": write_result, "small": small_step, "ctx": ctx_wait}
    looped = {"far": far_tile, "near": near_tile, "grad": grad_tile, "layer": layer_tile, "stat": stat_tile}
    for name, *at in PLAN:
        if name in ring:
            ring[name].advance(at[0])
        elif name in looped:
            lax.fori_loop(at[0], at[1], lambda r, c, name=name: looped[name](r) or c, 0)
        else:
            steps[name](*at)
    for k in range(min(len(bits), 4), len(bits)):
        small_step(k)

    for r in range(tiles):
        tok_copy(r).wait_send()
    grad_out.wait()
    result_out.wait()
    small_write.wait()
    for i in range(attend_units):
        ctx_copy(i).wait_send()
    for p in range(pairs):
        ctxc_copy(p).wait_send()
    for cp in (part_copy, back_copy, stats_copy):
        cp.wait_send()
    for k in range(len(bits)):
        small_copy(k).wait_send()
    for one in ring.values():
        one.finish()


def build(n, tokens, wqkv, wout, gain_one, shift_one, wup, b_up, wdown, gain_two, shift_two, perm, index,
          count, cot):
    rows, own = tokens.shape
    width = wout.shape[0]
    local = wqkv.shape[2]
    pairs = local // LANES
    heads = local // HEAD_DIM
    slots = index.shape[1]
    ff = wup.shape[1]
    block_len = rows // 2
    tile = 256
    steps = n.bit_length() - 1
    bits = [1 << k for k in range(steps)]
    depth = min(4, steps)
    units = 1 << depth
    halving, extra = bits[:depth], bits[depth:]

    vm = pltpu.VMEM
    groups = {"D": (ff, width), "U": (width, ff), "O": (local, width), "Q": (width, 3 * local)}
    shapes = {g: (CHUNKS[g] * units, r // (CHUNKS[g] * units), c) for g, (r, c) in groups.items()}
    names = [(g, k) for g in groups for k in range(CHUNKS[g])]
    dma = pltpu.SemaphoreType.DMA

    def ring_scratch(g):
        _, r, c = shapes[g]
        sizes = [units >> (k + 1) for k in range(depth)]
        return {
            "recv": [vm((s, r, c), LOW) for s in sizes],
            "send": [vm((s, r, c), LOW) for s in sizes[1:]],
            "keep": [vm((s, r, c), WIDE) for s in sizes[1:]],
            "xsend": vm((1, r, c) if extra else (1, 8, LANES), LOW),
            "xrecv": vm((len(extra), r, c) if extra else (1, 8, LANES), LOW),
            "sems": (dma((2 * depth + len(extra),)), dma((2 * depth + len(extra),)), dma(())),
        }

    f = [vm(shapes[g], LOW) for g in groups]
    x_slots = 3 * (rows // tile) + 3 * pairs + 3
    scratch = [
        vm((width, 3 * local), LOW), vm(wout.shape, LOW), vm(wup.shape, LOW), vm(wdown.shape, LOW), dma((6,)),
        vm((8, ff), WIDE),
        vm((rows, width), LOW), vm((3 * pairs, rows, LANES), LOW), vm((rows, slots), LOW), vm((slots, rows), LOW),
        vm((slots, LANES), WIDE), vm((slots, width), LOW), vm((pairs, slots, LANES), LOW),
        vm((heads, slots, block_len), WIDE), vm((2 * pairs, slots, LANES), LOW), vm((slots, width), WIDE),
        vm((slots, LANES), WIDE), vm((slots, width), WIDE), vm((slots, width), LOW), vm((slots, ff), WIDE),
        vm((slots, ff), LOW), vm((slots, width), LOW), vm((slots, width), LOW), vm((slots, width), LOW),
        vm((slots, width), WIDE), vm((slots, ff), LOW), vm((slots, width), LOW), vm((slots, width), LOW),
        vm((slots, width), LOW), vm((pairs, slots, LANES), LOW),
        vm((pairs, slots, LANES), LOW), vm((3 * pairs, rows, LANES), LOW), vm((rows, own), LOW),
        vm((rows, own), LOW), vm((rows, own), WIDE),
        vm((2 * pairs, rows, LANES), LOW), vm((rows, own), WIDE), vm((rows, own), LOW),
        vm((rows, own), LOW), vm((rows // tile, 8, tile), WIDE), vm((rows // tile, 8, tile), WIDE),
        *f, vm((8 * steps, ff), WIDE), vm((8 * steps, ff), WIDE), vm((8, ff), WIDE),
        dma((x_slots + steps,)), dma((x_slots + steps,)), dma((4,)),
    ]
    plain = len(scratch)
    ring_specs = [ring_scratch(g) for g, _ in names]
    flat, tree = jax.tree.flatten(ring_specs, is_leaf=lambda x: not isinstance(x, (dict, list, tuple)))
    n_in, n_out = 14, 7

    def run(*refs):
        head_refs = refs[:n_in + n_out + plain]
        rings = jax.tree.unflatten(tree, refs[n_in + n_out + plain:])
        firsts = head_refs[-(len(groups) + 6):-6]
        outs = refs[n_in + 2:n_in + 2 + len(groups)]
        full = {}
        for (g, k), ring in zip(names, rings):
            i = list(groups).index(g)
            part = pl.ds(k * units, units)
            full["%s%d" % (g, k)] = dict(order=[halving[j] for j in ORDERS[g][k] if j < depth], extra=extra,
                                         first=firsts[i].at[part], out=outs[i].at[part], **ring)
        kernel(n, (*head_refs, full))

    hbm = pl.BlockSpec(memory_space=pl.ANY)
    v = pl.BlockSpec(memory_space=pltpu.VMEM)
    shape = jax.ShapeDtypeStruct
    return pl.pallas_call(
        run,
        out_shape=(shape((rows, own), LOW), shape((rows, own), LOW),
                   *(shape(shapes[g], LOW) for g in groups), shape((8, ff), WIDE)),
        in_specs=[hbm, hbm, hbm, hbm, hbm, v, v, v, v, v, v, v, v, v],
        out_specs=(hbm,) * 7,
        scratch_shapes=scratch + flat,
        compiler_params=pltpu.CompilerParams(
            collective_id=0, has_side_effects=True, vmem_limit_bytes=VMEM_BYTES),
        name="layer",
    )(tokens, wqkv, wout, wup, wdown, gain_one, shift_one, gain_two, shift_two, b_up, perm, count, index, cot)


def finish(refs):
    (f_down, f_up, f_out, f_qkv, small, res_in, tok_in,
     down, up, out, qkv, gain_one, shift_one, bias, gain_two, shift_two, res, tok,
     b_down, b_up, b_out, b_qkv, w_down, w_up, w_out, w_qkv, b_res, b_tok, b_small, v_one, v_two, v_bias, v_three,
     v_four, isem, osem) = refs
    width = gain_one.shape[0]
    local = qkv.shape[2]
    reads, writes = [], []

    def read(src, dst):
        cp = pltpu.make_async_copy(src, dst, isem.at[len(reads)])
        cp.start()
        reads.append(cp)
        return cp

    def write(src, dst):
        cp = pltpu.make_async_copy(src, dst, osem.at[len(writes)])
        cp.start()
        writes.append(cp)

    parts = 4
    jobs = []
    for src, low, wide, dst in ((f_down, b_down, w_down, down), (f_up, b_up, w_up, up),
                                (f_out, b_out, w_out, out), (f_qkv, b_qkv, w_qkv, qkv)):
        step = src.shape[0] // parts if src.shape[0] % parts == 0 else src.shape[0]
        for u in range(0, src.shape[0], step):
            jobs.append((read(src.at[pl.ds(u, step)], low.at[pl.ds(u, step)]), u, step, low, wide, dst))
    pass_on = [(read(a, b), b, c) for a, b, c in ((res_in, b_res, res), (tok_in, b_tok, tok))]
    small_read = read(small, b_small)
    for cp, u, step, low, wide, dst in jobs:
        cp.wait()
        r = low.shape[1]

        def unit(j, c, u=u, low=low, wide=wide, r=r, dst=dst):
            v = low[u + j].astype(WIDE)
            rows = pl.ds(pl.multiple_of((u + j) * r, r), r)
            if dst is qkv:
                for k in range(3):
                    wide[k, rows, :] = v[:, k * local:(k + 1) * local]
            else:
                wide[rows, :] = v
            return c

        lax.fori_loop(0, step, unit, 0)
        rows = pl.ds(u * r, step * r)
        if dst is qkv:
            write(wide.at[:, rows, :], dst.at[:, rows, :])
        else:
            write(wide.at[rows, :], dst.at[rows, :])
    for cp, src, dst in pass_on:
        cp.wait()
        write(src, dst)
    small_read.wait()
    for row, at, vec, dst in ((1, 0, v_one, gain_one), (1, width, v_two, shift_one), (0, 0, v_bias, bias),
                              (2, 0, v_three, gain_two), (2, width, v_four, shift_two)):
        size = vec.shape[0]
        vec[...] = b_small[row:row + 1, at:at + size].reshape(size)
        write(vec, dst)
    for cp in writes:
        cp.wait()


def widen(g_down, g_up, g_out, g_qkv, small, result, grad_tokens):
    units, r_qkv, three = g_qkv.shape
    local, width, ff = three // 3, g_down.shape[2], g_up.shape[2]
    shape = jax.ShapeDtypeStruct
    hbm = pl.BlockSpec(memory_space=pl.ANY)
    wide = [(ff, width), (width, ff), (local, width), (3, width, local)]
    low = [g.shape for g in (g_down, g_up, g_out, g_qkv)]
    acts = [result.shape, grad_tokens.shape]
    return pl.pallas_call(
        lambda *refs: finish(refs),
        out_shape=(*(shape(x, WIDE) for x in wide), shape((width,), WIDE), shape((width,), WIDE),
                   shape((ff,), WIDE), shape((width,), WIDE), shape((width,), WIDE),
                   *(shape(x, LOW) for x in acts)),
        in_specs=[hbm] * 7,
        out_specs=(hbm,) * 11,
        scratch_shapes=[*(pltpu.VMEM(x, LOW) for x in low), *(pltpu.VMEM(x, WIDE) for x in wide),
                        *(pltpu.VMEM(x, LOW) for x in acts), pltpu.VMEM(small.shape, WIDE),
                        *(pltpu.VMEM(x, WIDE) for x in ((width,), (width,), (ff,), (width,), (width,))),
                        pltpu.SemaphoreType.DMA((24,)), pltpu.SemaphoreType.DMA((24,))],
        compiler_params=pltpu.CompilerParams(vmem_limit_bytes=VMEM_BYTES),
        name="widen",
    )(g_down, g_up, g_out, g_qkv, small, result, grad_tokens)


def body(n, tokens, w_qkv, w_out, gain_one, attention_norm_bias, w_up, b_up, w_down, gain_two, shift_two,
         block_perm, mask_index, mask_count, cotangent):
    result, grad_tokens, g_down, g_up, g_out, g_qkv, small = build(
        n, tokens, w_qkv.transpose(1, 0, 2), w_out, gain_one, attention_norm_bias, w_up, b_up, w_down, gain_two,
        shift_two, block_perm.T, mask_index, mask_count.reshape(1, 1), cotangent[0])
    (g_down, g_up, g_out, g_qkv, g_gain_one, g_shift_one, g_bias, g_gain_two, g_shift_two, result,
     grad_tokens) = widen(g_down, g_up, g_out, g_qkv, small, result, grad_tokens)
    return (result, grad_tokens, g_qkv.transpose(1, 0, 2), g_out, g_gain_one, g_shift_one, g_up, g_bias, g_down,
            g_gain_two, g_shift_two)


def solution(mesh):
    return jax.shard_map(
        functools.partial(body, mesh.shape["batch"]),
        mesh=mesh,
        in_specs=(P("batch", "head"), P(None, None, "head"), P(), P(), P(), P(None, "head"), P("head"),
                  P("head", None), P(), P(), P("head", None), P("batch", None), P("batch"),
                  P("batch", None, None)),
        out_specs=(P("batch", "head"), P("batch", "head"), P(None, None, "head"), P("head", None), P(), P(),
                   P(None, "head"), P("head"), P("head", None), P(), P()),
        check_vma=False,
    )
```

```python
import functools

import jax
import jax.numpy as jnp
from jax import lax
from jax.experimental import pallas as pl
from jax.experimental.pallas import tpu as pltpu
from jax.sharding import PartitionSpec as P

HEAD_DIM = 64
norm_eps = 1e-06
root_half = 0.7071067811865476
inv_root_two_pi = 0.3989422804014327
log2_e = 1.4426950408889634
LOW = jnp.bfloat16
WIDE = jnp.float32
LANES = 128
MESH = pl.DeviceIdType.MESH
VMEM_BYTES = 67043328
CUTS = (2, 4)
CHUNKS = {"D": 3, "U": 3, "O": 1, "Q": 2}
ORDERS = {"D": [[0, 2, 3, 1], [0, 1, 2, 3], [0, 1, 2, 3]],
          "U": [[0, 2, 1, 3], [0, 1, 2, 3], [0, 1, 2, 3]],
          "O": [[0, 1, 2, 3]],
          "Q": [[0, 1, 2, 3], [0, 1, 2, 3]]}
PLAN = (
    ("down", 0), ("in",), ("D0", 0), ("down", 1), ("down", 2), ("up", 0), ("up", 1), ("D1", 0), ("up", 2),
    ("D2", 0), ("U0", 0), ("U1", 0), ("attend",), ("U2", 0), ("D0", 1), ("ctx", 0), ("layer", 1, 2), ("D1", 1),
    ("U0", 1), ("norm",), ("D2", 1), ("mb", 0), ("D0", 2), ("D1", 2), ("mb", 1), ("U1", 1), ("D2", 2),
    ("small", 0), ("mb", 2), ("D1", 3), ("out",), ("U2", 1), ("U1", 2), ("qkv", 0), ("O0", 0), ("U0", 2),
    ("D2", 3), ("small", 1), ("qkv", 1), ("Q0", 0), ("D1", 4), ("U2", 2), ("far", 0, 2), ("Q1", 0), ("U1", 3),
    ("O0", 1), ("small", 2), ("far", 2, 3), ("U0", 3), ("ctx", 1), ("layer", 2, 3), ("D1", 5), ("D2", 4),
    ("Q0", 1), ("D0", 3), ("U2", 3), ("small", 3), ("far", 3, 4), ("O0", 2), ("layer", 0, 1), ("U1", 4),
    ("Q1", 1), ("D2", 5), ("layer", 3, 4), ("Q0", 2), ("D1", 6), ("U2", 4), ("O0", 3), ("near", 0, 1),
    ("U1", 5), ("near", 1, 2), ("D1", 7), ("near", 2, 4), ("Q1", 2), ("D2", 6), ("grad", 0, 3), ("stat", 1, 2),
    ("Q0", 3), ("stat", 2, 3), ("D2", 7), ("grad", 3, 4), ("gout",), ("U2", 5), ("O0", 4), ("U1", 6), ("Q1", 3),
    ("U0", 4), ("U1", 7), ("stat", 0, 1), ("Q0", 4), ("D0", 4), ("O0", 5), ("U2", 6), ("Q1", 4), ("U2", 7),
    ("stat", 3, 4), ("U0", 5), ("Q0", 5), ("stats",), ("result",), ("O0", 6), ("D0", 5), ("Q1", 5), ("O0", 7),
    ("Q0", 6), ("U0", 6), ("Q0", 7), ("U0", 7), ("Q1", 6), ("D0", 6), ("Q1", 7), ("D0", 7),
)


def dot(a, b):
    return lax.dot_general(a, b, (((1,), (0,)), ((), ())), preferred_element_type=WIDE)


def dot_nt(a, b):
    return lax.dot_general(a, b, (((1,), (1,)), ((), ())), preferred_element_type=WIDE)


def dot_tn(a, b):
    return lax.dot_general(a, b, (((0,), (0,)), ((), ())), preferred_element_type=WIDE)


def normalize(values):
    centered = values - jnp.mean(values, axis=-1, keepdims=True)
    inverse = lax.rsqrt(jnp.mean(centered * centered, axis=-1, keepdims=True) + norm_eps)
    return centered * inverse, inverse


def norm_backward(upstream, normal, inverse, gain_vec):
    scaled = upstream * gain_vec
    return inverse * (
        scaled
        - jnp.mean(scaled, axis=-1, keepdims=True)
        - normal * jnp.mean(scaled * normal, axis=-1, keepdims=True)
    )


def col_sum(x):
    return jnp.sum(x, axis=0, keepdims=True)


def cat(parts):
    return jnp.concatenate(parts, axis=1)


class Ring:
    def __init__(self, order, extra, first, out, recv, send, keep, xsend, xrecv, sems, peer, bit_of):
        self.order, self.extra = order, extra
        self.first, self.out = first, out
        self.recv, self.send, self.keep = recv, send, keep
        self.xsend, self.xrecv = xsend, xrecv
        self.ssem, self.rsem, self.lsem = sems
        self.peer = peer
        self.mine = [bit_of(b) for b in order]
        units = first.shape[0]
        self.sizes = [units >> (k + 1) for k in range(len(order))]
        self.base = []
        base = 0
        for k in range(len(order)):
            base = base + self.mine[k] * self.sizes[k]
            self.base.append(base)

    def _copy(self, src, dst, slot, bit):
        return pltpu.make_async_remote_copy(
            src_ref=src, dst_ref=dst, send_sem=self.ssem.at[slot], recv_sem=self.rsem.at[slot],
            device_id=self.peer(bit), device_id_type=MESH)

    def _rs(self, k):
        size = self.sizes[k]
        if k == 0:
            src = self.first.at[pl.ds((1 - self.mine[0]) * size, size)]
        else:
            src = self.send[k - 1]
        return self._copy(src, self.recv[k], k, self.order[k])

    def _x(self, j):
        return self._copy(self.xsend, self.xrecv.at[pl.ds(j, 1)], len(self.order) + j, self.extra[j])

    def _ag(self, k):
        slot = len(self.order) + len(self.extra) + k
        part = self.first.at[pl.ds(self.base[k], self.sizes[k])]
        return self._copy(part, part, slot, self.order[k])

    def _write(self):
        return pltpu.make_async_copy(self.first, self.out, self.lsem)

    def start(self):
        self._rs(0).start()

    def _value(self, k, u):
        got = self.recv[k][u].astype(WIDE)
        if k == 0:
            return self.first[self.mine[0] * self.sizes[0] + u].astype(WIDE) + got
        return self.keep[k - 1][u] + got

    def reduce(self, k):
        self._rs(k).wait_recv()
        if k == 0:
            self._rs(0).wait_send()
        if k + 1 < len(self.order):
            half = self.sizes[k + 1]
            mine = self.mine[k + 1]

            def out_part(j, c):
                self.send[k][j] = self._value(k, (1 - mine) * half + j).astype(LOW)
                return c

            lax.fori_loop(0, half, out_part, 0)
            self._rs(k + 1).start()

            def own_part(j, c):
                self.keep[k][j] = self._value(k, mine * half + j)
                return c

            lax.fori_loop(0, half, own_part, 0)
        else:
            total = self._value(k, 0)
            for j in range(len(self.extra)):
                self.xsend[0] = total.astype(LOW)
                self._x(j).start()
                self._x(j).wait()
                total = self.xsend[0].astype(WIDE) + self.xrecv[j].astype(WIDE)
            self.first[self.base[k]] = total.astype(LOW)
            self._ag(k).start()

    def gather(self, k):
        self._ag(k + 1).wait_recv()
        if k >= 0:
            self._ag(k).start()
        else:
            self._write().start()

    def advance(self, stage):
        depth = len(self.order)
        if stage < depth:
            self.reduce(stage)
        else:
            self.gather(2 * depth - 2 - stage)

    def finish(self):
        for k in range(len(self.order)):
            if k > 0:
                self._rs(k).wait_send()
            self._ag(k).wait_send()
        self._write().wait()


def kernel(n, refs):
    (tokens, wqkv_hbm, wout_hbm, wup_hbm, wdown_hbm, *vectors,
     perm, count, index, cot,
     result, grad_tokens, o_down, o_up, o_out, o_qkv, small_out,
     wqkv, wout, wup, wdown, wsem, vecs,
     tok, qkv, sel_t, sel, blk, tokc, qc, probs, ctxc, normal_one, inverse_one, normed_one, low_one, slope,
     hidden, part, part_got, gb, gtwo, gin, back, back_got, gattn, gctx, dqc, dall, far, far_got, near,
     ctx, pre_two, down_far, down_got, stats, stats_got,
     f_down, f_up, f_out, f_qkv, small, small_got, small_sum,
     xs_send, xs_recv, lsem, rings) = refs
    rows, own = tokens.shape
    width = wout.shape[0]
    local = wqkv.shape[1] // 3
    pairs = local // LANES
    slots = index.shape[1]
    ff = wup.shape[1]
    block_len = rows // 2
    tile = 256
    tiles = rows // tile
    scale = HEAD_DIM ** (-0.5)
    b = lax.axis_index("batch")
    h = lax.axis_index("head")
    other = 1 - h
    bits = [1 << k for k in range(n.bit_length() - 1)]

    def bit_of(bit):
        return lax.rem(lax.div(b, bit), 2)

    def peer(bit):
        return (b + bit - 2 * bit * bit_of(bit), h)

    x_peer = (b, other)

    def x_copy(src, dst, slot):
        return pltpu.make_async_remote_copy(
            src_ref=src, dst_ref=dst, send_sem=xs_send.at[slot], recv_sem=xs_recv.at[slot],
            device_id=x_peer, device_id_type=MESH)

    loads = [pltpu.make_async_copy(s, d, wsem.at[i]) for i, (s, d) in enumerate(
        [(wqkv_hbm.at[j], wqkv.at[:, pl.ds(j * local, local)]) for j in range(3)]
        + [(wout_hbm, wout), (wup_hbm, wup), (wdown_hbm, wdown)])]
    for cp in loads:
        cp.start()
    barrier = pltpu.get_barrier_semaphore()
    pl.semaphore_signal(barrier, inc=1, device_id=x_peer, device_id_type=MESH)
    for bit in bits:
        pl.semaphore_signal(barrier, inc=1, device_id=peer(bit), device_id_type=MESH)
    pl.semaphore_wait(barrier, 1 + len(bits))

    own_cols = pl.ds(pl.multiple_of(h * own, LANES), own)
    far_cols = pl.ds(pl.multiple_of(other * own, LANES), own)

    def row_tile(r):
        return pl.ds(pl.multiple_of(r * tile, tile), tile)

    def tok_copy(r):
        return x_copy(tokens.at[row_tile(r)], tok.at[row_tile(r), own_cols], r)

    for r in range(tiles):
        tok_copy(r).start()
    own_tok = pltpu.make_async_copy(tokens, tok.at[:, own_cols], lsem.at[0])
    own_tok.start()

    for i, vector in enumerate(vectors):
        vecs[i:i + 1, :vector.shape[0]] = vector[...].reshape(1, -1)
    gain_one, shift_one, gain_two, shift_two = (vecs.at[i:i + 1, :width] for i in range(4))
    b_up = vecs.at[4:5, :]

    lane_slot = lax.broadcasted_iota(jnp.int32, (1, slots), 1)
    idx = jnp.where(lane_slot < count[...], index[...], -1)
    picked = jnp.where(lax.broadcasted_iota(jnp.int32, (rows, slots), 0) == idx, 1.0, 0.0)
    sel_t[...] = picked.astype(LOW)
    picked = jnp.transpose(picked)
    sel[...] = picked.astype(LOW)
    blk[...] = jnp.broadcast_to(jnp.sum(picked[:, block_len:], axis=1, keepdims=True), blk.shape)
    own_tok.wait()
    for cp in loads[:3]:
        cp.wait()

    def qkv_tile(r, c):
        tok_copy(r).wait_recv()
        out = dot(tok[row_tile(r), :], wqkv[...]).astype(LOW)
        for j in range(3 * pairs):
            qkv[j, row_tile(r), :] = out[:, j * LANES:(j + 1) * LANES]
        return c

    lax.fori_loop(0, tiles, qkv_tile, 0)

    low_lane = lax.broadcasted_iota(jnp.int32, (1, LANES), 1) < HEAD_DIM
    def keep_head(x, e):
        return jnp.where(low_lane, x, 0.0).astype(LOW) if e == 0 else jnp.where(low_lane, 0.0, x).astype(LOW)

    order = perm[...].astype(WIDE)
    head_lane = lax.broadcasted_iota(jnp.int32, order.shape, 1)

    def blocks_of(head):
        return jnp.sum(jnp.where(head_lane == head, order, 0.0), axis=1, keepdims=True)

    def second(head):
        pair = blocks_of(head)
        return (pair[:1] + blk[:, :1] * (pair[1:] - pair[:1])) > 0.5

    def masked_attention(p, c):
        q2 = dot(sel[...], qkv[p]).astype(LOW)
        qc[p] = q2
        halves = []
        for e in range(2):
            head = 2 * p + e
            late = second(head)
            qm = keep_head(q2.astype(WIDE), e)
            s = jnp.where(late, dot_nt(qm, qkv[pairs + p, block_len:, :]),
                          dot_nt(qm, qkv[pairs + p, :block_len, :])) * (scale * log2_e)
            ex = jnp.exp2(s - jnp.max(s, axis=-1, keepdims=True))
            pr = ex * (1.0 / jnp.sum(ex, axis=-1, keepdims=True))
            probs[head] = pr
            pr = pr.astype(LOW)
            halves.append(jnp.where(late, dot(pr, qkv[2 * pairs + p, block_len:, :]),
                                    dot(pr, qkv[2 * pairs + p, :block_len, :])))
        ctxc[h * pairs + p] = jnp.where(low_lane, halves[0], halves[1]).astype(LOW)
        ctxc_copy(p).start()
        return c

    def ctxc_copy(p):
        mine_c = ctxc.at[pl.ds(h * pairs + p, 1)]
        return x_copy(mine_c, mine_c, tiles + p)

    lax.fori_loop(0, pairs, masked_attention, 0)

    def attend(i, c):
        p = lax.rem(i, pairs)
        q_block = lax.div(i, pairs)
        q_rows = pl.ds(pl.multiple_of(q_block * block_len, block_len), block_len)
        q2 = qkv[p, q_rows, :].astype(WIDE)
        even, odd = blocks_of(2 * p), blocks_of(2 * p + 1)
        late = jnp.where(low_lane, jnp.where(q_block == 0, even[:1], even[1:]),
                         jnp.where(q_block == 0, odd[:1], odd[1:])) > 0.5

        def chosen(j):
            return jnp.where(late, qkv[j, block_len:, :].astype(WIDE), qkv[j, :block_len, :].astype(WIDE)).astype(LOW)

        k2, v2 = chosen(pairs + p), chosen(2 * pairs + p)
        halves = []
        for e in range(2):
            s = dot_nt(keep_head(q2, e), k2) * (scale * log2_e)
            ex = jnp.exp2(s - jnp.max(s, axis=-1, keepdims=True))
            inv = 1.0 / jnp.sum(ex, axis=-1, keepdims=True)
            halves.append(dot(ex.astype(LOW), v2) * inv)
        ctx[h * pairs + p, q_rows, :] = jnp.where(low_lane, halves[0], halves[1]).astype(LOW)
        ctx_copy(i).start()
        return c

    x_base = tiles + pairs

    def ctx_copy(i):
        q_rows = pl.ds(pl.multiple_of(lax.div(i, pairs) * block_len, block_len), block_len)
        part_ref = ctx.at[pl.ds(h * pairs + lax.rem(i, pairs), 1), q_rows]
        return x_copy(part_ref, part_ref, x_base + i)

    tokc[...] = dot(sel[...], tok[...]).astype(LOW)
    attend_units = 2 * pairs
    x_base2 = x_base + attend_units
    lax.fori_loop(0, CUTS[0], attend, 0)

    for p in range(pairs):
        ctxc_copy(p).wait_recv()
    for cp in loads[3:]:
        cp.wait()
    pre = tokc[...].astype(WIDE) + dot(cat([ctxc[j] for j in range(2 * pairs)]), wout[...])
    nrm_c, inv_c = normalize(pre)
    normal_one[...] = nrm_c
    inverse_one[...] = jnp.broadcast_to(inv_c, inverse_one.shape)
    nrm_c = nrm_c * gain_one[...] + shift_one[...]
    normed_one[...] = nrm_c
    low_one[...] = nrm_c.astype(LOW)
    ff_tile = 384

    def up_tile(i, c):
        cols = pl.ds(pl.multiple_of(i * ff_tile, ff_tile), ff_tile)
        u = dot(low_one[...], wup[:, cols]) + vecs[4:5, cols]
        cdf = 0.5 * (1.0 + lax.erf(u * root_half))
        hidden[:, cols] = (u * cdf).astype(LOW)
        slope[:, cols] = cdf + u * inv_root_two_pi * jnp.exp(-0.5 * u * u)
        return c

    lax.fori_loop(0, ff // ff_tile, up_tile, 0)
    part[...] = dot(hidden[...], wdown[...]).astype(LOW)
    part_copy = x_copy(part, part_got, x_base2)
    part_copy.start()
    lax.fori_loop(CUTS[0], CUTS[1], attend, 0)
    part_copy.wait_recv()

    normal_two, inv_two = normalize(normed_one[...] + (part[...].astype(WIDE) + part_got[...].astype(WIDE)))
    alive = lax.broadcasted_iota(jnp.int32, (slots, 1), 0) < count[...]
    up = jnp.where(alive, cot[...].astype(WIDE), 0.0)
    g2 = norm_backward(up, normal_two, inv_two, gain_two[...])
    gtwo[...] = g2
    gb[...] = g2.astype(LOW)
    small[2:3, :] = cat([col_sum(up * normal_two), col_sum(up)])

    def put(first, unit, value):
        r = first.shape[1]
        for j in range(value.shape[0] // r):
            first[unit + j] = value[j * r:(j + 1) * r, :]

    ring = {name: Ring(peer=peer, bit_of=bit_of, **r) for name, r in rings.items()}

    def by_tiles(group, k, first, grad):
        units = first.shape[0] // CHUNKS[group]
        size = units * first.shape[1]
        step = 256 if size % 256 == 0 else 384

        def one_tile(i, c):
            at = k * size + i * step
            put(first, k * units + i * (step * units // size), grad(pl.ds(pl.multiple_of(at, LANES), step)))
            return c

        lax.fori_loop(0, size // step, one_tile, 0)
        ring["%s%d" % (group, k)].start()

    def down_grad(k):
        by_tiles("D", k, f_down, lambda cols: dot_tn(hidden[:, cols], gb[...]).astype(LOW))

    def up_grad(k):
        by_tiles("U", k, f_up, lambda cols: dot_tn(low_one[:, cols], gin[...]).astype(LOW))

    def in_tile(i, c):
        cols = pl.ds(pl.multiple_of(i * ff_tile, ff_tile), ff_tile)
        g = (dot_nt(gb[...], wdown[cols, :]) * slope[:, cols]).astype(LOW)
        gin[:, cols] = g
        small[0:1, cols] = col_sum(g.astype(WIDE))
        return c

    back_copy = x_copy(back, back_got, x_base2 + 1)

    def input_grad():
        lax.fori_loop(0, ff // ff_tile, in_tile, 0)
        back[...] = dot_nt(gin[...], wup[...]).astype(LOW)
        back_copy.start()

    def attend_more():
        lax.fori_loop(CUTS[1], attend_units, attend, 0)

    own_rows = pl.ds(pl.multiple_of(h * local, LANES), local)

    def first_norm():
        back_copy.wait_recv()
        gn = gtwo[...] + (back[...].astype(WIDE) + back_got[...].astype(WIDE))
        small[1:2, :] = cat([col_sum(gn * normal_one[...]), col_sum(gn)])
        g1 = norm_backward(gn, normal_one[...], inverse_one[:, :1], gain_one[...])
        gtwo[...] = g1
        gattn[...] = g1.astype(LOW)
        gc = dot_nt(gattn[...], wout[own_rows, :]).astype(LOW)
        for p in range(pairs):
            gctx[p] = gc[:, p * LANES:(p + 1) * LANES]
        small[3:8, :] = jnp.zeros((5, small.shape[1]), WIDE)
        small_copy(0).start()

    def masked_backward(p, c):
        q2 = qc[p].astype(WIDE)
        g2 = gctx[p].astype(WIDE)
        k2 = cat([qkv[pairs + p, :block_len, :], qkv[pairs + p, block_len:, :]])
        dk = jnp.zeros((block_len, 2 * LANES), WIDE)
        dv = jnp.zeros((block_len, 2 * LANES), WIDE)
        dq = []
        for e in range(2):
            head = 2 * p + e
            late = second(head)
            gm = keep_head(g2, e)
            dp = jnp.where(late, dot_nt(gm, qkv[2 * pairs + p, block_len:, :]),
                           dot_nt(gm, qkv[2 * pairs + p, :block_len, :]))
            pr = probs[head]
            t = dp * pr
            ds = (t - pr * jnp.sum(t, axis=-1, keepdims=True)).astype(LOW)
            qm = keep_head(q2, e).astype(WIDE)
            gm = gm.astype(WIDE)
            dk = dk + dot_tn(ds, cat([jnp.where(late, 0.0, qm), jnp.where(late, qm, 0.0)]).astype(LOW))
            dv = dv + dot_tn(pr.astype(LOW),
                             cat([jnp.where(late, 0.0, gm), jnp.where(late, gm, 0.0)]).astype(LOW))
            both = dot(ds, k2)
            dq.append(jnp.where(late, both[:, LANES:], both[:, :LANES]))
        d = (jnp.where(low_lane, dq[0], dq[1]) * scale).astype(LOW)
        dqc[p] = d
        dall[p] = dot(sel_t[...], d).astype(LOW)
        dk = (dk * scale).astype(LOW)
        dv = dv.astype(LOW)
        dall[pairs + p, :block_len, :] = dk[:, :LANES]
        dall[pairs + p, block_len:, :] = dk[:, LANES:]
        dall[2 * pairs + p, :block_len, :] = dv[:, :LANES]
        dall[2 * pairs + p, block_len:, :] = dv[:, LANES:]
        return c

    def small_copy(k):
        return pltpu.make_async_remote_copy(
            src_ref=small.at[pl.ds(8 * k, 8)], dst_ref=small_got.at[pl.ds(8 * k, 8)],
            send_sem=xs_send.at[x_slots + k], recv_sem=xs_recv.at[x_slots + k],
            device_id=peer(bits[k]), device_id_type=MESH)

    small_write = pltpu.make_async_copy(small_sum, small_out, lsem.at[3])

    def small_step(k):
        small_copy(k).wait_recv()
        total = small[8 * k:8 * k + 8, :] + small_got[8 * k:8 * k + 8, :]
        if k + 1 < len(bits):
            small[8 * k + 8:8 * k + 16, :] = total
            small_copy(k + 1).start()
        else:
            small_sum[...] = total
            small_write.start()

    def out_grad():
        put(f_out, 0, dot_tn(cat([ctxc[h * pairs + p] for p in range(pairs)]), gattn[...]).astype(LOW))
        ring["O0"].start()

    def qkv_grad(k):
        def grad(cols):
            gq = dot_tn(tokc[:, cols], cat([dqc[p] for p in range(pairs)]))
            gkv = dot_tn(tok[:, cols], cat([dall[pairs + j] for j in range(2 * pairs)]))
            return cat([gq, gkv]).astype(LOW)

        by_tiles("Q", k, f_qkv, grad)

    def far_copy(r):
        return x_copy(far.at[row_tile(r)], far_got.at[row_tile(r)], x_base2 + 2 + r)

    def far_tile(r):
        d = cat([dall[j, row_tile(r), :] for j in range(3 * pairs)])
        far[row_tile(r), :] = dot_nt(d, wqkv[far_cols, :]).astype(LOW)
        far_copy(r).start()

    def near_tile(r):
        mine = gtwo[:, own_cols]
        high = mine.astype(LOW)
        rest = (mine - high.astype(WIDE)).astype(LOW)
        d = cat([dall[j, row_tile(r), :] for j in range(3 * pairs)])
        spread = dot(sel_t[row_tile(r), :], cat([high, rest]))
        near[row_tile(r), :] = dot_nt(d, wqkv[own_cols, :]) + (spread[:, :own] + spread[:, own:])

    def grad_tile(r):
        far_copy(r).wait_recv()
        far_copy(r).wait_send()
        far[row_tile(r), :] = (near[row_tile(r), :] + far_got[row_tile(r), :].astype(WIDE)).astype(LOW)

    grad_out = pltpu.make_async_copy(far, grad_tokens, lsem.at[1])

    def down_copy(r):
        return x_copy(down_far.at[row_tile(r)], down_got.at[row_tile(r)], x_base2 + 2 + tiles + r)

    def ctx_wait(block):
        for i in range(block * pairs, (block + 1) * pairs):
            ctx_copy(i).wait_recv()

    def layer_tile(r):
        rs = row_tile(r)
        pre_r = tok[rs, :].astype(WIDE) + dot(cat([ctx[j, rs, :] for j in range(2 * pairs)]), wout[...])
        normed = normalize(pre_r)[0] * gain_one[...] + shift_one[...]
        normed_one[...] = normed
        u = dot(normed.astype(LOW), wup[...]) + b_up[...]
        hid = (u * (0.5 * (1.0 + lax.erf(u * root_half)))).astype(LOW)
        down_far[rs, :] = dot(hid, wdown[:, far_cols]).astype(LOW)
        down_copy(r).start()
        pre_two[rs, :] = normed_one[:, own_cols] + dot(hid, wdown[:, own_cols])

    first_lane = lax.broadcasted_iota(jnp.int32, (1, LANES), 1) < 1
    stats_copy = x_copy(stats, stats_got, x_base2 + 2 + 2 * tiles)

    def stat_tile(r):
        rs = row_tile(r)
        down_copy(r).wait_recv()
        x = pre_two[rs, :] + down_got[rs, :].astype(WIDE)
        pre_two[rs, :] = x
        mean = jnp.mean(x, axis=-1, keepdims=True)
        dev = x - mean
        var = jnp.mean(dev * dev, axis=-1, keepdims=True)
        both = jnp.where(first_lane, mean, var)
        stats[r] = jnp.transpose(both)[:8, :]

    def result_tile(r, c):
        rs = row_tile(r)
        x = pre_two[rs, :]
        fill = jnp.zeros((LANES - 8, tile), WIDE)
        one = jnp.transpose(jnp.concatenate([stats[r], fill], axis=0))
        two = jnp.transpose(jnp.concatenate([stats_got[r], fill], axis=0))
        mean = 0.5 * (one[:, :1] + two[:, :1])
        gap = 0.5 * (one[:, :1] - two[:, :1])
        var = 0.5 * (one[:, 1:2] + two[:, 1:2]) + gap * gap
        down_copy(r).wait_send()
        down_far[rs, :] = ((x - mean) * lax.rsqrt(var + norm_eps) * vecs[2:3, own_cols]
                         + vecs[3:4, own_cols]).astype(LOW)
        return c

    result_out = pltpu.make_async_copy(down_far, result, lsem.at[2])

    def write_result():
        stats_copy.wait_recv()
        lax.fori_loop(0, tiles, result_tile, 0)
        result_out.start()

    x_slots = x_base2 + 3 + 2 * tiles
    steps = {"down": down_grad, "in": input_grad, "up": up_grad, "norm": first_norm, "attend": attend_more,
             "mb": lambda p: masked_backward(p, 0), "out": out_grad, "qkv": qkv_grad, "gout": grad_out.start,
             "stats": stats_copy.start, "result": write_result, "small": small_step, "ctx": ctx_wait}
    looped = {"far": far_tile, "near": near_tile, "grad": grad_tile, "layer": layer_tile, "stat": stat_tile}
    for name, *at in PLAN:
        if name in ring:
            ring[name].advance(at[0])
        elif name in looped:
            lax.fori_loop(at[0], at[1], lambda r, c, name=name: looped[name](r) or c, 0)
        else:
            steps[name](*at)
    for k in range(min(len(bits), 4), len(bits)):
        small_step(k)

    for r in range(tiles):
        tok_copy(r).wait_send()
    grad_out.wait()
    result_out.wait()
    small_write.wait()
    for i in range(attend_units):
        ctx_copy(i).wait_send()
    for p in range(pairs):
        ctxc_copy(p).wait_send()
    for cp in (part_copy, back_copy, stats_copy):
        cp.wait_send()
    for k in range(len(bits)):
        small_copy(k).wait_send()
    for one in ring.values():
        one.finish()


def build(n, tokens, wqkv, wout, gain_one, shift_one, wup, b_up, wdown, gain_two, shift_two, perm, index,
          count, cot):
    rows, own = tokens.shape
    width = wout.shape[0]
    local = wqkv.shape[2]
    pairs = local // LANES
    heads = local // HEAD_DIM
    slots = index.shape[1]
    ff = wup.shape[1]
    block_len = rows // 2
    tile = 256
    steps = n.bit_length() - 1
    bits = [1 << k for k in range(steps)]
    depth = min(4, steps)
    units = 1 << depth
    halving, extra = bits[:depth], bits[depth:]

    vm = pltpu.VMEM
    groups = {"D": (ff, width), "U": (width, ff), "O": (local, width), "Q": (width, 3 * local)}
    shapes = {g: (CHUNKS[g] * units, r // (CHUNKS[g] * units), c) for g, (r, c) in groups.items()}
    names = [(g, k) for g in groups for k in range(CHUNKS[g])]
    dma = pltpu.SemaphoreType.DMA

    def ring_scratch(g):
        _, r, c = shapes[g]
        sizes = [units >> (k + 1) for k in range(depth)]
        return {
            "recv": [vm((s, r, c), LOW) for s in sizes],
            "send": [vm((s, r, c), LOW) for s in sizes[1:]],
            "keep": [vm((s, r, c), WIDE) for s in sizes[1:]],
            "xsend": vm((1, r, c) if extra else (1, 8, LANES), LOW),
            "xrecv": vm((len(extra), r, c) if extra else (1, 8, LANES), LOW),
            "sems": (dma((2 * depth + len(extra),)), dma((2 * depth + len(extra),)), dma(())),
        }

    f = [vm(shapes[g], LOW) for g in groups]
    x_slots = 3 * (rows // tile) + 3 * pairs + 3
    scratch = [
        vm((width, 3 * local), LOW), vm(wout.shape, LOW), vm(wup.shape, LOW), vm(wdown.shape, LOW), dma((6,)),
        vm((8, ff), WIDE),
        vm((rows, width), LOW), vm((3 * pairs, rows, LANES), LOW), vm((rows, slots), LOW), vm((slots, rows), LOW),
        vm((slots, LANES), WIDE), vm((slots, width), LOW), vm((pairs, slots, LANES), LOW),
        vm((heads, slots, block_len), WIDE), vm((2 * pairs, slots, LANES), LOW), vm((slots, width), WIDE),
        vm((slots, LANES), WIDE), vm((slots, width), WIDE), vm((slots, width), LOW), vm((slots, ff), WIDE),
        vm((slots, ff), LOW), vm((slots, width), LOW), vm((slots, width), LOW), vm((slots, width), LOW),
        vm((slots, width), WIDE), vm((slots, ff), LOW), vm((slots, width), LOW), vm((slots, width), LOW),
        vm((slots, width), LOW), vm((pairs, slots, LANES), LOW),
        vm((pairs, slots, LANES), LOW), vm((3 * pairs, rows, LANES), LOW), vm((rows, own), LOW),
        vm((rows, own), LOW), vm((rows, own), WIDE),
        vm((2 * pairs, rows, LANES), LOW), vm((rows, own), WIDE), vm((rows, own), LOW),
        vm((rows, own), LOW), vm((rows // tile, 8, tile), WIDE), vm((rows // tile, 8, tile), WIDE),
        *f, vm((8 * steps, ff), WIDE), vm((8 * steps, ff), WIDE), vm((8, ff), WIDE),
        dma((x_slots + steps,)), dma((x_slots + steps,)), dma((4,)),
    ]
    plain = len(scratch)
    ring_specs = [ring_scratch(g) for g, _ in names]
    flat, tree = jax.tree.flatten(ring_specs, is_leaf=lambda x: not isinstance(x, (dict, list, tuple)))
    n_in, n_out = 14, 7

    def run(*refs):
        head_refs = refs[:n_in + n_out + plain]
        rings = jax.tree.unflatten(tree, refs[n_in + n_out + plain:])
        firsts = head_refs[-(len(groups) + 6):-6]
        outs = refs[n_in + 2:n_in + 2 + len(groups)]
        full = {}
        for (g, k), ring in zip(names, rings):
            i = list(groups).index(g)
            part = pl.ds(k * units, units)
            full["%s%d" % (g, k)] = dict(order=[halving[j] for j in ORDERS[g][k] if j < depth], extra=extra,
                                         first=firsts[i].at[part], out=outs[i].at[part], **ring)
        kernel(n, (*head_refs, full))

    hbm = pl.BlockSpec(memory_space=pl.ANY)
    v = pl.BlockSpec(memory_space=pltpu.VMEM)
    shape = jax.ShapeDtypeStruct
    return pl.pallas_call(
        run,
        out_shape=(shape((rows, own), LOW), shape((rows, own), LOW),
                   *(shape(shapes[g], LOW) for g in groups), shape((8, ff), WIDE)),
        in_specs=[hbm, hbm, hbm, hbm, hbm, v, v, v, v, v, v, v, v, v],
        out_specs=(hbm,) * 7,
        scratch_shapes=scratch + flat,
        compiler_params=pltpu.CompilerParams(
            collective_id=0, has_side_effects=True, vmem_limit_bytes=VMEM_BYTES),
        name="layer",
    )(tokens, wqkv, wout, wup, wdown, gain_one, shift_one, gain_two, shift_two, b_up, perm, count, index, cot)


def finish(refs):
    (f_down, f_up, f_out, f_qkv, small, res_in, tok_in,
     down, up, out, qkv, gain_one, shift_one, bias, gain_two, shift_two, res, tok,
     b_down, b_up, b_out, b_qkv, w_down, w_up, w_out, w_qkv, b_res, b_tok, b_small, v_one, v_two, v_bias, v_three,
     v_four, isem, osem) = refs
    width = gain_one.shape[0]
    local = qkv.shape[2]
    reads, writes = [], []

    def read(src, dst):
        cp = pltpu.make_async_copy(src, dst, isem.at[len(reads)])
        cp.start()
        reads.append(cp)
        return cp

    def write(src, dst):
        cp = pltpu.make_async_copy(src, dst, osem.at[len(writes)])
        cp.start()
        writes.append(cp)

    parts = 4
    jobs = []
    for src, low, wide, dst in ((f_down, b_down, w_down, down), (f_up, b_up, w_up, up),
                                (f_out, b_out, w_out, out), (f_qkv, b_qkv, w_qkv, qkv)):
        step = src.shape[0] // parts if src.shape[0] % parts == 0 else src.shape[0]
        for u in range(0, src.shape[0], step):
            jobs.append((read(src.at[pl.ds(u, step)], low.at[pl.ds(u, step)]), u, step, low, wide, dst))
    pass_on = [(read(a, b), b, c) for a, b, c in ((res_in, b_res, res), (tok_in, b_tok, tok))]
    small_read = read(small, b_small)
    for cp, u, step, low, wide, dst in jobs:
        cp.wait()
        r = low.shape[1]

        def unit(j, c, u=u, low=low, wide=wide, r=r, dst=dst):
            v = low[u + j].astype(WIDE)
            rows = pl.ds(pl.multiple_of((u + j) * r, r), r)
            if dst is qkv:
                for k in range(3):
                    wide[k, rows, :] = v[:, k * local:(k + 1) * local]
            else:
                wide[rows, :] = v
            return c

        lax.fori_loop(0, step, unit, 0)
        rows = pl.ds(u * r, step * r)
        if dst is qkv:
            write(wide.at[:, rows, :], dst.at[:, rows, :])
        else:
            write(wide.at[rows, :], dst.at[rows, :])
    for cp, src, dst in pass_on:
        cp.wait()
        write(src, dst)
    small_read.wait()
    for row, at, vec, dst in ((1, 0, v_one, gain_one), (1, width, v_two, shift_one), (0, 0, v_bias, bias),
                              (2, 0, v_three, gain_two), (2, width, v_four, shift_two)):
        size = vec.shape[0]
        vec[...] = b_small[row:row + 1, at:at + size].reshape(size)
        write(vec, dst)
    for cp in writes:
        cp.wait()


def widen(g_down, g_up, g_out, g_qkv, small, result, grad_tokens):
    units, r_qkv, three = g_qkv.shape
    local, width, ff = three // 3, g_down.shape[2], g_up.shape[2]
    shape = jax.ShapeDtypeStruct
    hbm = pl.BlockSpec(memory_space=pl.ANY)
    wide = [(ff, width), (width, ff), (local, width), (3, width, local)]
    low = [g.shape for g in (g_down, g_up, g_out, g_qkv)]
    acts = [result.shape, grad_tokens.shape]
    return pl.pallas_call(
        lambda *refs: finish(refs),
        out_shape=(*(shape(x, WIDE) for x in wide), shape((width,), WIDE), shape((width,), WIDE),
                   shape((ff,), WIDE), shape((width,), WIDE), shape((width,), WIDE),
                   *(shape(x, LOW) for x in acts)),
        in_specs=[hbm] * 7,
        out_specs=(hbm,) * 11,
        scratch_shapes=[*(pltpu.VMEM(x, LOW) for x in low), *(pltpu.VMEM(x, WIDE) for x in wide),
                        *(pltpu.VMEM(x, LOW) for x in acts), pltpu.VMEM(small.shape, WIDE),
                        *(pltpu.VMEM(x, WIDE) for x in ((width,), (width,), (ff,), (width,), (width,))),
                        pltpu.SemaphoreType.DMA((24,)), pltpu.SemaphoreType.DMA((24,))],
        compiler_params=pltpu.CompilerParams(vmem_limit_bytes=VMEM_BYTES),
        name="widen",
    )(g_down, g_up, g_out, g_qkv, small, result, grad_tokens)


def body(n, tokens, w_qkv, w_out, gain_one, attention_norm_bias, w_up, b_up, w_down, gain_two, shift_two,
         block_perm, mask_index, mask_count, cotangent):
    result, grad_tokens, g_down, g_up, g_out, g_qkv, small = build(
        n, tokens, w_qkv.transpose(1, 0, 2), w_out, gain_one, attention_norm_bias, w_up, b_up, w_down, gain_two,
        shift_two, block_perm.T, mask_index, mask_count.reshape(1, 1), cotangent[0])
    (g_down, g_up, g_out, g_qkv, g_gain_one, g_shift_one, g_bias, g_gain_two, g_shift_two, result,
     grad_tokens) = widen(g_down, g_up, g_out, g_qkv, small, result, grad_tokens)
    return (result, grad_tokens, g_qkv.transpose(1, 0, 2), g_out, g_gain_one, g_shift_one, g_up, g_bias, g_down,
            g_gain_two, g_shift_two)


def solution(mesh):
    return jax.shard_map(
        functools.partial(body, mesh.shape["batch"]),
        mesh=mesh,
        in_specs=(P("batch", "head"), P(None, None, "head"), P(), P(), P(), P(None, "head"), P("head"),
                  P("head", None), P(), P(), P("head", None), P("batch", None), P("batch"),
                  P("batch", None, None)),
        out_specs=(P("batch", "head"), P("batch", "head"), P(None, None, "head"), P("head", None), P(), P(),
                   P(None, "head"), P("head"), P("head", None), P(), P()),
        check_vma=False,
    )
```

```python
import functools

import jax
import jax.numpy as jnp
from jax import lax
from jax.experimental import pallas as pl
from jax.experimental.pallas import tpu as pltpu
from jax.sharding import PartitionSpec as P

HEAD_DIM = 64
norm_eps = 1e-06
root_half = 0.7071067811865476
inv_root_two_pi = 0.3989422804014327
log2_e = 1.4426950408889634
LOW = jnp.bfloat16
WIDE = jnp.float32
LANES = 128
MESH = pl.DeviceIdType.MESH
VMEM_BYTES = 67043328
CUTS = (2, 4)
CHUNKS = {"D": 3, "U": 3, "O": 1, "Q": 2}
ORDERS = {"D": [[0, 1, 2, 3], [0, 1, 2, 3], [0, 2, 1, 3]],
          "U": [[0, 1, 2, 3], [0, 2, 1, 3], [0, 1, 2, 3]],
          "O": [[0, 1, 2, 3]],
          "Q": [[0, 1, 2, 3], [0, 1, 3, 2]]}
PLAN = (
    ("down", 0), ("down", 1), ("down", 2), ("in",), ("D0", 0), ("D1", 0), ("D2", 0), ("up", 0), ("up", 1),
    ("up", 2), ("attend",), ("U0", 0), ("U1", 0), ("U2", 0), ("D0", 1), ("ctx", 0), ("layer", 0, 1), ("D2", 1),
    ("D1", 1), ("norm",), ("U1", 1), ("mb", 0), ("D0", 2), ("U0", 1), ("mb", 1), ("D1", 2), ("small", 0),
    ("mb", 2), ("U2", 1), ("D0", 3), ("U0", 2), ("out",), ("qkv", 0), ("D1", 3), ("O0", 0), ("U1", 2),
    ("small", 1), ("U2", 2), ("far", 0, 1), ("Q0", 0), ("qkv", 1), ("D0", 4), ("far", 1, 2), ("U0", 3),
    ("small", 2), ("far", 2, 3), ("O0", 1), ("Q1", 0), ("D1", 4), ("ctx", 1), ("layer", 2, 3), ("U1", 3),
    ("D0", 5), ("Q0", 1), ("U2", 3), ("small", 3), ("O0", 2), ("far", 3, 4), ("near", 0, 1), ("U0", 4),
    ("near", 1, 2), ("D1", 5), ("near", 2, 4), ("Q1", 1), ("U1", 4), ("grad", 0, 1), ("layer", 3, 4), ("Q0", 2),
    ("U2", 4), ("D0", 6), ("O0", 3), ("grad", 1, 3), ("U0", 5), ("layer", 1, 2), ("D2", 2), ("D0", 7),
    ("D1", 6), ("Q1", 2), ("grad", 3, 4), ("gout",), ("stat", 0, 1), ("Q0", 3), ("U2", 5), ("stat", 2, 3),
    ("D1", 7), ("O0", 4), ("stat", 3, 4), ("D2", 3), ("Q1", 3), ("Q0", 4), ("O0", 5), ("stat", 1, 2), ("U0", 6),
    ("stats",), ("U2", 6), ("D2", 4), ("Q1", 4), ("U1", 5), ("U0", 7), ("U2", 7), ("result",), ("Q0", 5),
    ("O0", 6), ("O0", 7), ("D2", 5), ("Q1", 5), ("U1", 6), ("Q0", 6), ("U1", 7), ("Q0", 7), ("D2", 6),
    ("Q1", 6), ("D2", 7), ("Q1", 7),
)


def dot(a, b):
    return lax.dot_general(a, b, (((1,), (0,)), ((), ())), preferred_element_type=WIDE)


def dot_nt(a, b):
    return lax.dot_general(a, b, (((1,), (1,)), ((), ())), preferred_element_type=WIDE)


def dot_tn(a, b):
    return lax.dot_general(a, b, (((0,), (0,)), ((), ())), preferred_element_type=WIDE)


def normalize(values):
    centered = values - jnp.mean(values, axis=-1, keepdims=True)
    inverse = lax.rsqrt(jnp.mean(centered * centered, axis=-1, keepdims=True) + norm_eps)
    return centered * inverse, inverse


def norm_backward(upstream, normal, inverse, gain_vec):
    scaled = upstream * gain_vec
    return inverse * (
        scaled
        - jnp.mean(scaled, axis=-1, keepdims=True)
        - normal * jnp.mean(scaled * normal, axis=-1, keepdims=True)
    )


def col_sum(x):
    return jnp.sum(x, axis=0, keepdims=True)


def cat(parts):
    return jnp.concatenate(parts, axis=1)


class Ring:
    def __init__(self, order, extra, first, out, recv, send, keep, xsend, xrecv, sems, peer, bit_of):
        self.order, self.extra = order, extra
        self.first, self.out = first, out
        self.recv, self.send, self.keep = recv, send, keep
        self.xsend, self.xrecv = xsend, xrecv
        self.ssem, self.rsem, self.lsem = sems
        self.peer = peer
        self.mine = [bit_of(b) for b in order]
        units = first.shape[0]
        self.sizes = [units >> (k + 1) for k in range(len(order))]
        self.base = []
        base = 0
        for k in range(len(order)):
            base = base + self.mine[k] * self.sizes[k]
            self.base.append(base)

    def _copy(self, src, dst, slot, bit):
        return pltpu.make_async_remote_copy(
            src_ref=src, dst_ref=dst, send_sem=self.ssem.at[slot], recv_sem=self.rsem.at[slot],
            device_id=self.peer(bit), device_id_type=MESH)

    def _rs(self, k):
        size = self.sizes[k]
        if k == 0:
            src = self.first.at[pl.ds((1 - self.mine[0]) * size, size)]
        else:
            src = self.send[k - 1]
        return self._copy(src, self.recv[k], k, self.order[k])

    def _x(self, j):
        return self._copy(self.xsend, self.xrecv.at[pl.ds(j, 1)], len(self.order) + j, self.extra[j])

    def _ag(self, k):
        slot = len(self.order) + len(self.extra) + k
        part = self.first.at[pl.ds(self.base[k], self.sizes[k])]
        return self._copy(part, part, slot, self.order[k])

    def _write(self):
        return pltpu.make_async_copy(self.first, self.out, self.lsem)

    def start(self):
        self._rs(0).start()

    def _value(self, k, u):
        got = self.recv[k][u].astype(WIDE)
        if k == 0:
            return self.first[self.mine[0] * self.sizes[0] + u].astype(WIDE) + got
        return self.keep[k - 1][u] + got

    def reduce(self, k):
        self._rs(k).wait_recv()
        if k == 0:
            self._rs(0).wait_send()
        if k + 1 < len(self.order):
            half = self.sizes[k + 1]
            mine = self.mine[k + 1]

            def out_part(j, c):
                self.send[k][j] = self._value(k, (1 - mine) * half + j).astype(LOW)
                return c

            lax.fori_loop(0, half, out_part, 0)
            self._rs(k + 1).start()

            def own_part(j, c):
                self.keep[k][j] = self._value(k, mine * half + j)
                return c

            lax.fori_loop(0, half, own_part, 0)
        else:
            total = self._value(k, 0)
            for j in range(len(self.extra)):
                self.xsend[0] = total.astype(LOW)
                self._x(j).start()
                self._x(j).wait()
                total = self.xsend[0].astype(WIDE) + self.xrecv[j].astype(WIDE)
            self.first[self.base[k]] = total.astype(LOW)
            self._ag(k).start()

    def gather(self, k):
        self._ag(k + 1).wait_recv()
        if k >= 0:
            self._ag(k).start()
        else:
            self._write().start()

    def advance(self, stage):
        depth = len(self.order)
        if stage < depth:
            self.reduce(stage)
        else:
            self.gather(2 * depth - 2 - stage)

    def finish(self):
        for k in range(len(self.order)):
            if k > 0:
                self._rs(k).wait_send()
            self._ag(k).wait_send()
        self._write().wait()


def kernel(n, refs):
    (tokens, wqkv_hbm, wout_hbm, wup_hbm, wdown_hbm, *vectors,
     perm, count, index, cot,
     result, grad_tokens, o_down, o_up, o_out, o_qkv, small_out,
     wqkv, wout, wup, wdown, wsem, vecs,
     tok, qkv, sel_t, sel, blk, tokc, qc, probs, ctxc, normal_one, inverse_one, normed_one, low_one, slope,
     hidden, part, part_got, gb, gtwo, gin, back, back_got, gattn, gctx, dqc, dall, far, far_got, near,
     ctx, pre_two, down_far, down_got, stats, stats_got,
     f_down, f_up, f_out, f_qkv, small, small_got, small_sum,
     xs_send, xs_recv, lsem, rings) = refs
    rows, own = tokens.shape
    width = wout.shape[0]
    local = wqkv.shape[1] // 3
    pairs = local // LANES
    slots = index.shape[1]
    ff = wup.shape[1]
    block_len = rows // 2
    tile = 256
    tiles = rows // tile
    scale = HEAD_DIM ** (-0.5)
    b = lax.axis_index("batch")
    h = lax.axis_index("head")
    other = 1 - h
    bits = [1 << k for k in range(n.bit_length() - 1)]

    def bit_of(bit):
        return lax.rem(lax.div(b, bit), 2)

    def peer(bit):
        return (b + bit - 2 * bit * bit_of(bit), h)

    x_peer = (b, other)

    def x_copy(src, dst, slot):
        return pltpu.make_async_remote_copy(
            src_ref=src, dst_ref=dst, send_sem=xs_send.at[slot], recv_sem=xs_recv.at[slot],
            device_id=x_peer, device_id_type=MESH)

    loads = [pltpu.make_async_copy(s, d, wsem.at[i]) for i, (s, d) in enumerate(
        [(wqkv_hbm.at[j], wqkv.at[:, pl.ds(j * local, local)]) for j in range(3)]
        + [(wout_hbm, wout), (wup_hbm, wup), (wdown_hbm, wdown)])]
    for cp in loads:
        cp.start()
    barrier = pltpu.get_barrier_semaphore()
    pl.semaphore_signal(barrier, inc=1, device_id=x_peer, device_id_type=MESH)
    for bit in bits:
        pl.semaphore_signal(barrier, inc=1, device_id=peer(bit), device_id_type=MESH)
    pl.semaphore_wait(barrier, 1 + len(bits))

    own_cols = pl.ds(pl.multiple_of(h * own, LANES), own)
    far_cols = pl.ds(pl.multiple_of(other * own, LANES), own)

    def row_tile(r):
        return pl.ds(pl.multiple_of(r * tile, tile), tile)

    def tok_copy(r):
        return x_copy(tokens.at[row_tile(r)], tok.at[row_tile(r), own_cols], r)

    for r in range(tiles):
        tok_copy(r).start()
    own_tok = pltpu.make_async_copy(tokens, tok.at[:, own_cols], lsem.at[0])
    own_tok.start()

    for i, vector in enumerate(vectors):
        vecs[i:i + 1, :vector.shape[0]] = vector[...].reshape(1, -1)
    gain_one, shift_one, gain_two, shift_two = (vecs.at[i:i + 1, :width] for i in range(4))
    b_up = vecs.at[4:5, :]

    lane_slot = lax.broadcasted_iota(jnp.int32, (1, slots), 1)
    idx = jnp.where(lane_slot < count[...], index[...], -1)
    picked = jnp.where(lax.broadcasted_iota(jnp.int32, (rows, slots), 0) == idx, 1.0, 0.0)
    sel_t[...] = picked.astype(LOW)
    picked = jnp.transpose(picked)
    sel[...] = picked.astype(LOW)
    blk[...] = jnp.broadcast_to(jnp.sum(picked[:, block_len:], axis=1, keepdims=True), blk.shape)
    own_tok.wait()
    for cp in loads[:3]:
        cp.wait()

    def qkv_tile(r, c):
        tok_copy(r).wait_recv()
        out = dot(tok[row_tile(r), :], wqkv[...]).astype(LOW)
        for j in range(3 * pairs):
            qkv[j, row_tile(r), :] = out[:, j * LANES:(j + 1) * LANES]
        return c

    lax.fori_loop(0, tiles, qkv_tile, 0)

    low_lane = lax.broadcasted_iota(jnp.int32, (1, LANES), 1) < HEAD_DIM
    def keep_head(x, e):
        return jnp.where(low_lane, x, 0.0).astype(LOW) if e == 0 else jnp.where(low_lane, 0.0, x).astype(LOW)

    order = perm[...].astype(WIDE)
    head_lane = lax.broadcasted_iota(jnp.int32, order.shape, 1)

    def blocks_of(head):
        return jnp.sum(jnp.where(head_lane == head, order, 0.0), axis=1, keepdims=True)

    def second(head):
        pair = blocks_of(head)
        return (pair[:1] + blk[:, :1] * (pair[1:] - pair[:1])) > 0.5

    def masked_attention(p, c):
        q2 = dot(sel[...], qkv[p]).astype(LOW)
        qc[p] = q2
        halves = []
        for e in range(2):
            head = 2 * p + e
            late = second(head)
            qm = keep_head(q2.astype(WIDE), e)
            s = jnp.where(late, dot_nt(qm, qkv[pairs + p, block_len:, :]),
                          dot_nt(qm, qkv[pairs + p, :block_len, :])) * (scale * log2_e)
            ex = jnp.exp2(s - jnp.max(s, axis=-1, keepdims=True))
            pr = ex * (1.0 / jnp.sum(ex, axis=-1, keepdims=True))
            probs[head] = pr
            pr = pr.astype(LOW)
            halves.append(jnp.where(late, dot(pr, qkv[2 * pairs + p, block_len:, :]),
                                    dot(pr, qkv[2 * pairs + p, :block_len, :])))
        ctxc[h * pairs + p] = jnp.where(low_lane, halves[0], halves[1]).astype(LOW)
        ctxc_copy(p).start()
        return c

    def ctxc_copy(p):
        mine_c = ctxc.at[pl.ds(h * pairs + p, 1)]
        return x_copy(mine_c, mine_c, tiles + p)

    lax.fori_loop(0, pairs, masked_attention, 0)

    def attend(i, c):
        p = lax.rem(i, pairs)
        q_block = lax.div(i, pairs)
        q_rows = pl.ds(pl.multiple_of(q_block * block_len, block_len), block_len)
        q2 = qkv[p, q_rows, :].astype(WIDE)
        even, odd = blocks_of(2 * p), blocks_of(2 * p + 1)
        late = jnp.where(low_lane, jnp.where(q_block == 0, even[:1], even[1:]),
                         jnp.where(q_block == 0, odd[:1], odd[1:])) > 0.5

        def chosen(j):
            return jnp.where(late, qkv[j, block_len:, :].astype(WIDE), qkv[j, :block_len, :].astype(WIDE)).astype(LOW)

        k2, v2 = chosen(pairs + p), chosen(2 * pairs + p)
        halves = []
        for e in range(2):
            s = dot_nt(keep_head(q2, e), k2) * (scale * log2_e)
            ex = jnp.exp2(s - jnp.max(s, axis=-1, keepdims=True))
            inv = 1.0 / jnp.sum(ex, axis=-1, keepdims=True)
            halves.append(dot(ex.astype(LOW), v2) * inv)
        ctx[h * pairs + p, q_rows, :] = jnp.where(low_lane, halves[0], halves[1]).astype(LOW)
        ctx_copy(i).start()
        return c

    x_base = tiles + pairs

    def ctx_copy(i):
        q_rows = pl.ds(pl.multiple_of(lax.div(i, pairs) * block_len, block_len), block_len)
        part_ref = ctx.at[pl.ds(h * pairs + lax.rem(i, pairs), 1), q_rows]
        return x_copy(part_ref, part_ref, x_base + i)

    tokc[...] = dot(sel[...], tok[...]).astype(LOW)
    attend_units = 2 * pairs
    x_base2 = x_base + attend_units
    lax.fori_loop(0, CUTS[0], attend, 0)

    for p in range(pairs):
        ctxc_copy(p).wait_recv()
    for cp in loads[3:]:
        cp.wait()
    pre = tokc[...].astype(WIDE) + dot(cat([ctxc[j] for j in range(2 * pairs)]), wout[...])
    nrm_c, inv_c = normalize(pre)
    normal_one[...] = nrm_c
    inverse_one[...] = jnp.broadcast_to(inv_c, inverse_one.shape)
    nrm_c = nrm_c * gain_one[...] + shift_one[...]
    normed_one[...] = nrm_c
    low_one[...] = nrm_c.astype(LOW)
    ff_tile = 384

    def up_tile(i, c):
        cols = pl.ds(pl.multiple_of(i * ff_tile, ff_tile), ff_tile)
        u = dot(low_one[...], wup[:, cols]) + vecs[4:5, cols]
        cdf = 0.5 * (1.0 + lax.erf(u * root_half))
        hidden[:, cols] = (u * cdf).astype(LOW)
        slope[:, cols] = cdf + u * inv_root_two_pi * jnp.exp(-0.5 * u * u)
        return c

    lax.fori_loop(0, ff // ff_tile, up_tile, 0)
    part[...] = dot(hidden[...], wdown[...]).astype(LOW)
    part_copy = x_copy(part, part_got, x_base2)
    part_copy.start()
    lax.fori_loop(CUTS[0], CUTS[1], attend, 0)
    part_copy.wait_recv()

    normal_two, inv_two = normalize(normed_one[...] + (part[...].astype(WIDE) + part_got[...].astype(WIDE)))
    alive = lax.broadcasted_iota(jnp.int32, (slots, 1), 0) < count[...]
    up = jnp.where(alive, cot[...].astype(WIDE), 0.0)
    g2 = norm_backward(up, normal_two, inv_two, gain_two[...])
    gtwo[...] = g2
    gb[...] = g2.astype(LOW)
    small[2:3, :] = cat([col_sum(up * normal_two), col_sum(up)])

    def put(first, unit, value):
        r = first.shape[1]
        for j in range(value.shape[0] // r):
            first[unit + j] = value[j * r:(j + 1) * r, :]

    ring = {name: Ring(peer=peer, bit_of=bit_of, **r) for name, r in rings.items()}

    def by_tiles(group, k, first, grad):
        units = first.shape[0] // CHUNKS[group]
        size = units * first.shape[1]
        step = 256 if size % 256 == 0 else 384

        def one_tile(i, c):
            at = k * size + i * step
            put(first, k * units + i * (step * units // size), grad(pl.ds(pl.multiple_of(at, LANES), step)))
            return c

        lax.fori_loop(0, size // step, one_tile, 0)
        ring["%s%d" % (group, k)].start()

    def down_grad(k):
        by_tiles("D", k, f_down, lambda cols: dot_tn(hidden[:, cols], gb[...]).astype(LOW))

    def up_grad(k):
        by_tiles("U", k, f_up, lambda cols: dot_tn(low_one[:, cols], gin[...]).astype(LOW))

    def in_tile(i, c):
        cols = pl.ds(pl.multiple_of(i * ff_tile, ff_tile), ff_tile)
        g = (dot_nt(gb[...], wdown[cols, :]) * slope[:, cols]).astype(LOW)
        gin[:, cols] = g
        small[0:1, cols] = col_sum(g.astype(WIDE))
        return c

    back_copy = x_copy(back, back_got, x_base2 + 1)

    def input_grad():
        lax.fori_loop(0, ff // ff_tile, in_tile, 0)
        back[...] = dot_nt(gin[...], wup[...]).astype(LOW)
        back_copy.start()

    def attend_more():
        lax.fori_loop(CUTS[1], attend_units, attend, 0)

    own_rows = pl.ds(pl.multiple_of(h * local, LANES), local)

    def first_norm():
        back_copy.wait_recv()
        gn = gtwo[...] + (back[...].astype(WIDE) + back_got[...].astype(WIDE))
        small[1:2, :] = cat([col_sum(gn * normal_one[...]), col_sum(gn)])
        g1 = norm_backward(gn, normal_one[...], inverse_one[:, :1], gain_one[...])
        gtwo[...] = g1
        gattn[...] = g1.astype(LOW)
        gc = dot_nt(gattn[...], wout[own_rows, :]).astype(LOW)
        for p in range(pairs):
            gctx[p] = gc[:, p * LANES:(p + 1) * LANES]
        small[3:8, :] = jnp.zeros((5, small.shape[1]), WIDE)
        small_copy(0).start()

    def masked_backward(p, c):
        q2 = qc[p].astype(WIDE)
        g2 = gctx[p].astype(WIDE)
        k2 = cat([qkv[pairs + p, :block_len, :], qkv[pairs + p, block_len:, :]])
        dk = jnp.zeros((block_len, 2 * LANES), WIDE)
        dv = jnp.zeros((block_len, 2 * LANES), WIDE)
        dq = []
        for e in range(2):
            head = 2 * p + e
            late = second(head)
            gm = keep_head(g2, e)
            dp = jnp.where(late, dot_nt(gm, qkv[2 * pairs + p, block_len:, :]),
                           dot_nt(gm, qkv[2 * pairs + p, :block_len, :]))
            pr = probs[head]
            t = dp * pr
            ds = (t - pr * jnp.sum(t, axis=-1, keepdims=True)).astype(LOW)
            qm = keep_head(q2, e).astype(WIDE)
            gm = gm.astype(WIDE)
            dk = dk + dot_tn(ds, cat([jnp.where(late, 0.0, qm), jnp.where(late, qm, 0.0)]).astype(LOW))
            dv = dv + dot_tn(pr.astype(LOW),
                             cat([jnp.where(late, 0.0, gm), jnp.where(late, gm, 0.0)]).astype(LOW))
            both = dot(ds, k2)
            dq.append(jnp.where(late, both[:, LANES:], both[:, :LANES]))
        d = (jnp.where(low_lane, dq[0], dq[1]) * scale).astype(LOW)
        dqc[p] = d
        dall[p] = dot(sel_t[...], d).astype(LOW)
        dk = (dk * scale).astype(LOW)
        dv = dv.astype(LOW)
        dall[pairs + p, :block_len, :] = dk[:, :LANES]
        dall[pairs + p, block_len:, :] = dk[:, LANES:]
        dall[2 * pairs + p, :block_len, :] = dv[:, :LANES]
        dall[2 * pairs + p, block_len:, :] = dv[:, LANES:]
        return c

    def small_copy(k):
        return pltpu.make_async_remote_copy(
            src_ref=small.at[pl.ds(8 * k, 8)], dst_ref=small_got.at[pl.ds(8 * k, 8)],
            send_sem=xs_send.at[x_slots + k], recv_sem=xs_recv.at[x_slots + k],
            device_id=peer(bits[k]), device_id_type=MESH)

    small_write = pltpu.make_async_copy(small_sum, small_out, lsem.at[3])

    def small_step(k):
        small_copy(k).wait_recv()
        total = small[8 * k:8 * k + 8, :] + small_got[8 * k:8 * k + 8, :]
        if k + 1 < len(bits):
            small[8 * k + 8:8 * k + 16, :] = total
            small_copy(k + 1).start()
        else:
            small_sum[...] = total
            small_write.start()

    def out_grad():
        put(f_out, 0, dot_tn(cat([ctxc[h * pairs + p] for p in range(pairs)]), gattn[...]).astype(LOW))
        ring["O0"].start()

    def qkv_grad(k):
        def grad(cols):
            gq = dot_tn(tokc[:, cols], cat([dqc[p] for p in range(pairs)]))
            gkv = dot_tn(tok[:, cols], cat([dall[pairs + j] for j in range(2 * pairs)]))
            return cat([gq, gkv]).astype(LOW)

        by_tiles("Q", k, f_qkv, grad)

    def far_copy(r):
        return x_copy(far.at[row_tile(r)], far_got.at[row_tile(r)], x_base2 + 2 + r)

    def far_tile(r):
        d = cat([dall[j, row_tile(r), :] for j in range(3 * pairs)])
        far[row_tile(r), :] = dot_nt(d, wqkv[far_cols, :]).astype(LOW)
        far_copy(r).start()

    def near_tile(r):
        mine = gtwo[:, own_cols]
        high = mine.astype(LOW)
        rest = (mine - high.astype(WIDE)).astype(LOW)
        d = cat([dall[j, row_tile(r), :] for j in range(3 * pairs)])
        spread = dot(sel_t[row_tile(r), :], cat([high, rest]))
        near[row_tile(r), :] = dot_nt(d, wqkv[own_cols, :]) + (spread[:, :own] + spread[:, own:])

    def grad_tile(r):
        far_copy(r).wait_recv()
        far_copy(r).wait_send()
        far[row_tile(r), :] = (near[row_tile(r), :] + far_got[row_tile(r), :].astype(WIDE)).astype(LOW)

    grad_out = pltpu.make_async_copy(far, grad_tokens, lsem.at[1])

    def down_copy(r):
        return x_copy(down_far.at[row_tile(r)], down_got.at[row_tile(r)], x_base2 + 2 + tiles + r)

    def ctx_wait(block):
        for i in range(block * pairs, (block + 1) * pairs):
            ctx_copy(i).wait_recv()

    def layer_tile(r):
        rs = row_tile(r)
        pre_r = tok[rs, :].astype(WIDE) + dot(cat([ctx[j, rs, :] for j in range(2 * pairs)]), wout[...])
        normed = normalize(pre_r)[0] * gain_one[...] + shift_one[...]
        normed_one[...] = normed
        u = dot(normed.astype(LOW), wup[...]) + b_up[...]
        hid = (u * (0.5 * (1.0 + lax.erf(u * root_half)))).astype(LOW)
        down_far[rs, :] = dot(hid, wdown[:, far_cols]).astype(LOW)
        down_copy(r).start()
        pre_two[rs, :] = normed_one[:, own_cols] + dot(hid, wdown[:, own_cols])

    first_lane = lax.broadcasted_iota(jnp.int32, (1, LANES), 1) < 1
    stats_copy = x_copy(stats, stats_got, x_base2 + 2 + 2 * tiles)

    def stat_tile(r):
        rs = row_tile(r)
        down_copy(r).wait_recv()
        x = pre_two[rs, :] + down_got[rs, :].astype(WIDE)
        pre_two[rs, :] = x
        mean = jnp.mean(x, axis=-1, keepdims=True)
        dev = x - mean
        var = jnp.mean(dev * dev, axis=-1, keepdims=True)
        both = jnp.where(first_lane, mean, var)
        stats[r] = jnp.transpose(both)[:8, :]

    def result_tile(r, c):
        rs = row_tile(r)
        x = pre_two[rs, :]
        fill = jnp.zeros((LANES - 8, tile), WIDE)
        one = jnp.transpose(jnp.concatenate([stats[r], fill], axis=0))
        two = jnp.transpose(jnp.concatenate([stats_got[r], fill], axis=0))
        mean = 0.5 * (one[:, :1] + two[:, :1])
        gap = 0.5 * (one[:, :1] - two[:, :1])
        var = 0.5 * (one[:, 1:2] + two[:, 1:2]) + gap * gap
        down_copy(r).wait_send()
        down_far[rs, :] = ((x - mean) * lax.rsqrt(var + norm_eps) * vecs[2:3, own_cols]
                         + vecs[3:4, own_cols]).astype(LOW)
        return c

    result_out = pltpu.make_async_copy(down_far, result, lsem.at[2])

    def write_result():
        stats_copy.wait_recv()
        lax.fori_loop(0, tiles, result_tile, 0)
        result_out.start()

    x_slots = x_base2 + 3 + 2 * tiles
    steps = {"down": down_grad, "in": input_grad, "up": up_grad, "norm": first_norm, "attend": attend_more,
             "mb": lambda p: masked_backward(p, 0), "out": out_grad, "qkv": qkv_grad, "gout": grad_out.start,
             "stats": stats_copy.start, "result": write_result, "small": small_step, "ctx": ctx_wait}
    looped = {"far": far_tile, "near": near_tile, "grad": grad_tile, "layer": layer_tile, "stat": stat_tile}
    for name, *at in PLAN:
        if name in ring:
            ring[name].advance(at[0])
        elif name in looped:
            lax.fori_loop(at[0], at[1], lambda r, c, name=name: looped[name](r) or c, 0)
        else:
            steps[name](*at)
    for k in range(min(len(bits), 4), len(bits)):
        small_step(k)

    for r in range(tiles):
        tok_copy(r).wait_send()
    grad_out.wait()
    result_out.wait()
    small_write.wait()
    for i in range(attend_units):
        ctx_copy(i).wait_send()
    for p in range(pairs):
        ctxc_copy(p).wait_send()
    for cp in (part_copy, back_copy, stats_copy):
        cp.wait_send()
    for k in range(len(bits)):
        small_copy(k).wait_send()
    for one in ring.values():
        one.finish()


def build(n, tokens, wqkv, wout, gain_one, shift_one, wup, b_up, wdown, gain_two, shift_two, perm, index,
          count, cot):
    rows, own = tokens.shape
    width = wout.shape[0]
    local = wqkv.shape[2]
    pairs = local // LANES
    heads = local // HEAD_DIM
    slots = index.shape[1]
    ff = wup.shape[1]
    block_len = rows // 2
    tile = 256
    steps = n.bit_length() - 1
    bits = [1 << k for k in range(steps)]
    depth = min(4, steps)
    units = 1 << depth
    halving, extra = bits[:depth], bits[depth:]

    vm = pltpu.VMEM
    groups = {"D": (ff, width), "U": (width, ff), "O": (local, width), "Q": (width, 3 * local)}
    shapes = {g: (CHUNKS[g] * units, r // (CHUNKS[g] * units), c) for g, (r, c) in groups.items()}
    names = [(g, k) for g in groups for k in range(CHUNKS[g])]
    dma = pltpu.SemaphoreType.DMA

    def ring_scratch(g):
        _, r, c = shapes[g]
        sizes = [units >> (k + 1) for k in range(depth)]
        return {
            "recv": [vm((s, r, c), LOW) for s in sizes],
            "send": [vm((s, r, c), LOW) for s in sizes[1:]],
            "keep": [vm((s, r, c), WIDE) for s in sizes[1:]],
            "xsend": vm((1, r, c) if extra else (1, 8, LANES), LOW),
            "xrecv": vm((len(extra), r, c) if extra else (1, 8, LANES), LOW),
            "sems": (dma((2 * depth + len(extra),)), dma((2 * depth + len(extra),)), dma(())),
        }

    f = [vm(shapes[g], LOW) for g in groups]
    x_slots = 3 * (rows // tile) + 3 * pairs + 3
    scratch = [
        vm((width, 3 * local), LOW), vm(wout.shape, LOW), vm(wup.shape, LOW), vm(wdown.shape, LOW), dma((6,)),
        vm((8, ff), WIDE),
        vm((rows, width), LOW), vm((3 * pairs, rows, LANES), LOW), vm((rows, slots), LOW), vm((slots, rows), LOW),
        vm((slots, LANES), WIDE), vm((slots, width), LOW), vm((pairs, slots, LANES), LOW),
        vm((heads, slots, block_len), WIDE), vm((2 * pairs, slots, LANES), LOW), vm((slots, width), WIDE),
        vm((slots, LANES), WIDE), vm((slots, width), WIDE), vm((slots, width), LOW), vm((slots, ff), WIDE),
        vm((slots, ff), LOW), vm((slots, width), LOW), vm((slots, width), LOW), vm((slots, width), LOW),
        vm((slots, width), WIDE), vm((slots, ff), LOW), vm((slots, width), LOW), vm((slots, width), LOW),
        vm((slots, width), LOW), vm((pairs, slots, LANES), LOW),
        vm((pairs, slots, LANES), LOW), vm((3 * pairs, rows, LANES), LOW), vm((rows, own), LOW),
        vm((rows, own), LOW), vm((rows, own), WIDE),
        vm((2 * pairs, rows, LANES), LOW), vm((rows, own), WIDE), vm((rows, own), LOW),
        vm((rows, own), LOW), vm((rows // tile, 8, tile), WIDE), vm((rows // tile, 8, tile), WIDE),
        *f, vm((8 * steps, ff), WIDE), vm((8 * steps, ff), WIDE), vm((8, ff), WIDE),
        dma((x_slots + steps,)), dma((x_slots + steps,)), dma((4,)),
    ]
    plain = len(scratch)
    ring_specs = [ring_scratch(g) for g, _ in names]
    flat, tree = jax.tree.flatten(ring_specs, is_leaf=lambda x: not isinstance(x, (dict, list, tuple)))
    n_in, n_out = 14, 7

    def run(*refs):
        head_refs = refs[:n_in + n_out + plain]
        rings = jax.tree.unflatten(tree, refs[n_in + n_out + plain:])
        firsts = head_refs[-(len(groups) + 6):-6]
        outs = refs[n_in + 2:n_in + 2 + len(groups)]
        full = {}
        for (g, k), ring in zip(names, rings):
            i = list(groups).index(g)
            part = pl.ds(k * units, units)
            full["%s%d" % (g, k)] = dict(order=[halving[j] for j in ORDERS[g][k] if j < depth], extra=extra,
                                         first=firsts[i].at[part], out=outs[i].at[part], **ring)
        kernel(n, (*head_refs, full))

    hbm = pl.BlockSpec(memory_space=pl.ANY)
    v = pl.BlockSpec(memory_space=pltpu.VMEM)
    shape = jax.ShapeDtypeStruct
    return pl.pallas_call(
        run,
        out_shape=(shape((rows, own), LOW), shape((rows, own), LOW),
                   *(shape(shapes[g], LOW) for g in groups), shape((8, ff), WIDE)),
        in_specs=[hbm, hbm, hbm, hbm, hbm, v, v, v, v, v, v, v, v, v],
        out_specs=(hbm,) * 7,
        scratch_shapes=scratch + flat,
        compiler_params=pltpu.CompilerParams(
            collective_id=0, has_side_effects=True, vmem_limit_bytes=VMEM_BYTES),
        name="layer",
    )(tokens, wqkv, wout, wup, wdown, gain_one, shift_one, gain_two, shift_two, b_up, perm, count, index, cot)


def finish(refs):
    (f_down, f_up, f_out, f_qkv, small, res_in, tok_in,
     down, up, out, qkv, gain_one, shift_one, bias, gain_two, shift_two, res, tok,
     b_down, b_up, b_out, b_qkv, w_down, w_up, w_out, w_qkv, b_res, b_tok, b_small, v_one, v_two, v_bias, v_three,
     v_four, isem, osem) = refs
    width = gain_one.shape[0]
    local = qkv.shape[2]
    reads, writes = [], []

    def read(src, dst):
        cp = pltpu.make_async_copy(src, dst, isem.at[len(reads)])
        cp.start()
        reads.append(cp)
        return cp

    def write(src, dst):
        cp = pltpu.make_async_copy(src, dst, osem.at[len(writes)])
        cp.start()
        writes.append(cp)

    parts = 4
    jobs = []
    for src, low, wide, dst in ((f_down, b_down, w_down, down), (f_up, b_up, w_up, up),
                                (f_out, b_out, w_out, out), (f_qkv, b_qkv, w_qkv, qkv)):
        step = src.shape[0] // parts if src.shape[0] % parts == 0 else src.shape[0]
        for u in range(0, src.shape[0], step):
            jobs.append((read(src.at[pl.ds(u, step)], low.at[pl.ds(u, step)]), u, step, low, wide, dst))
    pass_on = [(read(a, b), b, c) for a, b, c in ((res_in, b_res, res), (tok_in, b_tok, tok))]
    small_read = read(small, b_small)
    for cp, u, step, low, wide, dst in jobs:
        cp.wait()
        r = low.shape[1]

        def unit(j, c, u=u, low=low, wide=wide, r=r, dst=dst):
            v = low[u + j].astype(WIDE)
            rows = pl.ds(pl.multiple_of((u + j) * r, r), r)
            if dst is qkv:
                for k in range(3):
                    wide[k, rows, :] = v[:, k * local:(k + 1) * local]
            else:
                wide[rows, :] = v
            return c

        lax.fori_loop(0, step, unit, 0)
        rows = pl.ds(u * r, step * r)
        if dst is qkv:
            write(wide.at[:, rows, :], dst.at[:, rows, :])
        else:
            write(wide.at[rows, :], dst.at[rows, :])
    for cp, src, dst in pass_on:
        cp.wait()
        write(src, dst)
    small_read.wait()
    for row, at, vec, dst in ((1, 0, v_one, gain_one), (1, width, v_two, shift_one), (0, 0, v_bias, bias),
                              (2, 0, v_three, gain_two), (2, width, v_four, shift_two)):
        size = vec.shape[0]
        vec[...] = b_small[row:row + 1, at:at + size].reshape(size)
        write(vec, dst)
    for cp in writes:
        cp.wait()


def widen(g_down, g_up, g_out, g_qkv, small, result, grad_tokens):
    units, r_qkv, three = g_qkv.shape
    local, width, ff = three // 3, g_down.shape[2], g_up.shape[2]
    shape = jax.ShapeDtypeStruct
    hbm = pl.BlockSpec(memory_space=pl.ANY)
    wide = [(ff, width), (width, ff), (local, width), (3, width, local)]
    low = [g.shape for g in (g_down, g_up, g_out, g_qkv)]
    acts = [result.shape, grad_tokens.shape]
    return pl.pallas_call(
        lambda *refs: finish(refs),
        out_shape=(*(shape(x, WIDE) for x in wide), shape((width,), WIDE), shape((width,), WIDE),
                   shape((ff,), WIDE), shape((width,), WIDE), shape((width,), WIDE),
                   *(shape(x, LOW) for x in acts)),
        in_specs=[hbm] * 7,
        out_specs=(hbm,) * 11,
        scratch_shapes=[*(pltpu.VMEM(x, LOW) for x in low), *(pltpu.VMEM(x, WIDE) for x in wide),
                        *(pltpu.VMEM(x, LOW) for x in acts), pltpu.VMEM(small.shape, WIDE),
                        *(pltpu.VMEM(x, WIDE) for x in ((width,), (width,), (ff,), (width,), (width,))),
                        pltpu.SemaphoreType.DMA((24,)), pltpu.SemaphoreType.DMA((24,))],
        compiler_params=pltpu.CompilerParams(vmem_limit_bytes=VMEM_BYTES),
        name="widen",
    )(g_down, g_up, g_out, g_qkv, small, result, grad_tokens)


def body(n, tokens, w_qkv, w_out, gain_one, attention_norm_bias, w_up, b_up, w_down, gain_two, shift_two,
         block_perm, mask_index, mask_count, cotangent):
    result, grad_tokens, g_down, g_up, g_out, g_qkv, small = build(
        n, tokens, w_qkv.transpose(1, 0, 2), w_out, gain_one, attention_norm_bias, w_up, b_up, w_down, gain_two,
        shift_two, block_perm.T, mask_index, mask_count.reshape(1, 1), cotangent[0])
    (g_down, g_up, g_out, g_qkv, g_gain_one, g_shift_one, g_bias, g_gain_two, g_shift_two, result,
     grad_tokens) = widen(g_down, g_up, g_out, g_qkv, small, result, grad_tokens)
    return (result, grad_tokens, g_qkv.transpose(1, 0, 2), g_out, g_gain_one, g_shift_one, g_up, g_bias, g_down,
            g_gain_two, g_shift_two)


def solution(mesh):
    return jax.shard_map(
        functools.partial(body, mesh.shape["batch"]),
        mesh=mesh,
        in_specs=(P("batch", "head"), P(None, None, "head"), P(), P(), P(), P(None, "head"), P("head"),
                  P("head", None), P(), P(), P("head", None), P("batch", None), P("batch"),
                  P("batch", None, None)),
        out_specs=(P("batch", "head"), P("batch", "head"), P(None, None, "head"), P("head", None), P(), P(),
                   P(None, "head"), P("head"), P("head", None), P(), P()),
        check_vma=False,
    )
```
